32 devices in a mesh: region: 16 (over z, x, core), head: 2 (over y).
Axes of the slice: x: 2, y: 2, z: 4, core: 2. Of those that a mesh axis runs over, the one named last changes fastest.
Arguments:
- points: bfloat16 [16384, 512], P('region'), may hold values from -6 to 6
- ln_gain: float32 [512], replicated, may hold values from 0.5 to 1.5
- ln_bias: float32 [512], replicated, may hold values from -3 to 3
- w_qkv: bfloat16 [512, 3, 512], P(None, None, 'head')
- b_qkv: float32 [3, 512], P(None, 'head'), may hold values from -3 to 3
- w_proj: bfloat16 [512, 512], P('head'), may hold values from -0.25 to 0.25
- b_proj: float32 [512], replicated, may hold values from -3 to 3
- counts: int32 [512], replicated, may hold values from 1 to 32
- hilbert_pos: int32 [512], replicated, may hold values from 0 to 511, as said below
Outputs:
- update: bfloat16 [16384, 512], P(('region', 'head'))
The draws below stay inside these ranges and needn't reach their ends.
Inputs may be any that keep to these rules, and one draw needn't show every extreme that they name: `hilbert_pos`: a permutation; the 32 z-order blocks of one region index land on exactly 8 region indices in Hilbert order, exactly 4 on each (position // 32 is the index).
All inputs are finite; a program needn't handle non-finite values.
Results may differ from the reference program's by a relative error of at most 0.014.
The reference program's roundings to bfloat16 on the way count: a program that leaves them out, or rounds other values in their place, can miss the bound.
Values may be sent and summed in bfloat16 or wider, within the bound.
A program may use at most 64 MiB of HBM per device.

```python
import jax
import jax.numpy as jnp
from jax import lax

D = 512
HEADS = 32
HD = 16
PATCH = 1024
BS = 32
BLK_DEV = 32
NBLK = 512
NPTS = 16384
PAIR_MOST = 4
HPD = 16
N_REGION = 16


def draw_hilbert_pos(key, part):
    devices = NBLK // BLK_DEV
    groups_count = BLK_DEV // PAIR_MOST
    subkeys = jax.random.split(key, 5)
    outer_order = jax.random.permutation(subkeys[0], devices)
    second = jax.random.permutation(subkeys[1], devices)
    offsets = jax.random.permutation(subkeys[2], devices)[:groups_count]
    local_order = jax.vmap(lambda sub: jax.random.permutation(sub, BLK_DEV))(jax.random.split(subkeys[3], devices))
    arrival = jax.vmap(lambda sub: jax.random.permutation(sub, BLK_DEV))(jax.random.split(subkeys[4], devices))
    group_of = local_order // PAIR_MOST
    within = local_order % PAIR_MOST
    source = jnp.arange(devices)[:, None]
    target = second[(outer_order[source] + offsets[group_of]) % devices]
    arrival_slot = arrival[target, group_of * PAIR_MOST + within]
    return (target * BLK_DEV + arrival_slot).reshape(-1).astype(jnp.int32)


def draw_w_qkv(key, part):
    subkeys = jax.random.split(key, 1)
    base = jax.random.normal(subkeys[0], (D, 3, D), jnp.float32) * (D // 3) ** (-0.5)
    return base.astype(jnp.bfloat16)


def set_ends(entries, stream_key, smallest, top_value):
    longest = entries.shape.index(max(entries.shape))
    spots = []
    for shift in (0, 1):
        where = [jax.random.randint(jax.random.fold_in(stream_key, axis), (), 0, length) for axis, length in enumerate(entries.shape)]
        where[longest] = (where[longest] + shift) % entries.shape[longest]
        spots.append(tuple(where))
    return entries.at[spots[0]].set(smallest).at[spots[1]].set(top_value)


def block_scale(rng, dims, pieces, smallest, largest):
    gain = 1.0
    for position, parts in pieces:
        steps = jax.random.uniform(jax.random.fold_in(jax.random.fold_in(rng, 6), position), (parts,), jnp.float32, smallest / len(pieces), largest / len(pieces))
        gain = gain * jnp.repeat(jnp.exp(steps), dims[position] // parts).reshape((-1,) + (1,) * (len(dims) - 1 - position))
    return gain


def noise(own_key, shape, spread, most, cuts=(), held_as=jnp.bfloat16):
    entries = jax.random.normal(own_key, shape, jnp.float32) * spread
    if len(cuts) > 0:
        entries = block_scale(own_key, shape, cuts, -0.22, 0.18) * entries
    return jnp.clip(entries, min=-most, max=most).astype(held_as)


def setup_inputs(seed: int = 0) -> dict:
    arg_keys = jax.random.split(jax.random.key(seed), 10)
    return {
        "points": noise(arg_keys[0], (NPTS, D), 1.0, 6.0, ((0, 16),)),
        "ln_gain": jnp.clip(jax.random.uniform(arg_keys[1], (D,), jnp.float32, 0.5, 1.5), 0.5, 1.5),
        "ln_bias": noise(arg_keys[2], (D,), 0.5, 3.0, (), jnp.float32),
        "w_qkv": draw_w_qkv(jax.random.fold_in(arg_keys[9], 71), 0),
        "b_qkv": noise(arg_keys[4], (3, D), 0.5, 3.0, ((1, 2),), jnp.float32),
        "w_proj": noise(arg_keys[5], (D, D), D ** -0.5, 0.25, ((0, 2),)),
        "b_proj": noise(arg_keys[6], (D,), 0.5, 3.0, (), jnp.float32),
        "counts": set_ends(jax.random.randint(arg_keys[7], (NBLK,), 1, BS + 1), jax.random.fold_in(arg_keys[7], 1), 1, BS).astype(jnp.int32),
        "hilbert_pos": draw_hilbert_pos(jax.random.fold_in(arg_keys[9], 71), 0),
    }


epsilon = 1e-05

def layer_norm(points, ln_gain, ln_bias):
    values = points.astype(jnp.float32)
    row_mean = lax.optimization_barrier(jnp.mean(values, axis=-1, keepdims=True))
    centred = values - row_mean
    row_var = lax.optimization_barrier(jnp.mean(centred * centred, axis=-1, keepdims=True))
    return (centred * lax.rsqrt(row_var + epsilon) * ln_gain + ln_bias).astype(jnp.bfloat16)

def reference(points, ln_gain, ln_bias, w_qkv, b_qkv, w_proj, b_proj, counts, hilbert_pos):
    total_blocks = N_REGION * BLK_DEV
    total_points = total_blocks * BS
    normed = layer_norm(points, ln_gain, ln_bias)
    projected = (jnp.dot(normed, w_qkv.reshape(D, 3 * D), preferred_element_type=jnp.float32) + b_qkv.reshape(3 * D)).astype(jnp.bfloat16)
    inverse = jnp.zeros((total_blocks,), jnp.int32).at[hilbert_pos].set(jnp.arange(total_blocks, dtype=jnp.int32))
    ordered = projected.reshape(total_blocks, BS, 3 * D)[inverse].reshape(total_points, 3 * D)
    valid = (jnp.arange(BS, dtype=jnp.int32)[None, :] < counts[inverse][:, None]).reshape(total_points)
    half_patch = PATCH // 2
    rolled = jnp.roll(ordered, half_patch, axis=0)
    rolled_valid = jnp.roll(valid, half_patch, axis=0)
    patches = rolled.reshape(total_points // PATCH, PATCH, 3, HEADS, HD)
    key_masks = rolled_valid.reshape(total_points // PATCH, PATCH)

    def attend_patch(tile_set):
        patch_rows, patch_mask = tile_set
        query_rows = patch_rows[:, 0].astype(jnp.float32)
        key_rows = patch_rows[:, 1].astype(jnp.float32)
        value_rows = patch_rows[:, 2].astype(jnp.float32)
        scores = jnp.einsum('qhe,khe->hqk', query_rows, key_rows) * HD ** (-0.5)
        scores = jnp.where(patch_mask[None, None, :], scores, -jnp.inf)
        row_peak = lax.optimization_barrier(jnp.max(scores, axis=-1, keepdims=True))
        expo = jnp.exp(scores - row_peak)
        row_total = lax.optimization_barrier(jnp.sum(expo, axis=-1, keepdims=True))
        weights = lax.optimization_barrier(expo.astype(jnp.bfloat16)).astype(jnp.float32)
        output = jnp.einsum('hqk,khe->qhe', weights, value_rows) / jnp.transpose(row_total, (1, 0, 2))
        return output.reshape(PATCH, D).astype(jnp.bfloat16)
    attended = lax.map(attend_patch, (patches, key_masks)).reshape(total_points, D)
    attended = jnp.roll(attended, -half_patch, axis=0)
    group_width = HPD * HD
    summed = jnp.zeros((total_points, D), jnp.float32)
    for group in range(HEADS // HPD):
        first_col = group * group_width
        partial_value = jnp.dot(attended[:, first_col:first_col + group_width], w_proj[first_col:first_col + group_width], preferred_element_type=jnp.float32)
        summed = summed + lax.optimization_barrier(partial_value.astype(jnp.bfloat16)).astype(jnp.float32)
    return jnp.where(valid[:, None], summed + b_proj, 0.0).astype(jnp.bfloat16)
```

```python
import functools

import jax
import jax.numpy as jnp
from jax import lax
from jax.experimental import pallas as pl
from jax.experimental.pallas import tpu as pltpu
from jax.sharding import PartitionSpec as P

HD = 16
PATCH = 1024
BS = 32
LANES = 128

epsilon = 1e-05
MESH = pl.DeviceIdType.MESH


def pack_kernel(total, parts, tile, pack_ref, head_ref, x_ref, gain_ref, bias_ref, out_ref, own):
    rows, depth = x_ref.shape
    width = depth // parts
    h = head_ref[0]

    def pick(value):
        chosen = value[:, :width]
        for part in range(1, parts):
            chosen = jnp.where(h == part, value[:, part * width:(part + 1) * width], chosen)
        return chosen

    gain = pick(gain_ref[...])
    bias = pick(bias_ref[...])

    def normalize(i, carry):
        part = pl.ds(pl.multiple_of(i * tile, tile), tile)
        values = x_ref[part, :].astype(jnp.float32)
        centred = values - jnp.mean(values, axis=-1, keepdims=True)
        row_var = jnp.mean(centred * centred, axis=-1, keepdims=True)
        own[part, :] = (pick(centred) * lax.rsqrt(row_var + epsilon) * gain + bias).astype(
            jnp.bfloat16
        )
        return carry

    lax.fori_loop(0, rows // tile, normalize, 0)

    def pack(j, carry):
        source = pl.multiple_of(pack_ref[j] * BS, BS)
        out_ref[pl.ds(pl.multiple_of(j * BS, BS), BS), :] = own[pl.ds(source, BS), :]
        return carry

    lax.fori_loop(0, total, pack, 0, unroll=8)


def pack_blocks(points, ln_gain, ln_bias, head, pack_table, parts, tile=256):
    total = pack_table.shape[0]
    rows, depth = points.shape
    vmem = pl.BlockSpec(memory_space=pltpu.VMEM)
    smem = pl.BlockSpec(memory_space=pltpu.SMEM)
    return pl.pallas_call(
        functools.partial(pack_kernel, total, parts, tile),
        out_shape=jax.ShapeDtypeStruct((total * BS, depth // parts), jnp.bfloat16),
        in_specs=[smem, smem, vmem, vmem, vmem],
        out_specs=vmem,
        scratch_shapes=[pltpu.VMEM((rows, depth // parts), jnp.bfloat16)],
        name="pack",
    )(pack_table, head.reshape(1), points, ln_gain.reshape(1, -1), ln_bias.reshape(1, -1))


def exchange_kernel(
    regions, heads_axis, chunk,
    send, recv, own_sem, send_sem, recv_sem, fsend_sem, frecv_sem,
):
    r = lax.axis_index("region")
    h = lax.axis_index("head")

    barrier = pltpu.get_barrier_semaphore()

    def greet(d, carry):
        pl.semaphore_signal(
            barrier, inc=1, device_id={"region": lax.rem(r + d, regions)}, device_id_type=MESH
        )
        return carry

    lax.fori_loop(1, regions, greet, 0)
    for e in range(1, heads_axis):
        pl.semaphore_signal(
            barrier, inc=1, device_id={"head": lax.rem(h + e, heads_axis)}, device_id_type=MESH
        )
    pl.semaphore_wait(barrier, regions - 1 + heads_axis - 1)

    def rows(s):
        return pl.ds(pl.multiple_of(s * chunk, chunk), chunk)

    def to_region(t):
        return pltpu.make_async_remote_copy(
            src_ref=send.at[rows(t)],
            dst_ref=recv.at[h, rows(r)],
            send_sem=send_sem.at[t],
            recv_sem=recv_sem.at[r],
            device_id={"region": t},
            device_id_type=MESH,
        )

    def from_region(s):
        return pltpu.make_async_remote_copy(
            src_ref=send.at[rows(s)],
            dst_ref=recv.at[h, rows(s)],
            send_sem=send_sem.at[s],
            recv_sem=recv_sem.at[s],
            device_id={"region": s},
            device_id_type=MESH,
        )

    def to_head(e, s, source):
        return pltpu.make_async_remote_copy(
            src_ref=source,
            dst_ref=recv.at[h, rows(s)],
            send_sem=fsend_sem.at[e, s],
            recv_sem=frecv_sem.at[h, s],
            device_id={"head": lax.rem(h + e, heads_axis)},
            device_id_type=MESH,
        )

    def from_head(e, s):
        other = lax.rem(h + e, heads_axis)
        return pltpu.make_async_remote_copy(
            src_ref=recv.at[other, rows(s)],
            dst_ref=recv.at[other, rows(s)],
            send_sem=fsend_sem.at[e, s],
            recv_sem=frecv_sem.at[other, s],
            device_id={"head": other},
            device_id_type=MESH,
        )

    def push(d, carry):
        to_region(lax.rem(r + d, regions)).start()
        return carry

    own = pltpu.make_async_copy(send.at[rows(r)], recv.at[h, rows(r)], own_sem)
    own.start()
    for e in range(1, heads_axis):
        to_head(e, r, send.at[rows(r)]).start()
    lax.fori_loop(1, regions, push, 0)

    def relay(d, carry):
        s = lax.rem(r - d + regions, regions)
        from_region(s).wait_recv()
        for e in range(1, heads_axis):
            to_head(e, s, recv.at[h, rows(s)]).start()
        return carry

    lax.fori_loop(1, regions, relay, 0)
    own.wait()

    def finish(d, carry):
        s = lax.rem(r - d + regions, regions)
        for e in range(1, heads_axis):
            from_head(e, s).wait_recv()
            to_head(e, s, recv.at[h, rows(s)]).wait_send()
        return carry

    lax.fori_loop(0, regions, finish, 0)

    def drain(d, carry):
        from_region(lax.rem(r + d, regions)).wait_send()
        return carry

    lax.fori_loop(1, regions, drain, 0)


def exchange(packed, regions, heads_axis):
    rows, width = packed.shape
    return pl.pallas_call(
        functools.partial(exchange_kernel, regions, heads_axis, rows // regions),
        out_shape=jax.ShapeDtypeStruct((heads_axis, rows, width), jnp.bfloat16),
        in_specs=[pl.BlockSpec(memory_space=pltpu.VMEM)],
        out_specs=pl.BlockSpec(memory_space=pltpu.VMEM),
        scratch_shapes=[
            pltpu.SemaphoreType.DMA,
            pltpu.SemaphoreType.DMA((regions,)),
            pltpu.SemaphoreType.DMA((regions,)),
            pltpu.SemaphoreType.DMA((heads_axis, regions)),
            pltpu.SemaphoreType.DMA((heads_axis, regions)),
        ],
        compiler_params=pltpu.CompilerParams(collective_id=0, has_side_effects=True),
        name="exchange",
    )(packed)


def project_kernel(
    blocks, tile, slot_ref, count_ref, recv, valid_ref, w_ref, b_ref, out_ref, full
):
    parts, _, piece = recv.shape
    width = w_ref.shape[1] // 3
    row_index = lax.broadcasted_iota(jnp.int32, (BS, piece), 0)

    def unpack(t, carry):
        source = pl.multiple_of(slot_ref[t] * BS, BS)
        count = count_ref[t]
        for part in range(parts):
            block = recv[part, pl.ds(source, BS), :].astype(jnp.float32)
            block = jnp.where(row_index < count, block, block[0:1, :])
            full[pl.ds(pl.multiple_of(t * BS, BS), BS), part * piece:(part + 1) * piece] = (
                block.astype(jnp.bfloat16)
            )
        return carry

    def multiply(i, carry):
        first = i * (tile // BS)
        lax.fori_loop(0, tile // BS, lambda t, c: unpack(first + t, c), 0, unroll=4)
        part = pl.ds(pl.multiple_of(i * tile, tile), tile)
        for c in range(3):
            columns = slice(c * width, (c + 1) * width)
            summed = jnp.dot(full[part, :], w_ref[:, columns], preferred_element_type=jnp.float32)
            summed = summed + b_ref[:, columns]
            if c == 0:
                summed = summed * HD ** (-0.5)
            if c == 2:
                keep = valid_ref[part, :].astype(jnp.float32)
                keep = jnp.concatenate([keep] * (width // LANES), axis=1)
                summed = jnp.where(keep > 0, summed, 0.0)
            out_ref[part, columns] = summed.astype(jnp.bfloat16)
        return carry

    lax.fori_loop(0, blocks * BS // tile, multiply, 0)


def project(recv, slot_table, own_counts, valid, weight, bias, tile=256):
    blocks = slot_table.shape[0]
    vmem = pl.BlockSpec(memory_space=pltpu.VMEM)
    smem = pl.BlockSpec(memory_space=pltpu.SMEM)
    return pl.pallas_call(
        functools.partial(project_kernel, blocks, tile),
        out_shape=jax.ShapeDtypeStruct((blocks * BS, weight.shape[1]), jnp.bfloat16),
        in_specs=[smem, smem, vmem, vmem, vmem, vmem],
        out_specs=vmem,
        scratch_shapes=[pltpu.VMEM((blocks * BS, weight.shape[0]), jnp.bfloat16)],
        name="project",
    )(slot_table, own_counts, recv, valid, weight, bias.reshape(1, -1))


def over_heads(heads, tile, q_ref, keys, vals, acc, den, ahead, peaks_out=None, peaks_in=None):
    queries, width = q_ref.shape
    lane = lax.broadcasted_iota(jnp.int32, (1, LANES), 1)
    steps = queries // tile
    per = LANES // HD

    for c in range(width // LANES):
        columns = slice(c * LANES, (c + 1) * LANES)
        count = min(per, heads - c * per)
        trip_heads = 4 if count % 4 == 0 else 2

        def score(n, i):
            mine = (lane // HD == n).astype(jnp.float32).astype(jnp.bfloat16)
            return lax.dot_general(
                q_ref[i * tile:(i + 1) * tile, columns] * mine, keys[:, columns],
                (((1,), (1,)), ((), ())), preferred_element_type=jnp.float32,
            )

        ahead[0] = score(0, 0)

        def several(trip, carry):
            order = [(trip_heads * trip + u, i) for u in range(trip_heads) for i in range(steps)]
            after = order[1:] + [(jnp.minimum(trip_heads * (trip + 1), count - 1), 0)]
            for turn, (n, i) in enumerate(order):
                part = slice(i * tile, (i + 1) * tile)
                ahead[(turn + 1) % 2] = score(*after[turn])
                scores = ahead[turn % 2]
                peak = jnp.max(scores, axis=-1, keepdims=True)
                if peaks_in is not None:
                    old = jnp.sum(
                        jnp.where(lane == n + c * per, peaks_in[part, :], 0.0),
                        axis=-1, keepdims=True,
                    )
                    peak = jnp.maximum(peak, old)
                    keep = jnp.exp(old - peak)
                if peaks_out is not None:
                    peaks_out[part, :] = jnp.where(
                        lane == n + c * per, peak, peaks_out[part, :]
                    )
                expo = jnp.exp(scores - peak).astype(jnp.bfloat16)
                result = jnp.dot(expo, vals[c], preferred_element_type=jnp.float32)
                mine = lane // HD == n
                over, under = acc[part, columns], den[part, columns]
                top, low = result[:, :LANES], result[:, LANES:]
                if peaks_in is not None:
                    top, low = over * keep + top, under * keep + low
                acc[part, columns] = jnp.where(mine, top, over)
                den[part, columns] = jnp.where(mine, low, under)
            return carry

        lax.fori_loop(0, count // trip_heads, several, 0)


def finish_heads(acc, den, w_ref, out_ref):
    attended = (acc[...] / den[...]).astype(jnp.bfloat16)
    out_ref[...] = jnp.dot(attended, w_ref[...], preferred_element_type=jnp.float32).astype(
        jnp.bfloat16
    )


def fill_values(vals, v_ref, on_ref, first):
    count = v_ref.shape[0]
    for c in range(vals.shape[0]):
        vals[c, first:first + count, :LANES] = v_ref[:, c * LANES:(c + 1) * LANES]
        vals[c, first:first + count, LANES:] = on_ref[...]


def near_kernel(
    heads, tile, half_ref, q_ref, kn_ref, vn_ref, on_ref, acc, den, peaks, vals, ahead
):
    fill_values(vals, vn_ref, on_ref, 0)
    acc[...] = jnp.zeros_like(acc)
    den[...] = jnp.ones_like(den)
    peaks[...] = jnp.zeros_like(peaks)
    over_heads(heads, tile, q_ref, kn_ref, vals, acc, den, ahead, peaks_out=peaks)


def far_kernel(
    heads, tile, half_ref, q_ref, kf_ref, vf_ref, of_ref, w_ref, acc0, den0, peaks, out_ref,
    vals, acc, den, ahead,
):
    fill_values(vals, vf_ref, of_ref, 0)
    acc[...] = acc0[...]
    den[...] = den0[...]
    over_heads(heads, tile, q_ref, kf_ref, vals, acc, den, ahead, peaks_in=peaks)
    finish_heads(acc, den, w_ref, out_ref)


def attend_kernel(
    heads, tile,
    half_ref, q_ref, kn_ref, vn_ref, on_ref, kf_ref, vf_ref, of_ref, w_ref, out_ref,
    keys, vals, acc, den, ahead,
):
    near = kn_ref.shape[0]
    keys[:near, :] = kn_ref[...]
    keys[near:, :] = kf_ref[...]
    fill_values(vals, vn_ref, on_ref, 0)
    fill_values(vals, vf_ref, of_ref, near)
    acc[...] = jnp.zeros_like(acc)
    den[...] = jnp.ones_like(den)
    over_heads(heads, tile, q_ref, keys, vals, acc, den, ahead)
    finish_heads(acc, den, w_ref, out_ref)


def whole_block(*shape):
    return pl.BlockSpec(shape, lambda i, half: (0,) * len(shape))


def half_block(queries, width, column):
    return pl.BlockSpec((queries, width), lambda i, half: (half[0], column))


def attend_cost(heads, queries, keys, width):
    return pl.CostEstimate(
        flops=heads * queries * keys * width * 4,
        bytes_accessed=queries * width * 20,
        transcendentals=heads * queries * keys,
    )


def attend_near(half, qkv, valid, width, queries, heads, tile=512):
    return pl.pallas_call(
        functools.partial(near_kernel, heads, tile),
        out_shape=[
            jax.ShapeDtypeStruct((queries, width), jnp.float32),
            jax.ShapeDtypeStruct((queries, width), jnp.float32),
            jax.ShapeDtypeStruct((queries, LANES), jnp.float32),
        ],
        grid_spec=pltpu.PrefetchScalarGridSpec(
            num_scalar_prefetch=1,
            grid=(1,),
            in_specs=[half_block(queries, width, c) for c in range(3)]
            + [half_block(queries, LANES, 0)],
            out_specs=[
                whole_block(queries, width), whole_block(queries, width),
                whole_block(queries, LANES),
            ],
            scratch_shapes=[pltpu.VMEM((width // LANES, queries, 2 * LANES), jnp.bfloat16)]
            + [pltpu.VMEM((2, tile, queries), jnp.float32)],
        ),
        cost_estimate=attend_cost(heads, queries, queries, width),
        name="attend_near",
    )(half.reshape(1), qkv, qkv, qkv, valid)


def attend_far(half, qkv, far_kv, far_valid, w_proj, state, heads, tile=512):
    width, columns = w_proj.shape
    queries = far_kv.shape[0]
    return pl.pallas_call(
        functools.partial(far_kernel, heads, tile),
        out_shape=jax.ShapeDtypeStruct((queries, columns), jnp.bfloat16),
        grid_spec=pltpu.PrefetchScalarGridSpec(
            num_scalar_prefetch=1,
            grid=(1,),
            in_specs=[
                half_block(queries, width, 0),
                pl.BlockSpec((queries, width), lambda i, half: (0, 0)),
                pl.BlockSpec((queries, width), lambda i, half: (0, 1)),
                whole_block(queries, LANES),
                whole_block(width, columns),
                whole_block(queries, width), whole_block(queries, width),
                whole_block(queries, LANES),
            ],
            out_specs=whole_block(queries, columns),
            scratch_shapes=[pltpu.VMEM((width // LANES, queries, 2 * LANES), jnp.bfloat16)]
            + [pltpu.VMEM((queries, width), jnp.float32)] * 2
            + [pltpu.VMEM((2, tile, queries), jnp.float32)],
        ),
        cost_estimate=attend_cost(heads, queries, queries, width),
        name="attend_far",
    )(half.reshape(1), qkv, far_kv, far_kv, far_valid, w_proj, *state)


def attend(half, qkv, valid, far_kv, far_valid, w_proj, heads, tile=512):
    width = w_proj.shape[0]
    columns = w_proj.shape[1]
    queries = far_kv.shape[0]
    whole = lambda *shape: pl.BlockSpec(shape, lambda i, half: (0,) * len(shape))
    part = lambda c, w=width: pl.BlockSpec((queries, w), lambda i, half: (half[0], c))
    return pl.pallas_call(
        functools.partial(attend_kernel, heads, tile),
        out_shape=jax.ShapeDtypeStruct((queries, columns), jnp.bfloat16),
        grid_spec=pltpu.PrefetchScalarGridSpec(
            num_scalar_prefetch=1,
            grid=(1,),
            in_specs=[
                part(0), part(1), part(2), part(0, LANES),
                pl.BlockSpec((queries, width), lambda i, half: (0, 0)),
                pl.BlockSpec((queries, width), lambda i, half: (0, 1)),
                whole(queries, LANES),
                whole(width, columns),
            ],
            out_specs=whole(queries, columns),
            scratch_shapes=[pltpu.VMEM((2 * queries, width), jnp.bfloat16)]
            + [pltpu.VMEM((width // LANES, 2 * queries, 2 * LANES), jnp.bfloat16)]
            + [pltpu.VMEM((queries, width), jnp.float32)] * 2
            + [pltpu.VMEM((2, tile, 2 * queries), jnp.float32)],
        ),
        cost_estimate=pl.CostEstimate(
            flops=heads * queries * 2 * queries * width * 4,
            bytes_accessed=queries * columns * 10,
            transcendentals=heads * queries * 2 * queries,
        ),
        name="attend",
    )(half.reshape(1), qkv, qkv, qkv, valid, far_kv, far_kv, far_valid, w_proj)


def gather_kernel(slots, pos_ref, x_ref, out_ref, taken):
    rows, depth = x_ref.shape
    parts, _, width = out_ref.shape
    blocks = rows // BS
    first = lax.axis_index("region") * blocks
    for d in range(taken.shape[0]):
        taken[d] = 0

    def place(i, carry):
        target = lax.div(pos_ref[first + i], blocks)
        used = taken[target]
        taken[target] = used + 1
        into = pl.ds(pl.multiple_of((target * slots + used) * BS, BS), BS)
        source = pl.ds(pl.multiple_of(i * BS, BS), BS)
        for part in range(parts):
            out_ref[part, into, :] = x_ref[source, part * width:(part + 1) * width]
        return carry

    lax.fori_loop(0, blocks, place, 0, unroll=4)


def gather_blocks(points, hilbert_pos, regions, slots, parts):
    rows, depth = points.shape
    vmem = pl.BlockSpec(memory_space=pltpu.VMEM)
    return pl.pallas_call(
        functools.partial(gather_kernel, slots),
        out_shape=jax.ShapeDtypeStruct(
            (parts, regions * slots * BS, depth // parts), jnp.bfloat16
        ),
        in_specs=[pl.BlockSpec(memory_space=pltpu.SMEM), vmem],
        out_specs=vmem,
        scratch_shapes=[pltpu.SMEM((regions,), jnp.int32)],
        name="gather_blocks",
    )(hilbert_pos, points)


def swap_kernel(
    regions, near,
    send, gain_ref, bias_ref, w_ref, b_ref, made,
    recv, send_sem, recv_sem, relay_sem,
):
    r = lax.axis_index("region")
    h = lax.axis_index("head")
    other = 1 - h
    chunk = recv.shape[1] // regions
    piece = recv.shape[2]
    width = w_ref.shape[2]
    seat = lax.rem(r, near)
    base = r - seat
    far = regions - near
    lag = 2

    barrier = pltpu.get_barrier_semaphore()

    def greet(d, carry):
        pl.semaphore_signal(
            barrier, inc=1, device_id={"region": lax.rem(r + d, regions)}, device_id_type=MESH
        )
        return carry

    lax.fori_loop(1, regions, greet, 0)
    pl.semaphore_signal(barrier, inc=1, device_id={"head": other}, device_id_type=MESH)
    pl.semaphore_wait(barrier, regions)

    def rows(s):
        return pl.ds(pl.multiple_of(s * chunk, chunk), chunk)

    def to_region(t, part):
        return pltpu.make_async_remote_copy(
            src_ref=send.at[part, rows(t)],
            dst_ref=recv.at[part, rows(r)],
            send_sem=send_sem.at[part, t],
            recv_sem=recv_sem.at[part, r],
            device_id={"region": t},
            device_id_type=MESH,
        )

    def arrival(s, part):
        return pltpu.make_async_remote_copy(
            src_ref=send.at[part, rows(s)],
            dst_ref=recv.at[part, rows(s)],
            send_sem=send_sem.at[part, s],
            recv_sem=recv_sem.at[part, s],
            device_id={"head": other},
            device_id_type=MESH,
        )

    def relay(s):
        return pltpu.make_async_remote_copy(
            src_ref=recv.at[h, rows(s)],
            dst_ref=recv.at[h, rows(s)],
            send_sem=relay_sem.at[s],
            recv_sem=recv_sem.at[h, s],
            device_id={"head": other},
            device_id_type=MESH,
        )

    def keep(part):
        return pltpu.make_async_copy(
            send.at[part, rows(r)], recv.at[part, rows(r)], recv_sem.at[part, r]
        )

    def near_target(j):
        return base + lax.rem(seat + j, near)

    def far_target(j):
        group = lax.div(j, near)
        return lax.rem(base + near * (group + 1), regions) + lax.rem(seat + lax.rem(j, near), near)

    def near_source(j):
        return base + lax.rem(seat + near - j, near)

    def far_source(j):
        group = lax.div(j, near)
        return lax.rem(base + regions - near * (group + 1), regions) + lax.rem(
            seat + near - lax.rem(j, near), near
        )

    keep(0).start()
    keep(1).start()

    def push_near(j, carry):
        t = near_target(j)
        to_region(t, 0).start()
        to_region(t, 1).start()
        return carry

    def push_far(j, carry):
        to_region(far_target(j), h).start()
        return carry

    lax.fori_loop(1, near, push_near, 0)
    lax.fori_loop(0, far, push_far, 0)

    def project(s):
        part = rows(s)
        left = recv[0, part, :].astype(jnp.float32)
        right = recv[1, part, :].astype(jnp.float32)
        depth = 2 * piece
        mean = (
            jnp.sum(left, axis=-1, keepdims=True) + jnp.sum(right, axis=-1, keepdims=True)
        ) * (1.0 / depth)
        left = left - mean
        right = right - mean
        row_var = (
            jnp.sum(left * left, axis=-1, keepdims=True)
            + jnp.sum(right * right, axis=-1, keepdims=True)
        ) * (1.0 / depth)
        scale = lax.rsqrt(row_var + epsilon)
        left = (left * scale * gain_ref[:, :piece] + bias_ref[:, :piece]).astype(jnp.bfloat16)
        right = (right * scale * gain_ref[:, piece:] + bias_ref[:, piece:]).astype(jnp.bfloat16)
        for c in range(3):
            summed = jnp.dot(left, w_ref[c, :piece, :], preferred_element_type=jnp.float32)
            summed = summed + jnp.dot(
                right, w_ref[c, piece:, :], preferred_element_type=jnp.float32
            )
            summed = summed + b_ref[c:c + 1, :]
            if c == 0:
                summed = summed * HD ** (-0.5)
            made[part, c * width:(c + 1) * width] = summed.astype(jnp.bfloat16)

    ahead = near - lag

    def forward(j):
        s = far_source(j)
        arrival(s, h).wait_recv()
        relay(s).start()

    def close(i, carry):
        @pl.when(i >= lag)
        def _():
            forward(i - lag)

        s = near_source(i)
        arrival(s, 0).wait_recv()
        arrival(s, 1).wait_recv()
        project(s)
        return carry

    def distant(j, carry):
        @pl.when(j < far - ahead)
        def _():
            forward(j + ahead)

        s = far_source(j)
        arrival(s, other).wait_recv()
        project(s)
        return carry

    lax.fori_loop(0, near, close, 0)
    lax.fori_loop(0, far, distant, 0)

    def drain_near(j, carry):
        t = near_target(j)
        to_region(t, 0).wait_send()
        to_region(t, 1).wait_send()
        return carry

    def drain_far(j, carry):
        to_region(far_target(j), h).wait_send()
        relay(far_source(j)).wait_send()
        return carry

    lax.fori_loop(1, near, drain_near, 0)
    lax.fori_loop(0, far, drain_far, 0)


def swap(send, ln_gain, ln_bias, weight, bias, regions):
    parts, rows, piece = send.shape
    width = weight.shape[2]
    vmem = pl.BlockSpec(memory_space=pltpu.VMEM)
    return pl.pallas_call(
        functools.partial(swap_kernel, regions, regions // 4),
        out_shape=jax.ShapeDtypeStruct((rows, 3 * width), jnp.bfloat16),
        in_specs=[pl.BlockSpec(memory_space=pl.ANY), vmem, vmem, vmem, vmem],
        out_specs=vmem,
        scratch_shapes=[
            pltpu.VMEM((parts, rows, piece), jnp.bfloat16),
            pltpu.SemaphoreType.DMA((parts, regions)),
            pltpu.SemaphoreType.DMA((parts, regions)),
            pltpu.SemaphoreType.DMA((regions,)),
        ],
        compiler_params=pltpu.CompilerParams(collective_id=1, has_side_effects=True),
        name="swap",
    )(send, ln_gain.reshape(1, -1), ln_bias.reshape(1, -1), weight, bias)


def unpack_kernel(slot_ref, count_ref, made, out_ref, sems):
    blocks = slot_ref.shape[0]
    width = out_ref.shape[1] // 3

    def fetch(t):
        return pltpu.make_async_copy(
            made.at[pl.ds(pl.multiple_of(slot_ref[t] * BS, BS), BS)],
            out_ref.at[pl.ds(pl.multiple_of(t * BS, BS), BS)],
            sems.at[t],
        )

    def begin(t, carry):
        fetch(t).start()
        return carry

    lax.fori_loop(0, blocks, begin, 0)
    row_index = lax.broadcasted_iota(jnp.int32, (BS, width), 0)

    def mask(t, carry):
        fetch(t).wait()
        into = pl.ds(pl.multiple_of(t * BS, BS), BS)
        live = row_index < count_ref[t]
        keys = out_ref[into, width:2 * width].astype(jnp.float32)
        out_ref[into, width:2 * width] = jnp.where(live, keys, keys[0:1, :]).astype(jnp.bfloat16)
        vals = out_ref[into, 2 * width:].astype(jnp.float32)
        out_ref[into, 2 * width:] = jnp.where(live, vals, 0.0).astype(jnp.bfloat16)
        return carry

    lax.fori_loop(0, blocks, mask, 0, unroll=4)


def unpack_blocks(made, slot_table, own_counts):
    blocks = slot_table.shape[0]
    vmem = pl.BlockSpec(memory_space=pltpu.VMEM)
    smem = pl.BlockSpec(memory_space=pltpu.SMEM)
    return pl.pallas_call(
        unpack_kernel,
        out_shape=jax.ShapeDtypeStruct((blocks * BS, made.shape[1]), jnp.bfloat16),
        in_specs=[smem, smem, pl.BlockSpec(memory_space=pl.ANY)],
        out_specs=vmem,
        scratch_shapes=[pltpu.SemaphoreType.DMA((blocks,))],
        name="unpack_blocks",
    )(slot_table, own_counts, made)


def shards(points, ln_gain, ln_bias, w_qkv, b_qkv, w_proj, b_proj, counts, hilbert_pos):
    regions = lax.axis_size("region")
    heads_axis = lax.axis_size("head")
    r = lax.axis_index("region")
    h = lax.axis_index("head")
    rows, model_width = points.shape
    group_width = w_qkv.shape[2]
    heads = group_width // HD
    width = max(group_width, LANES)
    blocks = rows // BS
    total_blocks = blocks * regions
    slots = max(2, 2 * blocks // regions)
    half_rows = PATCH // 2
    half_blocks = half_rows // BS

    position = jnp.arange(blocks, dtype=jnp.int32)
    my_dest = lax.dynamic_slice_in_dim(hilbert_pos, r * blocks, blocks) // blocks
    earlier = (my_dest[:, None] == my_dest[None, :]) & (position[None, :] < position[:, None])
    my_slot = my_dest * slots + jnp.sum(earlier, axis=1, dtype=jnp.int32)
    pack_table = jnp.sum(
        jnp.where(
            my_slot[None, :] == jnp.arange(regions * slots, dtype=jnp.int32)[:, None],
            position[None, :], 0,
        ),
        axis=1, dtype=jnp.int32,
    )
    every = jnp.arange(total_blocks, dtype=jnp.int32)
    ext = (
        r * blocks - half_blocks + jnp.arange(blocks + 2 * half_blocks, dtype=jnp.int32)
        + total_blocks
    ) % total_blocks
    here = hilbert_pos[None, :] == ext[:, None]
    ext_counts = jnp.sum(jnp.where(here, counts[None, :], 0), axis=1, dtype=jnp.int32)
    origin = jnp.sum(
        jnp.where(here[half_blocks:half_blocks + blocks], every[None, :], 0),
        axis=1, dtype=jnp.int32,
    )
    same = (
        (every[None, :] < origin[:, None])
        & (every[None, :] // blocks == origin[:, None] // blocks)
        & (hilbert_pos[None, :] // blocks == r)
    )
    slot_table = origin // blocks * slots + jnp.sum(same, axis=1, dtype=jnp.int32)
    own_counts = ext_counts[half_blocks:half_blocks + blocks]
    valid_ext = (
        jnp.arange(BS, dtype=jnp.int32)[None, :, None] < ext_counts[:, None, None]
    )
    valid_ext = jnp.broadcast_to(valid_ext, (blocks + 2 * half_blocks, BS, LANES))
    valid_ext = valid_ext.reshape(-1, LANES).astype(jnp.bfloat16)

    pad = width - group_width
    valid = valid_ext[half_rows:half_rows + rows]
    w_out = jnp.pad(w_proj, ((0, pad), (0, 0)))
    if heads_axis == 2:
        send = gather_blocks(points, hilbert_pos, regions, slots, heads_axis)
        made = swap(
            send, ln_gain, ln_bias, jnp.transpose(w_qkv, (1, 0, 2)), b_qkv, regions
        )
        qkv = unpack_blocks(made, slot_table, own_counts)
    else:
        packed = pack_blocks(points, ln_gain, ln_bias, h, pack_table, heads_axis)
        recv = exchange(packed, regions, heads_axis)
        weight = jnp.pad(w_qkv, ((0, 0), (0, 0), (0, pad))).reshape(model_width, 3 * width)
        bias = jnp.pad(b_qkv, ((0, 0), (0, pad))).reshape(3 * width)
        qkv = project(recv, slot_table, own_counts, valid, weight, bias)

    if heads_axis == 2:
        order = (1 - h, h)
        flat = lambda a, b: (a % regions) * 2 + b
        fars = []
        for turn in range(2):
            pairs = []
            for i in range(regions):
                for b in range(2):
                    upper = (1 - b if turn == 0 else b) == 1
                    pairs.append((flat(i + 1 if upper else i - 1, b), flat(i, b)))
            start = (1 - order[turn]) * half_rows
            piece = lax.dynamic_slice(qkv, (start, width), (half_rows, 2 * width))
            fars.append(lax.ppermute(piece, ("region", "head"), pairs))
        partials = []
        for turn in range(2):
            half = order[turn]
            far_valid = lax.dynamic_slice(
                valid_ext, (half * (rows + half_rows), 0), (half_rows, LANES)
            )
            if turn == 0:
                state = attend_near(half, qkv, valid, width, half_rows, heads)
                partials.append(
                    attend_far(half, qkv, fars[0], far_valid, w_out, state, heads)
                )
                arrived = lax.ppermute(partials[0], "head", [(0, 1), (1, 0)])
            else:
                partials.append(attend(half, qkv, valid, fars[1], far_valid, w_out, heads))
        summed_rows = partials[1].astype(jnp.float32) + arrived.astype(jnp.float32)
    else:
        up = [(i, (i + 1) % regions) for i in range(regions)]
        down = [(j, i) for i, j in up]
        kv = qkv[:, width:]
        before = lax.ppermute(kv[rows - half_rows:], "region", up)
        after = lax.ppermute(kv[:half_rows], "region", down)
        partials = [
            attend(jnp.int32(0), qkv, valid, before, valid_ext[:half_rows], w_out, heads),
            attend(jnp.int32(1), qkv, valid, after, valid_ext[rows + half_rows:], w_out, heads),
        ]
        summed_rows = lax.psum_scatter(
            jnp.concatenate(partials, axis=0), "head", scatter_dimension=0, tiled=True
        ).astype(jnp.float32)
    share = rows // heads_axis
    share_valid = lax.dynamic_slice(valid, (h * share, 0), (share, LANES))[:, :1] > 0
    return jnp.where(share_valid, summed_rows + b_proj, 0.0).astype(jnp.bfloat16)


def solution(mesh):
    return jax.shard_map(
        shards,
        mesh=mesh,
        in_specs=(
            P("region", None),
            P(),
            P(),
            P(None, None, "head"),
            P(None, "head"),
            P("head", None),
            P(),
            P(),
            P(),
        ),
        out_specs=P(("region", "head"), None),
        check_vma=False,
    )
```

```python
import functools

import jax
import jax.numpy as jnp
from jax import lax
from jax.experimental import pallas as pl
from jax.experimental.pallas import tpu as pltpu
from jax.sharding import PartitionSpec as P

HD = 16
PATCH = 1024
BS = 32
LANES = 128

epsilon = 1e-05
LOG2E = 1.4426950408889634
MESH = pl.DeviceIdType.MESH


def pack_kernel(total, parts, tile, pack_ref, head_ref, x_ref, gain_ref, bias_ref, out_ref, own):
    rows, depth = x_ref.shape
    width = depth // parts
    h = head_ref[0]

    def pick(value):
        chosen = value[:, :width]
        for part in range(1, parts):
            chosen = jnp.where(h == part, value[:, part * width:(part + 1) * width], chosen)
        return chosen

    gain = pick(gain_ref[...])
    bias = pick(bias_ref[...])

    def normalize(i, carry):
        part = pl.ds(pl.multiple_of(i * tile, tile), tile)
        values = x_ref[part, :].astype(jnp.float32)
        centred = values - jnp.mean(values, axis=-1, keepdims=True)
        row_var = jnp.mean(centred * centred, axis=-1, keepdims=True)
        own[part, :] = (pick(centred) * lax.rsqrt(row_var + epsilon) * gain + bias).astype(
            jnp.bfloat16
        )
        return carry

    lax.fori_loop(0, rows // tile, normalize, 0)

    def pack(j, carry):
        source = pl.multiple_of(pack_ref[j] * BS, BS)
        out_ref[pl.ds(pl.multiple_of(j * BS, BS), BS), :] = own[pl.ds(source, BS), :]
        return carry

    lax.fori_loop(0, total, pack, 0, unroll=8)


def pack_blocks(points, ln_gain, ln_bias, head, pack_table, parts, tile=256):
    total = pack_table.shape[0]
    rows, depth = points.shape
    vmem = pl.BlockSpec(memory_space=pltpu.VMEM)
    smem = pl.BlockSpec(memory_space=pltpu.SMEM)
    return pl.pallas_call(
        functools.partial(pack_kernel, total, parts, tile),
        out_shape=jax.ShapeDtypeStruct((total * BS, depth // parts), jnp.bfloat16),
        in_specs=[smem, smem, vmem, vmem, vmem],
        out_specs=vmem,
        scratch_shapes=[pltpu.VMEM((rows, depth // parts), jnp.bfloat16)],
        name="pack",
    )(pack_table, head.reshape(1), points, ln_gain.reshape(1, -1), ln_bias.reshape(1, -1))


def exchange_kernel(
    regions, heads_axis, chunk,
    send, recv, own_sem, send_sem, recv_sem, fsend_sem, frecv_sem,
):
    r = lax.axis_index("region")
    h = lax.axis_index("head")

    barrier = pltpu.get_barrier_semaphore()

    def greet(d, carry):
        pl.semaphore_signal(
            barrier, inc=1, device_id={"region": lax.rem(r + d, regions)}, device_id_type=MESH
        )
        return carry

    lax.fori_loop(1, regions, greet, 0)
    for e in range(1, heads_axis):
        pl.semaphore_signal(
            barrier, inc=1, device_id={"head": lax.rem(h + e, heads_axis)}, device_id_type=MESH
        )
    pl.semaphore_wait(barrier, regions - 1 + heads_axis - 1)

    def rows(s):
        return pl.ds(pl.multiple_of(s * chunk, chunk), chunk)

    def to_region(t):
        return pltpu.make_async_remote_copy(
            src_ref=send.at[rows(t)],
            dst_ref=recv.at[h, rows(r)],
            send_sem=send_sem.at[t],
            recv_sem=recv_sem.at[r],
            device_id={"region": t},
            device_id_type=MESH,
        )

    def from_region(s):
        return pltpu.make_async_remote_copy(
            src_ref=send.at[rows(s)],
            dst_ref=recv.at[h, rows(s)],
            send_sem=send_sem.at[s],
            recv_sem=recv_sem.at[s],
            device_id={"region": s},
            device_id_type=MESH,
        )

    def to_head(e, s, source):
        return pltpu.make_async_remote_copy(
            src_ref=source,
            dst_ref=recv.at[h, rows(s)],
            send_sem=fsend_sem.at[e, s],
            recv_sem=frecv_sem.at[h, s],
            device_id={"head": lax.rem(h + e, heads_axis)},
            device_id_type=MESH,
        )

    def from_head(e, s):
        other = lax.rem(h + e, heads_axis)
        return pltpu.make_async_remote_copy(
            src_ref=recv.at[other, rows(s)],
            dst_ref=recv.at[other, rows(s)],
            send_sem=fsend_sem.at[e, s],
            recv_sem=frecv_sem.at[other, s],
            device_id={"head": other},
            device_id_type=MESH,
        )

    def push(d, carry):
        to_region(lax.rem(r + d, regions)).start()
        return carry

    own = pltpu.make_async_copy(send.at[rows(r)], recv.at[h, rows(r)], own_sem)
    own.start()
    for e in range(1, heads_axis):
        to_head(e, r, send.at[rows(r)]).start()
    lax.fori_loop(1, regions, push, 0)

    def relay(d, carry):
        s = lax.rem(r - d + regions, regions)
        from_region(s).wait_recv()
        for e in range(1, heads_axis):
            to_head(e, s, recv.at[h, rows(s)]).start()
        return carry

    lax.fori_loop(1, regions, relay, 0)
    own.wait()

    def finish(d, carry):
        s = lax.rem(r - d + regions, regions)
        for e in range(1, heads_axis):
            from_head(e, s).wait_recv()
            to_head(e, s, recv.at[h, rows(s)]).wait_send()
        return carry

    lax.fori_loop(0, regions, finish, 0)

    def drain(d, carry):
        from_region(lax.rem(r + d, regions)).wait_send()
        return carry

    lax.fori_loop(1, regions, drain, 0)


def exchange(packed, regions, heads_axis):
    rows, width = packed.shape
    return pl.pallas_call(
        functools.partial(exchange_kernel, regions, heads_axis, rows // regions),
        out_shape=jax.ShapeDtypeStruct((heads_axis, rows, width), jnp.bfloat16),
        in_specs=[pl.BlockSpec(memory_space=pltpu.VMEM)],
        out_specs=pl.BlockSpec(memory_space=pltpu.VMEM),
        scratch_shapes=[
            pltpu.SemaphoreType.DMA,
            pltpu.SemaphoreType.DMA((regions,)),
            pltpu.SemaphoreType.DMA((regions,)),
            pltpu.SemaphoreType.DMA((heads_axis, regions)),
            pltpu.SemaphoreType.DMA((heads_axis, regions)),
        ],
        compiler_params=pltpu.CompilerParams(collective_id=0, has_side_effects=True),
        name="exchange",
    )(packed)


def project_kernel(
    blocks, tile, slot_ref, count_ref, recv, valid_ref, w_ref, b_ref, out_ref, full
):
    parts, _, piece = recv.shape
    width = w_ref.shape[1] // 3
    row_index = lax.broadcasted_iota(jnp.int32, (BS, piece), 0)

    def unpack(t, carry):
        source = pl.multiple_of(slot_ref[t] * BS, BS)
        count = count_ref[t]
        for part in range(parts):
            block = recv[part, pl.ds(source, BS), :].astype(jnp.float32)
            block = jnp.where(row_index < count, block, block[0:1, :])
            full[pl.ds(pl.multiple_of(t * BS, BS), BS), part * piece:(part + 1) * piece] = (
                block.astype(jnp.bfloat16)
            )
        return carry

    def multiply(i, carry):
        first = i * (tile // BS)
        lax.fori_loop(0, tile // BS, lambda t, c: unpack(first + t, c), 0, unroll=4)
        part = pl.ds(pl.multiple_of(i * tile, tile), tile)
        for c in range(3):
            columns = slice(c * width, (c + 1) * width)
            summed = jnp.dot(full[part, :], w_ref[:, columns], preferred_element_type=jnp.float32)
            summed = summed + b_ref[:, columns]
            if c == 0:
                summed = summed * HD ** (-0.5)
            if c == 2:
                keep = valid_ref[part, :].astype(jnp.float32)
                keep = jnp.concatenate([keep] * (width // LANES), axis=1)
                summed = jnp.where(keep > 0, summed, 0.0)
            out_ref[part, columns] = summed.astype(jnp.bfloat16)
        return carry

    lax.fori_loop(0, blocks * BS // tile, multiply, 0)


def project(recv, slot_table, own_counts, valid, weight, bias, tile=256):
    blocks = slot_table.shape[0]
    vmem = pl.BlockSpec(memory_space=pltpu.VMEM)
    smem = pl.BlockSpec(memory_space=pltpu.SMEM)
    return pl.pallas_call(
        functools.partial(project_kernel, blocks, tile),
        out_shape=jax.ShapeDtypeStruct((blocks * BS, weight.shape[1]), jnp.bfloat16),
        in_specs=[smem, smem, vmem, vmem, vmem, vmem],
        out_specs=vmem,
        scratch_shapes=[pltpu.VMEM((blocks * BS, weight.shape[0]), jnp.bfloat16)],
        name="project",
    )(slot_table, own_counts, recv, valid, weight, bias.reshape(1, -1))


def over_heads(heads, tile, q_ref, keys, vals, acc, den, ahead, peaks_out=None, peaks_in=None):
    queries, width = q_ref.shape
    lane = lax.broadcasted_iota(jnp.int32, (1, LANES), 1)
    steps = queries // tile
    per = LANES // HD

    for c in range(width // LANES):
        columns = slice(c * LANES, (c + 1) * LANES)
        count = min(per, heads - c * per)
        trip_heads = 4 if count % 4 == 0 else 2

        def score(n, i):
            mine = (lane // HD == n).astype(jnp.float32).astype(jnp.bfloat16)
            return lax.dot_general(
                q_ref[i * tile:(i + 1) * tile, columns] * mine, keys[:, columns],
                (((1,), (1,)), ((), ())), preferred_element_type=jnp.float32,
            )

        ahead[0] = score(0, 0)

        def several(trip, carry):
            order = [(trip_heads * trip + u, i) for u in range(trip_heads) for i in range(steps)]
            after = order[1:] + [(jnp.minimum(trip_heads * (trip + 1), count - 1), 0)]
            for turn, (n, i) in enumerate(order):
                part = slice(i * tile, (i + 1) * tile)
                ahead[(turn + 1) % 2] = score(*after[turn])
                scores = ahead[turn % 2]
                peak = jnp.max(scores, axis=-1, keepdims=True)
                if peaks_in is not None:
                    old = jnp.sum(
                        jnp.where(lane == n + c * per, peaks_in[part, :], 0.0),
                        axis=-1, keepdims=True,
                    )
                    peak = jnp.maximum(peak, old)
                    keep = jnp.exp(old - peak)
                if peaks_out is not None:
                    peaks_out[part, :] = jnp.where(
                        lane == n + c * per, peak, peaks_out[part, :]
                    )
                expo = jnp.exp(scores - peak).astype(jnp.bfloat16)
                result = jnp.dot(expo, vals[c], preferred_element_type=jnp.float32)
                mine = lane // HD == n
                over, under = acc[part, columns], den[part, columns]
                top, low = result[:, :LANES], result[:, LANES:]
                if peaks_in is not None:
                    top, low = over * keep + top, under * keep + low
                acc[part, columns] = jnp.where(mine, top, over)
                den[part, columns] = jnp.where(mine, low, under)
            return carry

        lax.fori_loop(0, count // trip_heads, several, 0)


def finish_heads(acc, den, w_ref, out_ref):
    attended = (acc[...] / den[...]).astype(jnp.bfloat16)
    out_ref[...] = jnp.dot(attended, w_ref[...], preferred_element_type=jnp.float32).astype(
        jnp.bfloat16
    )


def fill_values(vals, v_ref, on_ref, first):
    count = v_ref.shape[0]
    for c in range(vals.shape[0]):
        vals[c, first:first + count, :LANES] = v_ref[:, c * LANES:(c + 1) * LANES]
        vals[c, first:first + count, LANES:] = on_ref[...]


def attend_kernel(
    heads, tile,
    half_ref, q_ref, kn_ref, vn_ref, on_ref, kf_ref, vf_ref, of_ref, w_ref, out_ref,
    keys, vals, acc, den, ahead,
):
    near = kn_ref.shape[0]
    keys[:near, :] = kn_ref[...]
    keys[near:, :] = kf_ref[...]
    fill_values(vals, vn_ref, on_ref, 0)
    fill_values(vals, vf_ref, of_ref, near)
    acc[...] = jnp.zeros_like(acc)
    den[...] = jnp.ones_like(den)
    over_heads(heads, tile, q_ref, keys, vals, acc, den, ahead)
    finish_heads(acc, den, w_ref, out_ref)


def whole_block(*shape):
    return pl.BlockSpec(shape, lambda i, half: (0,) * len(shape))


def half_block(queries, width, column):
    return pl.BlockSpec((queries, width), lambda i, half: (half[0], column))


def attend_cost(heads, queries, keys, width):
    return pl.CostEstimate(
        flops=heads * queries * keys * width * 4,
        bytes_accessed=queries * width * 20,
        transcendentals=heads * queries * keys,
    )


def attend(half, qkv, valid, far_kv, far_valid, w_proj, heads, tile=512):
    width = w_proj.shape[0]
    columns = w_proj.shape[1]
    queries = far_kv.shape[0]
    whole = lambda *shape: pl.BlockSpec(shape, lambda i, half: (0,) * len(shape))
    part = lambda c, w=width: pl.BlockSpec((queries, w), lambda i, half: (half[0], c))
    return pl.pallas_call(
        functools.partial(attend_kernel, heads, tile),
        out_shape=jax.ShapeDtypeStruct((queries, columns), jnp.bfloat16),
        grid_spec=pltpu.PrefetchScalarGridSpec(
            num_scalar_prefetch=1,
            grid=(1,),
            in_specs=[
                part(0), part(1), part(2), part(0, LANES),
                pl.BlockSpec((queries, width), lambda i, half: (0, 0)),
                pl.BlockSpec((queries, width), lambda i, half: (0, 1)),
                whole(queries, LANES),
                whole(width, columns),
            ],
            out_specs=whole(queries, columns),
            scratch_shapes=[pltpu.VMEM((2 * queries, width), jnp.bfloat16)]
            + [pltpu.VMEM((width // LANES, 2 * queries, 2 * LANES), jnp.bfloat16)]
            + [pltpu.VMEM((queries, width), jnp.float32)] * 2
            + [pltpu.VMEM((2, tile, 2 * queries), jnp.float32)],
        ),
        cost_estimate=pl.CostEstimate(
            flops=heads * queries * 2 * queries * width * 4,
            bytes_accessed=queries * columns * 10,
            transcendentals=heads * queries * 2 * queries,
        ),
        name="attend",
    )(half.reshape(1), qkv, qkv, qkv, valid, far_kv, far_kv, far_valid, w_proj)


def gather_kernel(slots, pos_ref, x_ref, out_ref, taken):
    rows, depth = x_ref.shape
    parts, _, width = out_ref.shape
    blocks = rows // BS
    first = lax.axis_index("region") * blocks
    for d in range(taken.shape[0]):
        taken[d] = 0

    def place(i, carry):
        target = lax.div(pos_ref[first + i], blocks)
        used = taken[target]
        taken[target] = used + 1
        into = pl.ds(pl.multiple_of((target * slots + used) * BS, BS), BS)
        source = pl.ds(pl.multiple_of(i * BS, BS), BS)
        for part in range(parts):
            out_ref[part, into, :] = x_ref[source, part * width:(part + 1) * width]
        return carry

    lax.fori_loop(0, blocks, place, 0, unroll=4)


def gather_blocks(points, hilbert_pos, regions, slots, parts):
    rows, depth = points.shape
    vmem = pl.BlockSpec(memory_space=pltpu.VMEM)
    return pl.pallas_call(
        functools.partial(gather_kernel, slots),
        out_shape=jax.ShapeDtypeStruct(
            (parts, regions * slots * BS, depth // parts), jnp.bfloat16
        ),
        in_specs=[pl.BlockSpec(memory_space=pltpu.SMEM), vmem],
        out_specs=vmem,
        scratch_shapes=[pltpu.SMEM((regions,), jnp.int32)],
        name="gather_blocks",
    )(hilbert_pos, points)


def swap_kernel(
    regions, near,
    send, gain_ref, bias_ref, w_ref, b_ref, made,
    recv, send_sem, recv_sem, relay_sem,
):
    r = lax.axis_index("region")
    h = lax.axis_index("head")
    other = 1 - h
    chunk = recv.shape[1] // regions
    piece = recv.shape[2]
    width = w_ref.shape[2]
    seat = lax.rem(r, near)
    base = r - seat
    far = regions - near
    lag = 2

    barrier = pltpu.get_barrier_semaphore()

    def greet(d, carry):
        pl.semaphore_signal(
            barrier, inc=1, device_id={"region": lax.rem(r + d, regions)}, device_id_type=MESH
        )
        return carry

    lax.fori_loop(1, regions, greet, 0)
    pl.semaphore_signal(barrier, inc=1, device_id={"head": other}, device_id_type=MESH)
    pl.semaphore_wait(barrier, regions)

    def rows(s):
        return pl.ds(pl.multiple_of(s * chunk, chunk), chunk)

    def to_region(t, part):
        return pltpu.make_async_remote_copy(
            src_ref=send.at[part, rows(t)],
            dst_ref=recv.at[part, rows(r)],
            send_sem=send_sem.at[part, t],
            recv_sem=recv_sem.at[part, r],
            device_id={"region": t},
            device_id_type=MESH,
        )

    def arrival(s, part):
        return pltpu.make_async_remote_copy(
            src_ref=send.at[part, rows(s)],
            dst_ref=recv.at[part, rows(s)],
            send_sem=send_sem.at[part, s],
            recv_sem=recv_sem.at[part, s],
            device_id={"head": other},
            device_id_type=MESH,
        )

    def relay(s):
        return pltpu.make_async_remote_copy(
            src_ref=recv.at[h, rows(s)],
            dst_ref=recv.at[h, rows(s)],
            send_sem=relay_sem.at[s],
            recv_sem=recv_sem.at[h, s],
            device_id={"head": other},
            device_id_type=MESH,
        )

    def keep(part):
        return pltpu.make_async_copy(
            send.at[part, rows(r)], recv.at[part, rows(r)], recv_sem.at[part, r]
        )

    def near_target(j):
        return base + lax.rem(seat + j, near)

    def far_target(j):
        group = lax.div(j, near)
        return lax.rem(base + near * (group + 1), regions) + lax.rem(seat + lax.rem(j, near), near)

    def near_source(j):
        return base + lax.rem(seat + near - j, near)

    def far_source(j):
        group = lax.div(j, near)
        return lax.rem(base + regions - near * (group + 1), regions) + lax.rem(
            seat + near - lax.rem(j, near), near
        )

    keep(0).start()
    keep(1).start()

    def push_near(j, carry):
        t = near_target(j)
        to_region(t, 0).start()
        to_region(t, 1).start()
        return carry

    def push_far(j, carry):
        to_region(far_target(j), h).start()
        return carry

    lax.fori_loop(1, near, push_near, 0)
    lax.fori_loop(0, far, push_far, 0)

    def project(s):
        part = rows(s)
        left = recv[0, part, :].astype(jnp.float32)
        right = recv[1, part, :].astype(jnp.float32)
        depth = 2 * piece
        mean = (
            jnp.sum(left, axis=-1, keepdims=True) + jnp.sum(right, axis=-1, keepdims=True)
        ) * (1.0 / depth)
        left = left - mean
        right = right - mean
        row_var = (
            jnp.sum(left * left, axis=-1, keepdims=True)
            + jnp.sum(right * right, axis=-1, keepdims=True)
        ) * (1.0 / depth)
        scale = lax.rsqrt(row_var + epsilon)
        left = (left * scale * gain_ref[:, :piece] + bias_ref[:, :piece]).astype(jnp.bfloat16)
        right = (right * scale * gain_ref[:, piece:] + bias_ref[:, piece:]).astype(jnp.bfloat16)
        for c in range(3):
            summed = jnp.dot(left, w_ref[c, :piece, :], preferred_element_type=jnp.float32)
            summed = summed + jnp.dot(
                right, w_ref[c, piece:, :], preferred_element_type=jnp.float32
            )
            summed = summed + b_ref[c:c + 1, :]
            if c == 0:
                summed = summed * (HD ** (-0.5) * LOG2E)
            made[part, c * width:(c + 1) * width] = summed.astype(jnp.bfloat16)

    ahead = near - lag

    def forward(j):
        s = far_source(j)
        arrival(s, h).wait_recv()
        relay(s).start()

    def close(i, carry):
        @pl.when(i >= lag)
        def _():
            forward(i - lag)

        s = near_source(i)
        arrival(s, 0).wait_recv()
        arrival(s, 1).wait_recv()
        project(s)
        return carry

    def distant(j, carry):
        @pl.when(j < far - ahead)
        def _():
            forward(j + ahead)

        s = far_source(j)
        arrival(s, other).wait_recv()
        project(s)
        return carry

    lax.fori_loop(0, near, close, 0)
    lax.fori_loop(0, far, distant, 0)

    def drain_near(j, carry):
        t = near_target(j)
        to_region(t, 0).wait_send()
        to_region(t, 1).wait_send()
        return carry

    def drain_far(j, carry):
        to_region(far_target(j), h).wait_send()
        relay(far_source(j)).wait_send()
        return carry

    lax.fori_loop(1, near, drain_near, 0)
    lax.fori_loop(0, far, drain_far, 0)


def swap(send, ln_gain, ln_bias, weight, bias, regions):
    parts, rows, piece = send.shape
    width = weight.shape[2]
    vmem = pl.BlockSpec(memory_space=pltpu.VMEM)
    return pl.pallas_call(
        functools.partial(swap_kernel, regions, regions // 4),
        out_shape=jax.ShapeDtypeStruct((rows, 3 * width), jnp.bfloat16),
        in_specs=[pl.BlockSpec(memory_space=pl.ANY), vmem, vmem, vmem, vmem],
        out_specs=vmem,
        scratch_shapes=[
            pltpu.VMEM((parts, rows, piece), jnp.bfloat16),
            pltpu.SemaphoreType.DMA((parts, regions)),
            pltpu.SemaphoreType.DMA((parts, regions)),
            pltpu.SemaphoreType.DMA((regions,)),
        ],
        compiler_params=pltpu.CompilerParams(collective_id=1, has_side_effects=True),
        name="swap",
    )(send, ln_gain.reshape(1, -1), ln_bias.reshape(1, -1), weight, bias)


def unpack_kernel(slot_ref, count_ref, ext_ref, made, q_ref, k_ref, vt_ref, valid_ref, vals, sems):
    blocks = slot_ref.shape[0]
    width = q_ref.shape[1]
    near = (ext_ref.shape[1] - blocks) // 2

    def fetch(t, part, into):
        return pltpu.make_async_copy(
            made.at[
                pl.ds(pl.multiple_of(slot_ref[t] * BS, BS), BS), part * width:(part + 1) * width
            ],
            into.at[pl.ds(pl.multiple_of(t * BS, BS), BS)],
            sems.at[part, t],
        )

    def begin(t, carry):
        fetch(t, 2, vals).start()
        fetch(t, 1, k_ref).start()
        fetch(t, 0, q_ref).start()
        return carry

    lax.fori_loop(0, blocks, begin, 0)

    total = valid_ref.shape[1]
    spread = (
        lax.broadcasted_iota(jnp.int32, (ext_ref.shape[1], total), 1) // BS
        == lax.broadcasted_iota(jnp.int32, (ext_ref.shape[1], total), 0)
    ).astype(jnp.float32).astype(jnp.bfloat16)
    rows = valid_ref.shape[0]
    ext = jnp.broadcast_to(ext_ref[...].astype(jnp.float32), (rows, ext_ref.shape[1]))
    limit = jnp.dot(ext.astype(jnp.bfloat16), spread, preferred_element_type=jnp.float32)
    place = (lax.broadcasted_iota(jnp.int32, (rows, total), 1) % BS).astype(jnp.float32)
    valid_ref[...] = (place < limit).astype(jnp.float32).astype(jnp.bfloat16)

    def arrive_values(t, carry):
        fetch(t, 2, vals).wait()
        return carry

    lax.fori_loop(0, blocks, arrive_values, 0)
    step = 256
    for i in range(blocks * BS // step):
        part = slice(i * step, (i + 1) * step)
        own = valid_ref[0:1, near * BS + i * step:near * BS + (i + 1) * step].astype(jnp.float32)
        turned = jnp.transpose(vals[part, :].astype(jnp.float32))
        vt_ref[:, part] = (turned * own).astype(jnp.bfloat16)

    row_index = lax.broadcasted_iota(jnp.int32, (BS, width), 0)

    def mask(t, carry):
        fetch(t, 1, k_ref).wait()
        into = pl.ds(pl.multiple_of(t * BS, BS), BS)
        keys = k_ref[into, :].astype(jnp.float32)
        live = row_index < count_ref[near + t]
        k_ref[into, :] = jnp.where(live, keys, keys[0:1, :]).astype(jnp.bfloat16)
        return carry

    lax.fori_loop(0, blocks, mask, 0, unroll=4)

    def arrive_queries(t, carry):
        fetch(t, 0, q_ref).wait()
        return carry

    lax.fori_loop(0, blocks, arrive_queries, 0)


def unpack_blocks(made, slot_table, ext_counts):
    blocks = slot_table.shape[0]
    width = made.shape[1] // 3
    rows = blocks * BS
    vmem = pl.BlockSpec(memory_space=pltpu.VMEM)
    smem = pl.BlockSpec(memory_space=pltpu.SMEM)
    return pl.pallas_call(
        unpack_kernel,
        out_shape=[
            jax.ShapeDtypeStruct((rows, width), jnp.bfloat16),
            jax.ShapeDtypeStruct((rows, width), jnp.bfloat16),
            jax.ShapeDtypeStruct((width, rows), jnp.bfloat16),
            jax.ShapeDtypeStruct((HD, ext_counts.shape[0] * BS), jnp.bfloat16),
        ],
        in_specs=[smem, smem, vmem, pl.BlockSpec(memory_space=pl.ANY)],
        out_specs=[vmem] * 4,
        scratch_shapes=[
            pltpu.VMEM((rows, width), jnp.bfloat16), pltpu.SemaphoreType.DMA((3, blocks)),
        ],
        name="unpack_blocks",
    )(slot_table, ext_counts, ext_counts.reshape(1, -1), made)


def patch_kernel(
    regions, tile, group, chunk,
    q_ref, k_ref, vt_ref, valid_ref, w_ref, b_ref, out_ref,
    kh, vth, w_other, acc, peaks, att, att_in, ahead, ahead_peak,
    send_sem, recv_sem, side_sem,
):
    r = lax.axis_index("region")
    h = lax.axis_index("head")
    other = 1 - h
    half = kh.shape[1]
    width = q_ref.shape[1]
    heads = width // HD
    per = LANES // HD
    tiles = half // tile
    trips = heads // group
    lane = lax.broadcasted_iota(jnp.int32, (1, LANES), 1)

    def toward(a):
        return lax.rem(r + 1 - 2 * a + regions, regions)

    barrier = pltpu.get_barrier_semaphore()
    for a in range(2):
        pl.semaphore_signal(
            barrier, inc=1, device_id={"region": toward(a)}, device_id_type=MESH
        )
    pl.semaphore_signal(barrier, inc=1, device_id={"head": other}, device_id_type=MESH)
    pl.semaphore_wait(barrier, 3)

    def start_of(a):
        return pl.multiple_of(a * half, half)

    def halo(a, which):
        rows = pl.ds(start_of(1 - a), half)
        source = k_ref.at[rows, :] if which == 0 else vt_ref.at[:, rows]
        target = kh.at[a] if which == 0 else vth.at[a]
        return pltpu.make_async_remote_copy(
            src_ref=source, dst_ref=target,
            send_sem=send_sem.at[which, a], recv_sem=recv_sem.at[which, a],
            device_id={"region": toward(a)}, device_id_type=MESH,
        )

    def across(source, target, slot):
        return pltpu.make_async_remote_copy(
            src_ref=source, dst_ref=target,
            send_sem=side_sem.at[0, slot], recv_sem=side_sem.at[1, slot],
            device_id={"head": other}, device_id_type=MESH,
        )

    weights = across(w_ref, w_other, 0)
    halo(other, 0).start()
    halo(other, 1).start()
    halo(h, 0).start()
    halo(h, 1).start()
    weights.start()

    def score(slot, a, n, i, keys):
        columns = pl.ds(pl.multiple_of(n // per * LANES, LANES), LANES)
        mine = (lane // HD == n % per).astype(jnp.float32).astype(jnp.bfloat16)
        queries = q_ref[pl.ds(pl.multiple_of(a * half + i * tile, tile), tile), columns] * mine
        top = None
        for first in range(0, half, chunk):
            scores = lax.dot_general(
                keys(a, first, columns), queries, (((1,), (1,)), ((), ())),
                preferred_element_type=jnp.float32,
            )
            ahead[slot, first:first + chunk] = scores
            part = jnp.max(scores.reshape(chunk // 8, 8, tile), axis=0)
            top = part if top is None else jnp.maximum(top, part)
        ahead_peak[slot] = jnp.broadcast_to(jnp.max(top, axis=0, keepdims=True), (8, tile))

    def weigh(slot, a, n, peak, vals, flags):
        total = None
        rows = pl.ds(pl.multiple_of(n * HD, HD), HD)
        for first in range(0, half, chunk):
            scores = ahead[slot, first:first + chunk].reshape(chunk // 8, 8, tile)
            expo = jnp.exp2(scores - peak[None]).reshape(chunk, tile).astype(jnp.bfloat16)
            left = jnp.concatenate([vals(a, rows, first), flags(a, first)], axis=0)
            part = jnp.dot(left, expo, preferred_element_type=jnp.float32)
            total = part if total is None else total + part
        return total

    def run(trip_from, trip_to, limit, where, keys, use):
        def body(trip, carry):
            units = [(u, i) for u in range(group) for i in range(tiles)]
            for turn, (u, i) in enumerate(units):
                if turn + 1 < len(units):
                    v, j = units[turn + 1]
                    a, n = where(trip)
                    score((turn + 1) % 2, a, n + v, j, keys)
                else:
                    a, n = where(jnp.minimum(trip + 1, limit - 1))
                    score((turn + 1) % 2, a, n, 0, keys)
                a, n = where(trip)
                use(turn % 2, a, n + u, i)
            return carry

        lax.fori_loop(trip_from, trip_to, body, 0)

    def near_keys(a, first, columns):
        return k_ref[pl.ds(pl.multiple_of(a * half + first, chunk), chunk), columns]

    def near_vals(a, rows, first):
        return vt_ref[rows, pl.ds(pl.multiple_of(a * half + first, chunk), chunk)]

    def near_flags(a, first):
        return valid_ref[:, pl.ds(pl.multiple_of((a + 1) * half + first, chunk), chunk)]

    def far_keys(a, first, columns):
        return kh[a, first:first + chunk, columns]

    def far_vals(a, rows, first):
        return vth[a, rows, first:first + chunk]

    def far_flags(a, first):
        return valid_ref[:, pl.ds(pl.multiple_of(a * 3 * half + first, chunk), chunk)]

    def near_use(slot, a, n, i):
        peak = ahead_peak[slot]
        columns = slice(i * tile, (i + 1) * tile)
        acc[a, n, :, columns] = weigh(slot, a, n, peak, near_vals, near_flags)
        peaks[a, n, :, columns] = peak

    def far_use(slot, a, n, i):
        columns = slice(i * tile, (i + 1) * tile)
        old = peaks[a, n, :, columns]
        peak = jnp.maximum(ahead_peak[slot], old)
        keep = jnp.exp2(old - peak)
        total = weigh(slot, a, n, peak, far_vals, far_flags)
        before = acc[a, n, :, columns].reshape(2 * HD // 8, 8, tile)
        total = total + (before * keep[None]).reshape(2 * HD, tile)
        att[a, pl.ds(pl.multiple_of(n * HD, HD), HD), columns] = (
            total[:HD] / total[HD:]
        ).astype(jnp.bfloat16)

    def near_where(trip):
        late = lax.div(trip, trips)
        return lax.rem(other + late, 2), lax.rem(trip, trips) * group

    score(0, other, 0, 0, near_keys)
    run(0, 2 * trips, 2 * trips, near_where, near_keys, near_use)

    halo(other, 0).wait_recv()
    halo(other, 1).wait_recv()
    score(0, other, 0, 0, far_keys)
    run(0, trips, trips, lambda trip: (other, trip * group), far_keys, far_use)

    halo(h, 0).wait_recv()
    halo(h, 1).wait_recv()
    score(0, h, 0, 0, far_keys)
    swap_att = across(att.at[other], att_in, 1)
    run(0, 1, trips, lambda trip: (h, trip * group), far_keys, far_use)
    swap_att.start()
    run(1, trips, trips, lambda trip: (h, trip * group), far_keys, far_use)

    def share(attended, weight):
        return lax.dot_general(
            attended, weight, (((0,), (0,)), ((), ())), preferred_element_type=jnp.float32
        ).astype(jnp.bfloat16).astype(jnp.float32)

    flags = valid_ref[:, pl.ds(pl.multiple_of((h + 1) * half, half), half)]
    ones = jnp.full((HD, out_ref.shape[1]), 1.0 / HD, jnp.bfloat16)
    own = share(att[h], w_ref[...]) + b_ref[...]
    live = lax.dot_general(
        flags, ones, (((0,), (0,)), ((), ())), preferred_element_type=jnp.float32
    )
    weights.wait_recv()
    swap_att.wait_recv()
    update = own + share(att_in[...], w_other[...])
    out_ref[...] = jnp.where(live > 0.5, update, 0.0).astype(jnp.bfloat16)
    weights.wait_send()
    swap_att.wait_send()
    for a in range(2):
        for which in range(2):
            halo(a, which).wait_send()


def attend_patches(q, k, vt, valid, w_proj, b_proj, regions, tile=256, group=4, chunk=256):
    rows, width = q.shape
    half = rows // 2
    heads = width // HD
    columns = w_proj.shape[1]
    vmem = pl.BlockSpec(memory_space=pltpu.VMEM)
    return pl.pallas_call(
        functools.partial(patch_kernel, regions, tile, group, chunk),
        out_shape=jax.ShapeDtypeStruct((half, columns), jnp.bfloat16),
        in_specs=[vmem] * 6,
        out_specs=vmem,
        scratch_shapes=[
            pltpu.VMEM((2, half, width), jnp.bfloat16),
            pltpu.VMEM((2, width, half), jnp.bfloat16),
            pltpu.VMEM((width, columns), jnp.bfloat16),
            pltpu.VMEM((2, heads, 2 * HD, half), jnp.float32),
            pltpu.VMEM((2, heads, 8, half), jnp.float32),
            pltpu.VMEM((2, width, half), jnp.bfloat16),
            pltpu.VMEM((width, half), jnp.bfloat16),
            pltpu.VMEM((2, half, tile), jnp.float32),
            pltpu.VMEM((2, 8, tile), jnp.float32),
            pltpu.SemaphoreType.DMA((2, 2)),
            pltpu.SemaphoreType.DMA((2, 2)),
            pltpu.SemaphoreType.DMA((2, 2)),
        ],
        compiler_params=pltpu.CompilerParams(collective_id=2, has_side_effects=True),
        name="attend_patches",
    )(q, k, vt, valid, w_proj, b_proj.reshape(1, -1))


def shards(points, ln_gain, ln_bias, w_qkv, b_qkv, w_proj, b_proj, counts, hilbert_pos):
    regions = lax.axis_size("region")
    heads_axis = lax.axis_size("head")
    r = lax.axis_index("region")
    h = lax.axis_index("head")
    rows, model_width = points.shape
    group_width = w_qkv.shape[2]
    heads = group_width // HD
    width = max(group_width, LANES)
    blocks = rows // BS
    total_blocks = blocks * regions
    slots = max(2, 2 * blocks // regions)
    half_rows = PATCH // 2
    half_blocks = half_rows // BS

    position = jnp.arange(blocks, dtype=jnp.int32)
    my_dest = lax.dynamic_slice_in_dim(hilbert_pos, r * blocks, blocks) // blocks
    earlier = (my_dest[:, None] == my_dest[None, :]) & (position[None, :] < position[:, None])
    my_slot = my_dest * slots + jnp.sum(earlier, axis=1, dtype=jnp.int32)
    pack_table = jnp.sum(
        jnp.where(
            my_slot[None, :] == jnp.arange(regions * slots, dtype=jnp.int32)[:, None],
            position[None, :], 0,
        ),
        axis=1, dtype=jnp.int32,
    )
    every = jnp.arange(total_blocks, dtype=jnp.int32)
    ext = (
        r * blocks - half_blocks + jnp.arange(blocks + 2 * half_blocks, dtype=jnp.int32)
        + total_blocks
    ) % total_blocks
    here = hilbert_pos[None, :] == ext[:, None]
    ext_counts = jnp.sum(jnp.where(here, counts[None, :], 0), axis=1, dtype=jnp.int32)
    origin = jnp.sum(
        jnp.where(here[half_blocks:half_blocks + blocks], every[None, :], 0),
        axis=1, dtype=jnp.int32,
    )
    same = (
        (every[None, :] < origin[:, None])
        & (every[None, :] // blocks == origin[:, None] // blocks)
        & (hilbert_pos[None, :] // blocks == r)
    )
    slot_table = origin // blocks * slots + jnp.sum(same, axis=1, dtype=jnp.int32)
    own_counts = ext_counts[half_blocks:half_blocks + blocks]
    valid_ext = (
        jnp.arange(BS, dtype=jnp.int32)[None, :, None] < ext_counts[:, None, None]
    )
    valid_ext = jnp.broadcast_to(valid_ext, (blocks + 2 * half_blocks, BS, LANES))
    valid_ext = valid_ext.reshape(-1, LANES).astype(jnp.bfloat16)

    pad = width - group_width
    valid = valid_ext[half_rows:half_rows + rows]
    w_out = jnp.pad(w_proj, ((0, pad), (0, 0)))
    if heads_axis == 2:
        send = gather_blocks(points, hilbert_pos, regions, slots, heads_axis)
        made = swap(
            send, ln_gain, ln_bias, jnp.transpose(w_qkv, (1, 0, 2)), b_qkv, regions
        )
        q, k, vt, flags = unpack_blocks(made, slot_table, ext_counts)
        return attend_patches(q, k, vt, flags, w_proj, b_proj, regions)

    packed = pack_blocks(points, ln_gain, ln_bias, h, pack_table, heads_axis)
    recv = exchange(packed, regions, heads_axis)
    weight = jnp.pad(w_qkv, ((0, 0), (0, 0), (0, pad))).reshape(model_width, 3 * width)
    bias = jnp.pad(b_qkv, ((0, 0), (0, pad))).reshape(3 * width)
    qkv = project(recv, slot_table, own_counts, valid, weight, bias)

    up = [(i, (i + 1) % regions) for i in range(regions)]
    down = [(j, i) for i, j in up]
    kv = qkv[:, width:]
    before = lax.ppermute(kv[rows - half_rows:], "region", up)
    after = lax.ppermute(kv[:half_rows], "region", down)
    partials = [
        attend(jnp.int32(0), qkv, valid, before, valid_ext[:half_rows], w_out, heads),
        attend(jnp.int32(1), qkv, valid, after, valid_ext[rows + half_rows:], w_out, heads),
    ]
    summed_rows = lax.psum_scatter(
        jnp.concatenate(partials, axis=0), "head", scatter_dimension=0, tiled=True
    ).astype(jnp.float32)
    share = rows // heads_axis
    share_valid = lax.dynamic_slice(valid, (h * share, 0), (share, LANES))[:, :1] > 0
    return jnp.where(share_valid, summed_rows + b_proj, 0.0).astype(jnp.bfloat16)


def solution(mesh):
    return jax.shard_map(
        shards,
        mesh=mesh,
        in_specs=(
            P("region", None),
            P(),
            P(),
            P(None, None, "head"),
            P(None, "head"),
            P("head", None),
            P(),
            P(),
            P(),
        ),
        out_specs=P(("region", "head"), None),
        check_vma=False,
    )
```

```python
import functools

import jax
import jax.numpy as jnp
from jax import lax
from jax.experimental import pallas as pl
from jax.experimental.pallas import tpu as pltpu
from jax.sharding import PartitionSpec as P

HD = 16
PATCH = 1024
BS = 32
LANES = 128

epsilon = 1e-05
LOG2E = 1.4426950408889634
MESH = pl.DeviceIdType.MESH


def pack_kernel(total, parts, tile, pack_ref, head_ref, x_ref, gain_ref, bias_ref, out_ref, own):
    rows, depth = x_ref.shape
    width = depth // parts
    h = head_ref[0]

    def pick(value):
        chosen = value[:, :width]
        for part in range(1, parts):
            chosen = jnp.where(h == part, value[:, part * width:(part + 1) * width], chosen)
        return chosen

    gain = pick(gain_ref[...])
    bias = pick(bias_ref[...])

    def normalize(i, carry):
        part = pl.ds(pl.multiple_of(i * tile, tile), tile)
        values = x_ref[part, :].astype(jnp.float32)
        centred = values - jnp.mean(values, axis=-1, keepdims=True)
        row_var = jnp.mean(centred * centred, axis=-1, keepdims=True)
        own[part, :] = (pick(centred) * lax.rsqrt(row_var + epsilon) * gain + bias).astype(
            jnp.bfloat16
        )
        return carry

    lax.fori_loop(0, rows // tile, normalize, 0)

    def pack(j, carry):
        source = pl.multiple_of(pack_ref[j] * BS, BS)
        out_ref[pl.ds(pl.multiple_of(j * BS, BS), BS), :] = own[pl.ds(source, BS), :]
        return carry

    lax.fori_loop(0, total, pack, 0, unroll=8)


def pack_blocks(points, ln_gain, ln_bias, head, pack_table, parts, tile=256):
    total = pack_table.shape[0]
    rows, depth = points.shape
    vmem = pl.BlockSpec(memory_space=pltpu.VMEM)
    smem = pl.BlockSpec(memory_space=pltpu.SMEM)
    return pl.pallas_call(
        functools.partial(pack_kernel, total, parts, tile),
        out_shape=jax.ShapeDtypeStruct((total * BS, depth // parts), jnp.bfloat16),
        in_specs=[smem, smem, vmem, vmem, vmem],
        out_specs=vmem,
        scratch_shapes=[pltpu.VMEM((rows, depth // parts), jnp.bfloat16)],
        name="pack",
    )(pack_table, head.reshape(1), points, ln_gain.reshape(1, -1), ln_bias.reshape(1, -1))


def exchange_kernel(
    regions, heads_axis, chunk,
    send, recv, own_sem, send_sem, recv_sem, fsend_sem, frecv_sem,
):
    r = lax.axis_index("region")
    h = lax.axis_index("head")

    barrier = pltpu.get_barrier_semaphore()

    def greet(d, carry):
        pl.semaphore_signal(
            barrier, inc=1, device_id={"region": lax.rem(r + d, regions)}, device_id_type=MESH
        )
        return carry

    lax.fori_loop(1, regions, greet, 0)
    for e in range(1, heads_axis):
        pl.semaphore_signal(
            barrier, inc=1, device_id={"head": lax.rem(h + e, heads_axis)}, device_id_type=MESH
        )
    pl.semaphore_wait(barrier, regions - 1 + heads_axis - 1)

    def rows(s):
        return pl.ds(pl.multiple_of(s * chunk, chunk), chunk)

    def to_region(t):
        return pltpu.make_async_remote_copy(
            src_ref=send.at[rows(t)],
            dst_ref=recv.at[h, rows(r)],
            send_sem=send_sem.at[t],
            recv_sem=recv_sem.at[r],
            device_id={"region": t},
            device_id_type=MESH,
        )

    def from_region(s):
        return pltpu.make_async_remote_copy(
            src_ref=send.at[rows(s)],
            dst_ref=recv.at[h, rows(s)],
            send_sem=send_sem.at[s],
            recv_sem=recv_sem.at[s],
            device_id={"region": s},
            device_id_type=MESH,
        )

    def to_head(e, s, source):
        return pltpu.make_async_remote_copy(
            src_ref=source,
            dst_ref=recv.at[h, rows(s)],
            send_sem=fsend_sem.at[e, s],
            recv_sem=frecv_sem.at[h, s],
            device_id={"head": lax.rem(h + e, heads_axis)},
            device_id_type=MESH,
        )

    def from_head(e, s):
        other = lax.rem(h + e, heads_axis)
        return pltpu.make_async_remote_copy(
            src_ref=recv.at[other, rows(s)],
            dst_ref=recv.at[other, rows(s)],
            send_sem=fsend_sem.at[e, s],
            recv_sem=frecv_sem.at[other, s],
            device_id={"head": other},
            device_id_type=MESH,
        )

    def push(d, carry):
        to_region(lax.rem(r + d, regions)).start()
        return carry

    own = pltpu.make_async_copy(send.at[rows(r)], recv.at[h, rows(r)], own_sem)
    own.start()
    for e in range(1, heads_axis):
        to_head(e, r, send.at[rows(r)]).start()
    lax.fori_loop(1, regions, push, 0)

    def relay(d, carry):
        s = lax.rem(r - d + regions, regions)
        from_region(s).wait_recv()
        for e in range(1, heads_axis):
            to_head(e, s, recv.at[h, rows(s)]).start()
        return carry

    lax.fori_loop(1, regions, relay, 0)
    own.wait()

    def finish(d, carry):
        s = lax.rem(r - d + regions, regions)
        for e in range(1, heads_axis):
            from_head(e, s).wait_recv()
            to_head(e, s, recv.at[h, rows(s)]).wait_send()
        return carry

    lax.fori_loop(0, regions, finish, 0)

    def drain(d, carry):
        from_region(lax.rem(r + d, regions)).wait_send()
        return carry

    lax.fori_loop(1, regions, drain, 0)


def exchange(packed, regions, heads_axis):
    rows, width = packed.shape
    return pl.pallas_call(
        functools.partial(exchange_kernel, regions, heads_axis, rows // regions),
        out_shape=jax.ShapeDtypeStruct((heads_axis, rows, width), jnp.bfloat16),
        in_specs=[pl.BlockSpec(memory_space=pltpu.VMEM)],
        out_specs=pl.BlockSpec(memory_space=pltpu.VMEM),
        scratch_shapes=[
            pltpu.SemaphoreType.DMA,
            pltpu.SemaphoreType.DMA((regions,)),
            pltpu.SemaphoreType.DMA((regions,)),
            pltpu.SemaphoreType.DMA((heads_axis, regions)),
            pltpu.SemaphoreType.DMA((heads_axis, regions)),
        ],
        compiler_params=pltpu.CompilerParams(collective_id=0, has_side_effects=True),
        name="exchange",
    )(packed)


def project_kernel(
    blocks, tile, slot_ref, count_ref, recv, valid_ref, w_ref, b_ref, out_ref, full
):
    parts, _, piece = recv.shape
    width = w_ref.shape[1] // 3
    row_index = lax.broadcasted_iota(jnp.int32, (BS, piece), 0)

    def unpack(t, carry):
        source = pl.multiple_of(slot_ref[t] * BS, BS)
        count = count_ref[t]
        for part in range(parts):
            block = recv[part, pl.ds(source, BS), :].astype(jnp.float32)
            block = jnp.where(row_index < count, block, block[0:1, :])
            full[pl.ds(pl.multiple_of(t * BS, BS), BS), part * piece:(part + 1) * piece] = (
                block.astype(jnp.bfloat16)
            )
        return carry

    def multiply(i, carry):
        first = i * (tile // BS)
        lax.fori_loop(0, tile // BS, lambda t, c: unpack(first + t, c), 0, unroll=4)
        part = pl.ds(pl.multiple_of(i * tile, tile), tile)
        for c in range(3):
            columns = slice(c * width, (c + 1) * width)
            summed = jnp.dot(full[part, :], w_ref[:, columns], preferred_element_type=jnp.float32)
            summed = summed + b_ref[:, columns]
            if c == 0:
                summed = summed * HD ** (-0.5)
            if c == 2:
                keep = valid_ref[part, :].astype(jnp.float32)
                keep = jnp.concatenate([keep] * (width // LANES), axis=1)
                summed = jnp.where(keep > 0, summed, 0.0)
            out_ref[part, columns] = summed.astype(jnp.bfloat16)
        return carry

    lax.fori_loop(0, blocks * BS // tile, multiply, 0)


def project(recv, slot_table, own_counts, valid, weight, bias, tile=256):
    blocks = slot_table.shape[0]
    vmem = pl.BlockSpec(memory_space=pltpu.VMEM)
    smem = pl.BlockSpec(memory_space=pltpu.SMEM)
    return pl.pallas_call(
        functools.partial(project_kernel, blocks, tile),
        out_shape=jax.ShapeDtypeStruct((blocks * BS, weight.shape[1]), jnp.bfloat16),
        in_specs=[smem, smem, vmem, vmem, vmem, vmem],
        out_specs=vmem,
        scratch_shapes=[pltpu.VMEM((blocks * BS, weight.shape[0]), jnp.bfloat16)],
        name="project",
    )(slot_table, own_counts, recv, valid, weight, bias.reshape(1, -1))


def over_heads(heads, tile, q_ref, keys, vals, acc, den, ahead, peaks_out=None, peaks_in=None):
    queries, width = q_ref.shape
    lane = lax.broadcasted_iota(jnp.int32, (1, LANES), 1)
    steps = queries // tile
    per = LANES // HD

    for c in range(width // LANES):
        columns = slice(c * LANES, (c + 1) * LANES)
        count = min(per, heads - c * per)
        trip_heads = 4 if count % 4 == 0 else 2

        def score(n, i):
            mine = (lane // HD == n).astype(jnp.float32).astype(jnp.bfloat16)
            return lax.dot_general(
                q_ref[i * tile:(i + 1) * tile, columns] * mine, keys[:, columns],
                (((1,), (1,)), ((), ())), preferred_element_type=jnp.float32,
            )

        ahead[0] = score(0, 0)

        def several(trip, carry):
            order = [(trip_heads * trip + u, i) for u in range(trip_heads) for i in range(steps)]
            after = order[1:] + [(jnp.minimum(trip_heads * (trip + 1), count - 1), 0)]
            for turn, (n, i) in enumerate(order):
                part = slice(i * tile, (i + 1) * tile)
                ahead[(turn + 1) % 2] = score(*after[turn])
                scores = ahead[turn % 2]
                peak = jnp.max(scores, axis=-1, keepdims=True)
                if peaks_in is not None:
                    old = jnp.sum(
                        jnp.where(lane == n + c * per, peaks_in[part, :], 0.0),
                        axis=-1, keepdims=True,
                    )
                    peak = jnp.maximum(peak, old)
                    keep = jnp.exp(old - peak)
                if peaks_out is not None:
                    peaks_out[part, :] = jnp.where(
                        lane == n + c * per, peak, peaks_out[part, :]
                    )
                expo = jnp.exp(scores - peak).astype(jnp.bfloat16)
                result = jnp.dot(expo, vals[c], preferred_element_type=jnp.float32)
                mine = lane // HD == n
                over, under = acc[part, columns], den[part, columns]
                top, low = result[:, :LANES], result[:, LANES:]
                if peaks_in is not None:
                    top, low = over * keep + top, under * keep + low
                acc[part, columns] = jnp.where(mine, top, over)
                den[part, columns] = jnp.where(mine, low, under)
            return carry

        lax.fori_loop(0, count // trip_heads, several, 0)


def finish_heads(acc, den, w_ref, out_ref):
    attended = (acc[...] / den[...]).astype(jnp.bfloat16)
    out_ref[...] = jnp.dot(attended, w_ref[...], preferred_element_type=jnp.float32).astype(
        jnp.bfloat16
    )


def fill_values(vals, v_ref, on_ref, first):
    count = v_ref.shape[0]
    for c in range(vals.shape[0]):
        vals[c, first:first + count, :LANES] = v_ref[:, c * LANES:(c + 1) * LANES]
        vals[c, first:first + count, LANES:] = on_ref[...]


def attend_kernel(
    heads, tile,
    half_ref, q_ref, kn_ref, vn_ref, on_ref, kf_ref, vf_ref, of_ref, w_ref, out_ref,
    keys, vals, acc, den, ahead,
):
    near = kn_ref.shape[0]
    keys[:near, :] = kn_ref[...]
    keys[near:, :] = kf_ref[...]
    fill_values(vals, vn_ref, on_ref, 0)
    fill_values(vals, vf_ref, of_ref, near)
    acc[...] = jnp.zeros_like(acc)
    den[...] = jnp.ones_like(den)
    over_heads(heads, tile, q_ref, keys, vals, acc, den, ahead)
    finish_heads(acc, den, w_ref, out_ref)


def whole_block(*shape):
    return pl.BlockSpec(shape, lambda i, half: (0,) * len(shape))


def half_block(queries, width, column):
    return pl.BlockSpec((queries, width), lambda i, half: (half[0], column))


def attend_cost(heads, queries, keys, width):
    return pl.CostEstimate(
        flops=heads * queries * keys * width * 4,
        bytes_accessed=queries * width * 20,
        transcendentals=heads * queries * keys,
    )


def attend(half, qkv, valid, far_kv, far_valid, w_proj, heads, tile=512):
    width = w_proj.shape[0]
    columns = w_proj.shape[1]
    queries = far_kv.shape[0]
    whole = lambda *shape: pl.BlockSpec(shape, lambda i, half: (0,) * len(shape))
    part = lambda c, w=width: pl.BlockSpec((queries, w), lambda i, half: (half[0], c))
    return pl.pallas_call(
        functools.partial(attend_kernel, heads, tile),
        out_shape=jax.ShapeDtypeStruct((queries, columns), jnp.bfloat16),
        grid_spec=pltpu.PrefetchScalarGridSpec(
            num_scalar_prefetch=1,
            grid=(1,),
            in_specs=[
                part(0), part(1), part(2), part(0, LANES),
                pl.BlockSpec((queries, width), lambda i, half: (0, 0)),
                pl.BlockSpec((queries, width), lambda i, half: (0, 1)),
                whole(queries, LANES),
                whole(width, columns),
            ],
            out_specs=whole(queries, columns),
            scratch_shapes=[pltpu.VMEM((2 * queries, width), jnp.bfloat16)]
            + [pltpu.VMEM((width // LANES, 2 * queries, 2 * LANES), jnp.bfloat16)]
            + [pltpu.VMEM((queries, width), jnp.float32)] * 2
            + [pltpu.VMEM((2, tile, 2 * queries), jnp.float32)],
        ),
        cost_estimate=pl.CostEstimate(
            flops=heads * queries * 2 * queries * width * 4,
            bytes_accessed=queries * columns * 10,
            transcendentals=heads * queries * 2 * queries,
        ),
        name="attend",
    )(half.reshape(1), qkv, qkv, qkv, valid, far_kv, far_kv, far_valid, w_proj)


def gather_kernel(slots, pos_ref, x_ref, out_ref, taken):
    rows, depth = x_ref.shape
    parts, _, width = out_ref.shape
    blocks = rows // BS
    first = lax.axis_index("region") * blocks
    for d in range(taken.shape[0]):
        taken[d] = 0

    def place(i, carry):
        target = lax.div(pos_ref[first + i], blocks)
        used = taken[target]
        taken[target] = used + 1
        into = pl.ds(pl.multiple_of((target * slots + used) * BS, BS), BS)
        source = pl.ds(pl.multiple_of(i * BS, BS), BS)
        for part in range(parts):
            out_ref[part, into, :] = x_ref[source, part * width:(part + 1) * width]
        return carry

    lax.fori_loop(0, blocks, place, 0, unroll=4)


def gather_blocks(points, hilbert_pos, regions, slots, parts):
    rows, depth = points.shape
    vmem = pl.BlockSpec(memory_space=pltpu.VMEM)
    return pl.pallas_call(
        functools.partial(gather_kernel, slots),
        out_shape=jax.ShapeDtypeStruct(
            (parts, regions * slots * BS, depth // parts), jnp.bfloat16
        ),
        in_specs=[pl.BlockSpec(memory_space=pltpu.SMEM), vmem],
        out_specs=vmem,
        scratch_shapes=[pltpu.SMEM((regions,), jnp.int32)],
        name="gather_blocks",
    )(hilbert_pos, points)


def swap_kernel(
    regions, near,
    send, gain_ref, bias_ref, w_ref, b_ref, out_ref,
    recv, made, send_sem, recv_sem, relay_sem, leave_sem,
):
    r = lax.axis_index("region")
    h = lax.axis_index("head")
    other = 1 - h
    chunk = recv.shape[1] // regions
    piece = recv.shape[2]
    width = w_ref.shape[2]
    seat = lax.rem(r, near)
    level = lax.div(r, near)
    high = lax.div(level, 2)
    low = lax.rem(level, 2)
    whole = 2 * near

    barrier = pltpu.get_barrier_semaphore()

    def greet(d, carry):
        pl.semaphore_signal(
            barrier, inc=1, device_id={"region": lax.rem(r + d, regions)}, device_id_type=MESH
        )
        return carry

    lax.fori_loop(1, regions, greet, 0)
    pl.semaphore_signal(barrier, inc=1, device_id={"head": other}, device_id_type=MESH)
    pl.semaphore_wait(barrier, regions)

    def rows(s):
        return pl.ds(pl.multiple_of(s * chunk, chunk), chunk)

    def to_region(t, part):
        return pltpu.make_async_remote_copy(
            src_ref=send.at[part, rows(t)],
            dst_ref=recv.at[part, rows(r)],
            send_sem=send_sem.at[part, t],
            recv_sem=recv_sem.at[part, r],
            device_id={"region": t},
            device_id_type=MESH,
        )

    def arrival(s, part):
        return pltpu.make_async_remote_copy(
            src_ref=send.at[part, rows(s)],
            dst_ref=recv.at[part, rows(s)],
            send_sem=send_sem.at[part, s],
            recv_sem=recv_sem.at[part, s],
            device_id={"head": other},
            device_id_type=MESH,
        )

    def relay(s):
        return pltpu.make_async_remote_copy(
            src_ref=recv.at[h, rows(s)],
            dst_ref=recv.at[h, rows(s)],
            send_sem=relay_sem.at[s],
            recv_sem=recv_sem.at[h, s],
            device_id={"head": other},
            device_id_type=MESH,
        )

    def keep(part):
        return pltpu.make_async_copy(
            send.at[part, rows(r)], recv.at[part, rows(r)], recv_sem.at[part, r]
        )

    def target(i):
        group = lax.div(i, near)
        beyond = lax.div(group, 2)
        there = 2 * lax.rem(high + beyond, 2) + lax.rem(low + group, 2)
        return there * near + lax.rem(seat + i, near)

    def source(i):
        group = lax.div(i, near)
        beyond = lax.div(group, 2)
        inner = (1 - beyond) * low + beyond * high + group
        there = 2 * lax.rem(high + beyond, 2) + lax.rem(inner, 2)
        return there * near + lax.rem(seat + regions - i, near)

    def push_whole(i, carry):
        t = target(i)
        to_region(t, h).start()
        to_region(t, other).start()
        return carry

    def push_part(i, carry):
        to_region(target(i), h).start()
        return carry

    keep(0).start()
    keep(1).start()
    lax.fori_loop(1, whole, push_whole, 0)
    lax.fori_loop(whole, regions, push_part, 0)

    def project(s):
        part = rows(s)
        left = recv[0, part, :].astype(jnp.float32)
        right = recv[1, part, :].astype(jnp.float32)
        depth = 2 * piece
        mean = (
            jnp.sum(left, axis=-1, keepdims=True) + jnp.sum(right, axis=-1, keepdims=True)
        ) * (1.0 / depth)
        left = left - mean
        right = right - mean
        row_var = (
            jnp.sum(left * left, axis=-1, keepdims=True)
            + jnp.sum(right * right, axis=-1, keepdims=True)
        ) * (1.0 / depth)
        scale = lax.rsqrt(row_var + epsilon)
        left = (left * scale * gain_ref[:, :piece] + bias_ref[:, :piece]).astype(jnp.bfloat16)
        right = (right * scale * gain_ref[:, piece:] + bias_ref[:, piece:]).astype(jnp.bfloat16)
        for c in range(3):
            summed = jnp.dot(left, w_ref[c, :piece, :], preferred_element_type=jnp.float32)
            summed = summed + jnp.dot(
                right, w_ref[c, piece:, :], preferred_element_type=jnp.float32
            )
            summed = summed + b_ref[c:c + 1, :]
            if c == 0:
                summed = summed * (HD ** (-0.5) * LOG2E)
            made[part, c * width:(c + 1) * width] = summed.astype(jnp.bfloat16)

    def leave(s):
        return pltpu.make_async_copy(made.at[rows(s)], out_ref.at[rows(s)], leave_sem.at[s])

    def forward(i):
        s = source(i)
        arrival(s, h).wait_recv()
        relay(s).start()

    last = regions - near

    def close(i, carry):
        @pl.when((i >= 1) & (i < 1 + near))
        def _():
            forward(whole + i - 1)

        s = source(i)
        arrival(s, 0).wait_recv()
        arrival(s, 1).wait_recv()
        project(s)
        leave(s).start()
        return carry

    def distant(i, carry):
        @pl.when(i == last - 2)
        def _():
            forward(last)

        @pl.when((i >= last) & (i < regions - 1))
        def _():
            forward(i + 1)

        s = source(i)
        arrival(s, other).wait_recv()
        project(s)
        leave(s).start()
        return carry

    lax.fori_loop(0, whole, close, 0)
    lax.fori_loop(whole, regions, distant, 0)

    def drain_whole(i, carry):
        t = target(i)
        to_region(t, h).wait_send()
        to_region(t, other).wait_send()
        return carry

    def drain_part(i, carry):
        to_region(target(i), h).wait_send()
        relay(source(i)).wait_send()
        return carry

    def drain_leave(i, carry):
        leave(i).wait()
        return carry

    lax.fori_loop(1, whole, drain_whole, 0)
    lax.fori_loop(whole, regions, drain_part, 0)
    lax.fori_loop(0, regions, drain_leave, 0)


def swap(send, ln_gain, ln_bias, weight, bias, regions):
    parts, rows, piece = send.shape
    width = weight.shape[2]
    vmem = pl.BlockSpec(memory_space=pltpu.VMEM)
    return pl.pallas_call(
        functools.partial(swap_kernel, regions, regions // 4),
        out_shape=jax.ShapeDtypeStruct((rows, 3 * width), jnp.bfloat16),
        in_specs=[pl.BlockSpec(memory_space=pl.ANY), vmem, vmem, vmem, vmem],
        out_specs=pl.BlockSpec(memory_space=pl.ANY),
        scratch_shapes=[
            pltpu.VMEM((parts, rows, piece), jnp.bfloat16),
            pltpu.VMEM((rows, 3 * width), jnp.bfloat16),
            pltpu.SemaphoreType.DMA((parts, regions)),
            pltpu.SemaphoreType.DMA((parts, regions)),
            pltpu.SemaphoreType.DMA((regions,)),
            pltpu.SemaphoreType.DMA((regions,)),
        ],
        compiler_params=pltpu.CompilerParams(collective_id=1, has_side_effects=True),
        name="swap",
    )(send, ln_gain.reshape(1, -1), ln_bias.reshape(1, -1), weight, bias)


def unpack_kernel(slot_ref, count_ref, ext_ref, made, q_ref, k_ref, vt_ref, valid_ref, vals, sems):
    blocks = slot_ref.shape[0]
    width = q_ref.shape[1]
    near = (ext_ref.shape[1] - blocks) // 2

    def fetch(t, part, into):
        return pltpu.make_async_copy(
            made.at[
                pl.ds(pl.multiple_of(slot_ref[t] * BS, BS), BS), part * width:(part + 1) * width
            ],
            into.at[pl.ds(pl.multiple_of(t * BS, BS), BS)],
            sems.at[part, t],
        )

    def begin(t, carry):
        fetch(t, 2, vals).start()
        fetch(t, 1, k_ref).start()
        fetch(t, 0, q_ref).start()
        return carry

    lax.fori_loop(0, blocks, begin, 0)

    total = valid_ref.shape[1]
    spread = (
        lax.broadcasted_iota(jnp.int32, (ext_ref.shape[1], total), 1) // BS
        == lax.broadcasted_iota(jnp.int32, (ext_ref.shape[1], total), 0)
    ).astype(jnp.float32).astype(jnp.bfloat16)
    rows = valid_ref.shape[0]
    ext = jnp.broadcast_to(ext_ref[...].astype(jnp.float32), (rows, ext_ref.shape[1]))
    limit = jnp.dot(ext.astype(jnp.bfloat16), spread, preferred_element_type=jnp.float32)
    place = (lax.broadcasted_iota(jnp.int32, (rows, total), 1) % BS).astype(jnp.float32)
    valid_ref[...] = (place < limit).astype(jnp.float32).astype(jnp.bfloat16)

    def arrive_values(t, carry):
        fetch(t, 2, vals).wait()
        return carry

    lax.fori_loop(0, blocks, arrive_values, 0)
    step = 256
    for i in range(blocks * BS // step):
        part = slice(i * step, (i + 1) * step)
        own = valid_ref[0:1, near * BS + i * step:near * BS + (i + 1) * step].astype(jnp.float32)
        turned = jnp.transpose(vals[part, :].astype(jnp.float32))
        vt_ref[:, part] = (turned * own).astype(jnp.bfloat16)

    row_index = lax.broadcasted_iota(jnp.int32, (BS, width), 0)

    def mask(t, carry):
        fetch(t, 1, k_ref).wait()
        into = pl.ds(pl.multiple_of(t * BS, BS), BS)
        keys = k_ref[into, :].astype(jnp.float32)
        live = row_index < count_ref[near + t]
        k_ref[into, :] = jnp.where(live, keys, keys[0:1, :]).astype(jnp.bfloat16)
        return carry

    lax.fori_loop(0, blocks, mask, 0, unroll=4)

    def arrive_queries(t, carry):
        fetch(t, 0, q_ref).wait()
        return carry

    lax.fori_loop(0, blocks, arrive_queries, 0)


def unpack_blocks(made, slot_table, ext_counts):
    blocks = slot_table.shape[0]
    width = made.shape[1] // 3
    rows = blocks * BS
    vmem = pl.BlockSpec(memory_space=pltpu.VMEM)
    smem = pl.BlockSpec(memory_space=pltpu.SMEM)
    return pl.pallas_call(
        unpack_kernel,
        out_shape=[
            jax.ShapeDtypeStruct((rows, width), jnp.bfloat16),
            jax.ShapeDtypeStruct((rows, width), jnp.bfloat16),
            jax.ShapeDtypeStruct((width, rows), jnp.bfloat16),
            jax.ShapeDtypeStruct((HD, ext_counts.shape[0] * BS), jnp.bfloat16),
        ],
        in_specs=[smem, smem, vmem, pl.BlockSpec(memory_space=pl.ANY)],
        out_specs=[vmem] * 4,
        scratch_shapes=[
            pltpu.VMEM((rows, width), jnp.bfloat16), pltpu.SemaphoreType.DMA((3, blocks)),
        ],
        name="unpack_blocks",
    )(slot_table, ext_counts, ext_counts.reshape(1, -1), made)


def patch_kernel(
    regions, tile, group, chunk,
    q_ref, k_ref, vt_ref, valid_ref, w_ref, b_ref, out_ref,
    kh, vth, w_other, acc, peaks, att, att_in, ahead, ahead_peak,
    send_sem, recv_sem, side_sem,
):
    r = lax.axis_index("region")
    h = lax.axis_index("head")
    other = 1 - h
    half = kh.shape[1]
    width = q_ref.shape[1]
    heads = width // HD
    per = LANES // HD
    tiles = half // tile
    trips = heads // group
    lane = lax.broadcasted_iota(jnp.int32, (1, LANES), 1)

    def toward(a):
        return lax.rem(r + 1 - 2 * a + regions, regions)

    barrier = pltpu.get_barrier_semaphore()
    for a in range(2):
        pl.semaphore_signal(
            barrier, inc=1, device_id={"region": toward(a)}, device_id_type=MESH
        )
    pl.semaphore_signal(barrier, inc=1, device_id={"head": other}, device_id_type=MESH)
    pl.semaphore_wait(barrier, 3)

    def start_of(a):
        return pl.multiple_of(a * half, half)

    def halo(a, which):
        rows = pl.ds(start_of(1 - a), half)
        source = k_ref.at[rows, :] if which == 0 else vt_ref.at[:, rows]
        target = kh.at[a] if which == 0 else vth.at[a]
        return pltpu.make_async_remote_copy(
            src_ref=source, dst_ref=target,
            send_sem=send_sem.at[which, a], recv_sem=recv_sem.at[which, a],
            device_id={"region": toward(a)}, device_id_type=MESH,
        )

    def across(source, target, slot):
        return pltpu.make_async_remote_copy(
            src_ref=source, dst_ref=target,
            send_sem=side_sem.at[0, slot], recv_sem=side_sem.at[1, slot],
            device_id={"head": other}, device_id_type=MESH,
        )

    weights = across(w_ref, w_other, 0)
    halo(other, 0).start()
    halo(other, 1).start()
    halo(h, 0).start()
    halo(h, 1).start()
    weights.start()

    def score(slot, a, n, i, keys):
        columns = pl.ds(pl.multiple_of(n // per * LANES, LANES), LANES)
        mine = (lane // HD == n % per).astype(jnp.float32).astype(jnp.bfloat16)
        queries = q_ref[pl.ds(pl.multiple_of(a * half + i * tile, tile), tile), columns] * mine
        top = None
        for first in range(0, half, chunk):
            scores = lax.dot_general(
                keys(a, first, columns), queries, (((1,), (1,)), ((), ())),
                preferred_element_type=jnp.float32,
            )
            ahead[slot, first:first + chunk] = scores
            part = jnp.max(scores.reshape(chunk // 8, 8, tile), axis=0)
            top = part if top is None else jnp.maximum(top, part)
        ahead_peak[slot] = jnp.broadcast_to(jnp.max(top, axis=0, keepdims=True), (8, tile))

    def weigh(slot, a, n, peak, vals, flags):
        total = None
        rows = pl.ds(pl.multiple_of(n * HD, HD), HD)
        for first in range(0, half, chunk):
            scores = ahead[slot, first:first + chunk].reshape(chunk // 8, 8, tile)
            expo = jnp.exp2(scores - peak[None]).reshape(chunk, tile).astype(jnp.bfloat16)
            left = jnp.concatenate([vals(a, rows, first), flags(a, first)], axis=0)
            part = jnp.dot(left, expo, preferred_element_type=jnp.float32)
            total = part if total is None else total + part
        return total

    def run(trip_from, trip_to, limit, where, keys, use):
        def body(trip, carry):
            units = [(u, i) for u in range(group) for i in range(tiles)]
            for turn, (u, i) in enumerate(units):
                if turn + 1 < len(units):
                    v, j = units[turn + 1]
                    a, n = where(trip)
                    score((turn + 1) % 2, a, n + v, j, keys)
                else:
                    a, n = where(jnp.minimum(trip + 1, limit - 1))
                    score((turn + 1) % 2, a, n, 0, keys)
                a, n = where(trip)
                use(turn % 2, a, n + u, i)
            return carry

        lax.fori_loop(trip_from, trip_to, body, 0)

    def near_keys(a, first, columns):
        return k_ref[pl.ds(pl.multiple_of(a * half + first, chunk), chunk), columns]

    def near_vals(a, rows, first):
        return vt_ref[rows, pl.ds(pl.multiple_of(a * half + first, chunk), chunk)]

    def near_flags(a, first):
        return valid_ref[:, pl.ds(pl.multiple_of((a + 1) * half + first, chunk), chunk)]

    def far_keys(a, first, columns):
        return kh[a, first:first + chunk, columns]

    def far_vals(a, rows, first):
        return vth[a, rows, first:first + chunk]

    def far_flags(a, first):
        return valid_ref[:, pl.ds(pl.multiple_of(a * 3 * half + first, chunk), chunk)]

    def near_use(slot, a, n, i):
        peak = ahead_peak[slot]
        columns = slice(i * tile, (i + 1) * tile)
        acc[a, n, :, columns] = weigh(slot, a, n, peak, near_vals, near_flags)
        peaks[a, n, :, columns] = peak

    def far_use(slot, a, n, i):
        columns = slice(i * tile, (i + 1) * tile)
        old = peaks[a, n, :, columns]
        peak = jnp.maximum(ahead_peak[slot], old)
        keep = jnp.exp2(old - peak)
        total = weigh(slot, a, n, peak, far_vals, far_flags)
        before = acc[a, n, :, columns].reshape(2 * HD // 8, 8, tile)
        total = total + (before * keep[None]).reshape(2 * HD, tile)
        att[a, pl.ds(pl.multiple_of(n * HD, HD), HD), columns] = (
            total[:HD] / total[HD:]
        ).astype(jnp.bfloat16)

    def near_where(trip):
        late = lax.div(trip, trips)
        return lax.rem(other + late, 2), lax.rem(trip, trips) * group

    score(0, other, 0, 0, near_keys)
    run(0, 2 * trips, 2 * trips, near_where, near_keys, near_use)

    halo(other, 0).wait_recv()
    halo(other, 1).wait_recv()
    score(0, other, 0, 0, far_keys)
    run(0, trips, trips, lambda trip: (other, trip * group), far_keys, far_use)

    halo(h, 0).wait_recv()
    halo(h, 1).wait_recv()
    score(0, h, 0, 0, far_keys)
    swap_att = across(att.at[other], att_in, 1)
    run(0, 1, trips, lambda trip: (h, trip * group), far_keys, far_use)
    swap_att.start()
    run(1, trips, trips, lambda trip: (h, trip * group), far_keys, far_use)

    def share(attended, weight):
        return lax.dot_general(
            attended, weight, (((0,), (0,)), ((), ())), preferred_element_type=jnp.float32
        ).astype(jnp.bfloat16).astype(jnp.float32)

    flags = valid_ref[:, pl.ds(pl.multiple_of((h + 1) * half, half), half)]
    ones = jnp.full((HD, out_ref.shape[1]), 1.0 / HD, jnp.bfloat16)
    own = share(att[h], w_ref[...]) + b_ref[...]
    live = lax.dot_general(
        flags, ones, (((0,), (0,)), ((), ())), preferred_element_type=jnp.float32
    )
    weights.wait_recv()
    swap_att.wait_recv()
    update = own + share(att_in[...], w_other[...])
    out_ref[...] = jnp.where(live > 0.5, update, 0.0).astype(jnp.bfloat16)
    weights.wait_send()
    swap_att.wait_send()
    for a in range(2):
        for which in range(2):
            halo(a, which).wait_send()


def attend_patches(q, k, vt, valid, w_proj, b_proj, regions, tile=256, group=4, chunk=256):
    rows, width = q.shape
    half = rows // 2
    heads = width // HD
    columns = w_proj.shape[1]
    vmem = pl.BlockSpec(memory_space=pltpu.VMEM)
    return pl.pallas_call(
        functools.partial(patch_kernel, regions, tile, group, chunk),
        out_shape=jax.ShapeDtypeStruct((half, columns), jnp.bfloat16),
        in_specs=[vmem] * 6,
        out_specs=vmem,
        scratch_shapes=[
            pltpu.VMEM((2, half, width), jnp.bfloat16),
            pltpu.VMEM((2, width, half), jnp.bfloat16),
            pltpu.VMEM((width, columns), jnp.bfloat16),
            pltpu.VMEM((2, heads, 2 * HD, half), jnp.float32),
            pltpu.VMEM((2, heads, 8, half), jnp.float32),
            pltpu.VMEM((2, width, half), jnp.bfloat16),
            pltpu.VMEM((width, half), jnp.bfloat16),
            pltpu.VMEM((2, half, tile), jnp.float32),
            pltpu.VMEM((2, 8, tile), jnp.float32),
            pltpu.SemaphoreType.DMA((2, 2)),
            pltpu.SemaphoreType.DMA((2, 2)),
            pltpu.SemaphoreType.DMA((2, 2)),
        ],
        compiler_params=pltpu.CompilerParams(collective_id=2, has_side_effects=True),
        name="attend_patches",
    )(q, k, vt, valid, w_proj, b_proj.reshape(1, -1))


def shards(points, ln_gain, ln_bias, w_qkv, b_qkv, w_proj, b_proj, counts, hilbert_pos):
    regions = lax.axis_size("region")
    heads_axis = lax.axis_size("head")
    r = lax.axis_index("region")
    h = lax.axis_index("head")
    rows, model_width = points.shape
    group_width = w_qkv.shape[2]
    heads = group_width // HD
    width = max(group_width, LANES)
    blocks = rows // BS
    total_blocks = blocks * regions
    slots = max(2, 2 * blocks // regions)
    half_rows = PATCH // 2
    half_blocks = half_rows // BS

    position = jnp.arange(blocks, dtype=jnp.int32)
    my_dest = lax.dynamic_slice_in_dim(hilbert_pos, r * blocks, blocks) // blocks
    earlier = (my_dest[:, None] == my_dest[None, :]) & (position[None, :] < position[:, None])
    my_slot = my_dest * slots + jnp.sum(earlier, axis=1, dtype=jnp.int32)
    pack_table = jnp.sum(
        jnp.where(
            my_slot[None, :] == jnp.arange(regions * slots, dtype=jnp.int32)[:, None],
            position[None, :], 0,
        ),
        axis=1, dtype=jnp.int32,
    )
    every = jnp.arange(total_blocks, dtype=jnp.int32)
    ext = (
        r * blocks - half_blocks + jnp.arange(blocks + 2 * half_blocks, dtype=jnp.int32)
        + total_blocks
    ) % total_blocks
    here = hilbert_pos[None, :] == ext[:, None]
    ext_counts = jnp.sum(jnp.where(here, counts[None, :], 0), axis=1, dtype=jnp.int32)
    origin = jnp.sum(
        jnp.where(here[half_blocks:half_blocks + blocks], every[None, :], 0),
        axis=1, dtype=jnp.int32,
    )
    same = (
        (every[None, :] < origin[:, None])
        & (every[None, :] // blocks == origin[:, None] // blocks)
        & (hilbert_pos[None, :] // blocks == r)
    )
    slot_table = origin // blocks * slots + jnp.sum(same, axis=1, dtype=jnp.int32)
    own_counts = ext_counts[half_blocks:half_blocks + blocks]
    valid_ext = (
        jnp.arange(BS, dtype=jnp.int32)[None, :, None] < ext_counts[:, None, None]
    )
    valid_ext = jnp.broadcast_to(valid_ext, (blocks + 2 * half_blocks, BS, LANES))
    valid_ext = valid_ext.reshape(-1, LANES).astype(jnp.bfloat16)

    pad = width - group_width
    valid = valid_ext[half_rows:half_rows + rows]
    w_out = jnp.pad(w_proj, ((0, pad), (0, 0)))
    if heads_axis == 2:
        send = gather_blocks(points, hilbert_pos, regions, slots, heads_axis)
        made = swap(
            send, ln_gain, ln_bias, jnp.transpose(w_qkv, (1, 0, 2)), b_qkv, regions
        )
        q, k, vt, flags = unpack_blocks(made, slot_table, ext_counts)
        return attend_patches(q, k, vt, flags, w_proj, b_proj, regions)

    packed = pack_blocks(points, ln_gain, ln_bias, h, pack_table, heads_axis)
    recv = exchange(packed, regions, heads_axis)
    weight = jnp.pad(w_qkv, ((0, 0), (0, 0), (0, pad))).reshape(model_width, 3 * width)
    bias = jnp.pad(b_qkv, ((0, 0), (0, pad))).reshape(3 * width)
    qkv = project(recv, slot_table, own_counts, valid, weight, bias)

    up = [(i, (i + 1) % regions) for i in range(regions)]
    down = [(j, i) for i, j in up]
    kv = qkv[:, width:]
    before = lax.ppermute(kv[rows - half_rows:], "region", up)
    after = lax.ppermute(kv[:half_rows], "region", down)
    partials = [
        attend(jnp.int32(0), qkv, valid, before, valid_ext[:half_rows], w_out, heads),
        attend(jnp.int32(1), qkv, valid, after, valid_ext[rows + half_rows:], w_out, heads),
    ]
    summed_rows = lax.psum_scatter(
        jnp.concatenate(partials, axis=0), "head", scatter_dimension=0, tiled=True
    ).astype(jnp.float32)
    share = rows // heads_axis
    share_valid = lax.dynamic_slice(valid, (h * share, 0), (share, LANES))[:, :1] > 0
    return jnp.where(share_valid, summed_rows + b_proj, 0.0).astype(jnp.bfloat16)


def solution(mesh):
    return jax.shard_map(
        shards,
        mesh=mesh,
        in_specs=(
            P("region", None),
            P(),
            P(),
            P(None, None, "head"),
            P(None, "head"),
            P("head", None),
            P(),
            P(),
            P(),
        ),
        out_specs=P(("region", "head"), None),
        check_vma=False,
    )
```

```python
import functools

import jax
import jax.numpy as jnp
from jax import lax
from jax.experimental import pallas as pl
from jax.experimental.pallas import tpu as pltpu
from jax.sharding import PartitionSpec as P

HD = 16
PATCH = 1024
BS = 32
LANES = 128

epsilon = 1e-05
LOG2E = 1.4426950408889634
MESH = pl.DeviceIdType.MESH


def pack_kernel(total, parts, tile, pack_ref, head_ref, x_ref, gain_ref, bias_ref, out_ref, own):
    rows, depth = x_ref.shape
    width = depth // parts
    h = head_ref[0]

    def pick(value):
        chosen = value[:, :width]
        for part in range(1, parts):
            chosen = jnp.where(h == part, value[:, part * width:(part + 1) * width], chosen)
        return chosen

    gain = pick(gain_ref[...])
    bias = pick(bias_ref[...])

    def normalize(i, carry):
        part = pl.ds(pl.multiple_of(i * tile, tile), tile)
        values = x_ref[part, :].astype(jnp.float32)
        centred = values - jnp.mean(values, axis=-1, keepdims=True)
        row_var = jnp.mean(centred * centred, axis=-1, keepdims=True)
        own[part, :] = (pick(centred) * lax.rsqrt(row_var + epsilon) * gain + bias).astype(
            jnp.bfloat16
        )
        return carry

    lax.fori_loop(0, rows // tile, normalize, 0)

    def pack(j, carry):
        source = pl.multiple_of(pack_ref[j] * BS, BS)
        out_ref[pl.ds(pl.multiple_of(j * BS, BS), BS), :] = own[pl.ds(source, BS), :]
        return carry

    lax.fori_loop(0, total, pack, 0, unroll=8)


def pack_blocks(points, ln_gain, ln_bias, head, pack_table, parts, tile=256):
    total = pack_table.shape[0]
    rows, depth = points.shape
    vmem = pl.BlockSpec(memory_space=pltpu.VMEM)
    smem = pl.BlockSpec(memory_space=pltpu.SMEM)
    return pl.pallas_call(
        functools.partial(pack_kernel, total, parts, tile),
        out_shape=jax.ShapeDtypeStruct((total * BS, depth // parts), jnp.bfloat16),
        in_specs=[smem, smem, vmem, vmem, vmem],
        out_specs=vmem,
        scratch_shapes=[pltpu.VMEM((rows, depth // parts), jnp.bfloat16)],
        name="pack",
    )(pack_table, head.reshape(1), points, ln_gain.reshape(1, -1), ln_bias.reshape(1, -1))


def exchange_kernel(
    regions, heads_axis, chunk,
    send, recv, own_sem, send_sem, recv_sem, fsend_sem, frecv_sem,
):
    r = lax.axis_index("region")
    h = lax.axis_index("head")

    barrier = pltpu.get_barrier_semaphore()

    def greet(d, carry):
        pl.semaphore_signal(
            barrier, inc=1, device_id={"region": lax.rem(r + d, regions)}, device_id_type=MESH
        )
        return carry

    lax.fori_loop(1, regions, greet, 0)
    for e in range(1, heads_axis):
        pl.semaphore_signal(
            barrier, inc=1, device_id={"head": lax.rem(h + e, heads_axis)}, device_id_type=MESH
        )
    pl.semaphore_wait(barrier, regions - 1 + heads_axis - 1)

    def rows(s):
        return pl.ds(pl.multiple_of(s * chunk, chunk), chunk)

    def to_region(t):
        return pltpu.make_async_remote_copy(
            src_ref=send.at[rows(t)],
            dst_ref=recv.at[h, rows(r)],
            send_sem=send_sem.at[t],
            recv_sem=recv_sem.at[r],
            device_id={"region": t},
            device_id_type=MESH,
        )

    def from_region(s):
        return pltpu.make_async_remote_copy(
            src_ref=send.at[rows(s)],
            dst_ref=recv.at[h, rows(s)],
            send_sem=send_sem.at[s],
            recv_sem=recv_sem.at[s],
            device_id={"region": s},
            device_id_type=MESH,
        )

    def to_head(e, s, source):
        return pltpu.make_async_remote_copy(
            src_ref=source,
            dst_ref=recv.at[h, rows(s)],
            send_sem=fsend_sem.at[e, s],
            recv_sem=frecv_sem.at[h, s],
            device_id={"head": lax.rem(h + e, heads_axis)},
            device_id_type=MESH,
        )

    def from_head(e, s):
        other = lax.rem(h + e, heads_axis)
        return pltpu.make_async_remote_copy(
            src_ref=recv.at[other, rows(s)],
            dst_ref=recv.at[other, rows(s)],
            send_sem=fsend_sem.at[e, s],
            recv_sem=frecv_sem.at[other, s],
            device_id={"head": other},
            device_id_type=MESH,
        )

    def push(d, carry):
        to_region(lax.rem(r + d, regions)).start()
        return carry

    own = pltpu.make_async_copy(send.at[rows(r)], recv.at[h, rows(r)], own_sem)
    own.start()
    for e in range(1, heads_axis):
        to_head(e, r, send.at[rows(r)]).start()
    lax.fori_loop(1, regions, push, 0)

    def relay(d, carry):
        s = lax.rem(r - d + regions, regions)
        from_region(s).wait_recv()
        for e in range(1, heads_axis):
            to_head(e, s, recv.at[h, rows(s)]).start()
        return carry

    lax.fori_loop(1, regions, relay, 0)
    own.wait()

    def finish(d, carry):
        s = lax.rem(r - d + regions, regions)
        for e in range(1, heads_axis):
            from_head(e, s).wait_recv()
            to_head(e, s, recv.at[h, rows(s)]).wait_send()
        return carry

    lax.fori_loop(0, regions, finish, 0)

    def drain(d, carry):
        from_region(lax.rem(r + d, regions)).wait_send()
        return carry

    lax.fori_loop(1, regions, drain, 0)


def exchange(packed, regions, heads_axis):
    rows, width = packed.shape
    return pl.pallas_call(
        functools.partial(exchange_kernel, regions, heads_axis, rows // regions),
        out_shape=jax.ShapeDtypeStruct((heads_axis, rows, width), jnp.bfloat16),
        in_specs=[pl.BlockSpec(memory_space=pltpu.VMEM)],
        out_specs=pl.BlockSpec(memory_space=pltpu.VMEM),
        scratch_shapes=[
            pltpu.SemaphoreType.DMA,
            pltpu.SemaphoreType.DMA((regions,)),
            pltpu.SemaphoreType.DMA((regions,)),
            pltpu.SemaphoreType.DMA((heads_axis, regions)),
            pltpu.SemaphoreType.DMA((heads_axis, regions)),
        ],
        compiler_params=pltpu.CompilerParams(collective_id=0, has_side_effects=True),
        name="exchange",
    )(packed)


def project_kernel(
    blocks, tile, slot_ref, count_ref, recv, valid_ref, w_ref, b_ref, out_ref, full
):
    parts, _, piece = recv.shape
    width = w_ref.shape[1] // 3
    row_index = lax.broadcasted_iota(jnp.int32, (BS, piece), 0)

    def unpack(t, carry):
        source = pl.multiple_of(slot_ref[t] * BS, BS)
        count = count_ref[t]
        for part in range(parts):
            block = recv[part, pl.ds(source, BS), :].astype(jnp.float32)
            block = jnp.where(row_index < count, block, block[0:1, :])
            full[pl.ds(pl.multiple_of(t * BS, BS), BS), part * piece:(part + 1) * piece] = (
                block.astype(jnp.bfloat16)
            )
        return carry

    def multiply(i, carry):
        first = i * (tile // BS)
        lax.fori_loop(0, tile // BS, lambda t, c: unpack(first + t, c), 0, unroll=4)
        part = pl.ds(pl.multiple_of(i * tile, tile), tile)
        for c in range(3):
            columns = slice(c * width, (c + 1) * width)
            summed = jnp.dot(full[part, :], w_ref[:, columns], preferred_element_type=jnp.float32)
            summed = summed + b_ref[:, columns]
            if c == 0:
                summed = summed * HD ** (-0.5)
            if c == 2:
                keep = valid_ref[part, :].astype(jnp.float32)
                keep = jnp.concatenate([keep] * (width // LANES), axis=1)
                summed = jnp.where(keep > 0, summed, 0.0)
            out_ref[part, columns] = summed.astype(jnp.bfloat16)
        return carry

    lax.fori_loop(0, blocks * BS // tile, multiply, 0)


def project(recv, slot_table, own_counts, valid, weight, bias, tile=256):
    blocks = slot_table.shape[0]
    vmem = pl.BlockSpec(memory_space=pltpu.VMEM)
    smem = pl.BlockSpec(memory_space=pltpu.SMEM)
    return pl.pallas_call(
        functools.partial(project_kernel, blocks, tile),
        out_shape=jax.ShapeDtypeStruct((blocks * BS, weight.shape[1]), jnp.bfloat16),
        in_specs=[smem, smem, vmem, vmem, vmem, vmem],
        out_specs=vmem,
        scratch_shapes=[pltpu.VMEM((blocks * BS, weight.shape[0]), jnp.bfloat16)],
        name="project",
    )(slot_table, own_counts, recv, valid, weight, bias.reshape(1, -1))


def over_heads(heads, tile, q_ref, keys, vals, acc, den, ahead, peaks_out=None, peaks_in=None):
    queries, width = q_ref.shape
    lane = lax.broadcasted_iota(jnp.int32, (1, LANES), 1)
    steps = queries // tile
    per = LANES // HD

    for c in range(width // LANES):
        columns = slice(c * LANES, (c + 1) * LANES)
        count = min(per, heads - c * per)
        trip_heads = 4 if count % 4 == 0 else 2

        def score(n, i):
            mine = (lane // HD == n).astype(jnp.float32).astype(jnp.bfloat16)
            return lax.dot_general(
                q_ref[i * tile:(i + 1) * tile, columns] * mine, keys[:, columns],
                (((1,), (1,)), ((), ())), preferred_element_type=jnp.float32,
            )

        ahead[0] = score(0, 0)

        def several(trip, carry):
            order = [(trip_heads * trip + u, i) for u in range(trip_heads) for i in range(steps)]
            after = order[1:] + [(jnp.minimum(trip_heads * (trip + 1), count - 1), 0)]
            for turn, (n, i) in enumerate(order):
                part = slice(i * tile, (i + 1) * tile)
                ahead[(turn + 1) % 2] = score(*after[turn])
                scores = ahead[turn % 2]
                peak = jnp.max(scores, axis=-1, keepdims=True)
                if peaks_in is not None:
                    old = jnp.sum(
                        jnp.where(lane == n + c * per, peaks_in[part, :], 0.0),
                        axis=-1, keepdims=True,
                    )
                    peak = jnp.maximum(peak, old)
                    keep = jnp.exp(old - peak)
                if peaks_out is not None:
                    peaks_out[part, :] = jnp.where(
                        lane == n + c * per, peak, peaks_out[part, :]
                    )
                expo = jnp.exp(scores - peak).astype(jnp.bfloat16)
                result = jnp.dot(expo, vals[c], preferred_element_type=jnp.float32)
                mine = lane // HD == n
                over, under = acc[part, columns], den[part, columns]
                top, low = result[:, :LANES], result[:, LANES:]
                if peaks_in is not None:
                    top, low = over * keep + top, under * keep + low
                acc[part, columns] = jnp.where(mine, top, over)
                den[part, columns] = jnp.where(mine, low, under)
            return carry

        lax.fori_loop(0, count // trip_heads, several, 0)


def finish_heads(acc, den, w_ref, out_ref):
    attended = (acc[...] / den[...]).astype(jnp.bfloat16)
    out_ref[...] = jnp.dot(attended, w_ref[...], preferred_element_type=jnp.float32).astype(
        jnp.bfloat16
    )


def fill_values(vals, v_ref, on_ref, first):
    count = v_ref.shape[0]
    for c in range(vals.shape[0]):
        vals[c, first:first + count, :LANES] = v_ref[:, c * LANES:(c + 1) * LANES]
        vals[c, first:first + count, LANES:] = on_ref[...]


def attend_kernel(
    heads, tile,
    half_ref, q_ref, kn_ref, vn_ref, on_ref, kf_ref, vf_ref, of_ref, w_ref, out_ref,
    keys, vals, acc, den, ahead,
):
    near = kn_ref.shape[0]
    keys[:near, :] = kn_ref[...]
    keys[near:, :] = kf_ref[...]
    fill_values(vals, vn_ref, on_ref, 0)
    fill_values(vals, vf_ref, of_ref, near)
    acc[...] = jnp.zeros_like(acc)
    den[...] = jnp.ones_like(den)
    over_heads(heads, tile, q_ref, keys, vals, acc, den, ahead)
    finish_heads(acc, den, w_ref, out_ref)


def whole_block(*shape):
    return pl.BlockSpec(shape, lambda i, half: (0,) * len(shape))


def half_block(queries, width, column):
    return pl.BlockSpec((queries, width), lambda i, half: (half[0], column))


def attend_cost(heads, queries, keys, width):
    return pl.CostEstimate(
        flops=heads * queries * keys * width * 4,
        bytes_accessed=queries * width * 20,
        transcendentals=heads * queries * keys,
    )


def attend(half, qkv, valid, far_kv, far_valid, w_proj, heads, tile=512):
    width = w_proj.shape[0]
    columns = w_proj.shape[1]
    queries = far_kv.shape[0]
    whole = lambda *shape: pl.BlockSpec(shape, lambda i, half: (0,) * len(shape))
    part = lambda c, w=width: pl.BlockSpec((queries, w), lambda i, half: (half[0], c))
    return pl.pallas_call(
        functools.partial(attend_kernel, heads, tile),
        out_shape=jax.ShapeDtypeStruct((queries, columns), jnp.bfloat16),
        grid_spec=pltpu.PrefetchScalarGridSpec(
            num_scalar_prefetch=1,
            grid=(1,),
            in_specs=[
                part(0), part(1), part(2), part(0, LANES),
                pl.BlockSpec((queries, width), lambda i, half: (0, 0)),
                pl.BlockSpec((queries, width), lambda i, half: (0, 1)),
                whole(queries, LANES),
                whole(width, columns),
            ],
            out_specs=whole(queries, columns),
            scratch_shapes=[pltpu.VMEM((2 * queries, width), jnp.bfloat16)]
            + [pltpu.VMEM((width // LANES, 2 * queries, 2 * LANES), jnp.bfloat16)]
            + [pltpu.VMEM((queries, width), jnp.float32)] * 2
            + [pltpu.VMEM((2, tile, 2 * queries), jnp.float32)],
        ),
        cost_estimate=pl.CostEstimate(
            flops=heads * queries * 2 * queries * width * 4,
            bytes_accessed=queries * columns * 10,
            transcendentals=heads * queries * 2 * queries,
        ),
        name="attend",
    )(half.reshape(1), qkv, qkv, qkv, valid, far_kv, far_kv, far_valid, w_proj)


def gather_kernel(slots, pos_ref, x_ref, out_ref, taken, sems):
    rows, depth = x_ref.shape
    parts, _, width = out_ref.shape
    blocks = rows // BS
    first = lax.axis_index("region") * blocks
    for d in range(taken.shape[0]):
        taken[d] = 0

    def move(i, part, into):
        return pltpu.make_async_copy(
            x_ref.at[
                pl.ds(pl.multiple_of(i * BS, BS), BS), part * width:(part + 1) * width
            ],
            out_ref.at[part, pl.ds(pl.multiple_of(into * BS, BS), BS)],
            sems.at[part, i],
        )

    def place(i, carry):
        target = lax.div(pos_ref[first + i], blocks)
        used = taken[target]
        taken[target] = used + 1
        for part in range(parts):
            move(i, part, target * slots + used).start()
        return carry

    def settle(i, carry):
        for part in range(parts):
            move(i, part, i).wait()
        return carry

    lax.fori_loop(0, blocks, place, 0, unroll=4)
    lax.fori_loop(0, blocks, settle, 0, unroll=4)


def gather_blocks(points, hilbert_pos, regions, slots, parts):
    rows, depth = points.shape
    vmem = pl.BlockSpec(memory_space=pltpu.VMEM)
    return pl.pallas_call(
        functools.partial(gather_kernel, slots),
        out_shape=jax.ShapeDtypeStruct(
            (parts, regions * slots * BS, depth // parts), jnp.bfloat16
        ),
        in_specs=[pl.BlockSpec(memory_space=pltpu.SMEM), vmem],
        out_specs=pl.BlockSpec(memory_space=pl.ANY),
        scratch_shapes=[
            pltpu.SMEM((regions,), jnp.int32), pltpu.SemaphoreType.DMA((parts, rows // BS)),
        ],
        name="gather_blocks",
    )(hilbert_pos, points)


def tabulate(slots, r, pos_ref, amount_ref, slot_ref, count_ref):
    total = pos_ref.shape[1]
    rows = 8
    span = slot_ref.shape[1]
    blocks = slots[1]
    position = jnp.broadcast_to(pos_ref[...], (rows, total))
    lane = lax.broadcasted_iota(jnp.int32, (rows, total), 1)
    within = lax.rem(lane, blocks)
    goal = lax.div(position, blocks)
    rank = jnp.zeros((rows, total), jnp.int32)
    for k in range(1, blocks):
        same = (pltpu.roll(goal, k, 1) == goal) & (within >= k)
        rank = rank + same.astype(jnp.int32)
    slot = (lax.div(lane, blocks) * slots[0] + rank).astype(jnp.float32).astype(jnp.bfloat16)
    amount = jnp.broadcast_to(amount_ref[...], (rows, total)).astype(jnp.float32)
    wanted = lax.rem(
        lax.broadcasted_iota(jnp.int32, (span, total), 0)
        + (r * blocks - (span - blocks) // 2 + total),
        total,
    )
    found = (jnp.broadcast_to(pos_ref[...], (span, total)) == wanted).astype(jnp.float32)
    found = found.astype(jnp.bfloat16)

    def pick(values):
        picked = lax.dot_general(
            values, found, (((1,), (1,)), ((), ())), preferred_element_type=jnp.float32
        )
        return picked[0:1, :].astype(jnp.int32)

    slot_ref[...] = pick(slot)
    count_ref[...] = pick(amount.astype(jnp.bfloat16))


def swap_kernel(
    regions, near, slots,
    send, pos_ref, amount_ref, gain_ref, bias_ref, w_ref, b_ref, out_ref, slot_ref, count_ref,
    recv, made, send_sem, recv_sem, relay_sem, leave_sem,
):
    r = lax.axis_index("region")
    h = lax.axis_index("head")
    other = 1 - h
    chunk = recv.shape[1] // regions
    piece = recv.shape[2]
    width = w_ref.shape[2]
    seat = lax.rem(r, near)
    level = lax.div(r, near)
    high = lax.div(level, 2)
    low = lax.rem(level, 2)
    whole = 2 * near

    barrier = pltpu.get_barrier_semaphore()

    def greet(d, carry):
        pl.semaphore_signal(
            barrier, inc=1, device_id={"region": lax.rem(r + d, regions)}, device_id_type=MESH
        )
        return carry

    lax.fori_loop(1, regions, greet, 0)
    pl.semaphore_signal(barrier, inc=1, device_id={"head": other}, device_id_type=MESH)
    pl.semaphore_wait(barrier, regions)

    def rows(s):
        return pl.ds(pl.multiple_of(s * chunk, chunk), chunk)

    def to_region(t, part):
        return pltpu.make_async_remote_copy(
            src_ref=send.at[part, rows(t)],
            dst_ref=recv.at[part, rows(r)],
            send_sem=send_sem.at[part, t],
            recv_sem=recv_sem.at[part, r],
            device_id={"region": t},
            device_id_type=MESH,
        )

    def arrival(s, part):
        return pltpu.make_async_remote_copy(
            src_ref=send.at[part, rows(s)],
            dst_ref=recv.at[part, rows(s)],
            send_sem=send_sem.at[part, s],
            recv_sem=recv_sem.at[part, s],
            device_id={"head": other},
            device_id_type=MESH,
        )

    def relay(s):
        return pltpu.make_async_remote_copy(
            src_ref=recv.at[h, rows(s)],
            dst_ref=recv.at[h, rows(s)],
            send_sem=relay_sem.at[s],
            recv_sem=recv_sem.at[h, s],
            device_id={"head": other},
            device_id_type=MESH,
        )

    def keep(part):
        return pltpu.make_async_copy(
            send.at[part, rows(r)], recv.at[part, rows(r)], recv_sem.at[part, r]
        )

    def target(i):
        group = lax.div(i, near)
        beyond = lax.div(group, 2)
        there = 2 * lax.rem(high + beyond, 2) + lax.rem(low + group, 2)
        return there * near + lax.rem(seat + i, near)

    def source(i):
        group = lax.div(i, near)
        beyond = lax.div(group, 2)
        inner = (1 - beyond) * low + beyond * high + group
        there = 2 * lax.rem(high + beyond, 2) + lax.rem(inner, 2)
        return there * near + lax.rem(seat + regions - i, near)

    def push_whole(i, carry):
        t = target(i)
        to_region(t, h).start()
        to_region(t, other).start()
        return carry

    def push_part(i, carry):
        to_region(target(i), h).start()
        return carry

    keep(0).start()
    keep(1).start()
    lax.fori_loop(1, whole, push_whole, 0)
    lax.fori_loop(whole, regions, push_part, 0)

    def project(s):
        part = rows(s)
        left = recv[0, part, :].astype(jnp.float32)
        right = recv[1, part, :].astype(jnp.float32)
        depth = 2 * piece
        mean = (
            jnp.sum(left, axis=-1, keepdims=True) + jnp.sum(right, axis=-1, keepdims=True)
        ) * (1.0 / depth)
        left = left - mean
        right = right - mean
        row_var = (
            jnp.sum(left * left, axis=-1, keepdims=True)
            + jnp.sum(right * right, axis=-1, keepdims=True)
        ) * (1.0 / depth)
        scale = lax.rsqrt(row_var + epsilon)
        left = (left * scale * gain_ref[:, :piece] + bias_ref[:, :piece]).astype(jnp.bfloat16)
        right = (right * scale * gain_ref[:, piece:] + bias_ref[:, piece:]).astype(jnp.bfloat16)
        for c in range(3):
            summed = jnp.dot(left, w_ref[c, :piece, :], preferred_element_type=jnp.float32)
            summed = summed + jnp.dot(
                right, w_ref[c, piece:, :], preferred_element_type=jnp.float32
            )
            summed = summed + b_ref[c:c + 1, :]
            if c == 0:
                summed = summed * (HD ** (-0.5) * LOG2E)
            made[part, c * width:(c + 1) * width] = summed.astype(jnp.bfloat16)

    def leave(s):
        return pltpu.make_async_copy(made.at[rows(s)], out_ref.at[rows(s)], leave_sem.at[s])

    def forward(i):
        s = source(i)
        arrival(s, h).wait_recv()
        relay(s).start()

    last = regions - near

    def close(i, carry):
        @pl.when((i >= 1) & (i < 1 + near))
        def _():
            forward(whole + i - 1)

        s = source(i)
        arrival(s, 0).wait_recv()
        arrival(s, 1).wait_recv()
        project(s)
        leave(s).start()
        return carry

    def distant(i, carry):
        @pl.when(i == last - 2)
        def _():
            forward(last)

        @pl.when((i >= last) & (i < regions - 1))
        def _():
            forward(i + 1)

        s = source(i)
        arrival(s, other).wait_recv()
        project(s)
        leave(s).start()
        return carry

    tabulate(slots, r, pos_ref, amount_ref, slot_ref, count_ref)
    lax.fori_loop(0, whole, close, 0)
    lax.fori_loop(whole, regions, distant, 0)

    def drain_whole(i, carry):
        t = target(i)
        to_region(t, h).wait_send()
        to_region(t, other).wait_send()
        return carry

    def drain_part(i, carry):
        to_region(target(i), h).wait_send()
        relay(source(i)).wait_send()
        return carry

    def drain_leave(i, carry):
        leave(i).wait()
        return carry

    lax.fori_loop(1, whole, drain_whole, 0)
    lax.fori_loop(whole, regions, drain_part, 0)
    lax.fori_loop(0, regions, drain_leave, 0)


def swap(send, hilbert_pos, counts, ln_gain, ln_bias, weight, bias, regions, slots, blocks, near):
    parts, rows, piece = send.shape
    width = weight.shape[2]
    vmem = pl.BlockSpec(memory_space=pltpu.VMEM)
    return pl.pallas_call(
        functools.partial(swap_kernel, regions, regions // 4, (slots, blocks)),
        out_shape=[
            jax.ShapeDtypeStruct((rows, 3 * width), jnp.bfloat16),
            jax.ShapeDtypeStruct((1, blocks + 2 * near), jnp.int32),
            jax.ShapeDtypeStruct((1, blocks + 2 * near), jnp.int32),
        ],
        in_specs=[pl.BlockSpec(memory_space=pl.ANY)] + [vmem] * 6,
        out_specs=[pl.BlockSpec(memory_space=pl.ANY), vmem, vmem],
        scratch_shapes=[
            pltpu.VMEM((parts, rows, piece), jnp.bfloat16),
            pltpu.VMEM((rows, 3 * width), jnp.bfloat16),
            pltpu.SemaphoreType.DMA((parts, regions)),
            pltpu.SemaphoreType.DMA((parts, regions)),
            pltpu.SemaphoreType.DMA((regions,)),
            pltpu.SemaphoreType.DMA((regions,)),
        ],
        compiler_params=pltpu.CompilerParams(collective_id=1, has_side_effects=True),
        name="swap",
    )(
        send, hilbert_pos.reshape(1, -1), counts.reshape(1, -1), ln_gain.reshape(1, -1),
        ln_bias.reshape(1, -1), weight, bias,
    )


def unpack_kernel(slot_ref, count_ref, ext_ref, made, q_ref, k_ref, vt_ref, valid_ref, vals, sems):
    blocks = q_ref.shape[0] // BS
    width = q_ref.shape[1]
    near = (ext_ref.shape[1] - blocks) // 2

    def fetch(t, part, into):
        return pltpu.make_async_copy(
            made.at[
                pl.ds(pl.multiple_of(slot_ref[0, near + t] * BS, BS), BS), part * width:(part + 1) * width
            ],
            into.at[pl.ds(pl.multiple_of(t * BS, BS), BS)],
            sems.at[part, t],
        )

    def begin(t, carry):
        fetch(t, 2, vals).start()
        fetch(t, 1, k_ref).start()
        fetch(t, 0, q_ref).start()
        return carry

    lax.fori_loop(0, blocks, begin, 0)

    total = valid_ref.shape[1]
    spread = (
        lax.broadcasted_iota(jnp.int32, (ext_ref.shape[1], total), 1) // BS
        == lax.broadcasted_iota(jnp.int32, (ext_ref.shape[1], total), 0)
    ).astype(jnp.float32).astype(jnp.bfloat16)
    rows = valid_ref.shape[0]
    ext = jnp.broadcast_to(ext_ref[...].astype(jnp.float32), (rows, ext_ref.shape[1]))
    limit = jnp.dot(ext.astype(jnp.bfloat16), spread, preferred_element_type=jnp.float32)
    place = (lax.broadcasted_iota(jnp.int32, (rows, total), 1) % BS).astype(jnp.float32)
    valid_ref[...] = (place < limit).astype(jnp.float32).astype(jnp.bfloat16)

    def arrive_values(t, carry):
        fetch(t, 2, vals).wait()
        return carry

    lax.fori_loop(0, blocks, arrive_values, 0)
    step = 256
    for i in range(blocks * BS // step):
        part = slice(i * step, (i + 1) * step)
        own = valid_ref[0:1, near * BS + i * step:near * BS + (i + 1) * step].astype(jnp.float32)
        turned = jnp.transpose(vals[part, :].astype(jnp.float32))
        vt_ref[:, part] = (turned * own).astype(jnp.bfloat16)

    row_index = lax.broadcasted_iota(jnp.int32, (BS, width), 0)

    def mask(t, carry):
        fetch(t, 1, k_ref).wait()
        into = pl.ds(pl.multiple_of(t * BS, BS), BS)
        keys = k_ref[into, :].astype(jnp.float32)
        live = row_index < count_ref[0, near + t]
        k_ref[into, :] = jnp.where(live, keys, keys[0:1, :]).astype(jnp.bfloat16)
        return carry

    lax.fori_loop(0, blocks, mask, 0, unroll=4)

    def arrive_queries(t, carry):
        fetch(t, 0, q_ref).wait()
        return carry

    lax.fori_loop(0, blocks, arrive_queries, 0)


def unpack_blocks(made, slot_table, ext_counts, blocks):
    width = made.shape[1] // 3
    rows = blocks * BS
    vmem = pl.BlockSpec(memory_space=pltpu.VMEM)
    smem = pl.BlockSpec(memory_space=pltpu.SMEM)
    return pl.pallas_call(
        unpack_kernel,
        out_shape=[
            jax.ShapeDtypeStruct((rows, width), jnp.bfloat16),
            jax.ShapeDtypeStruct((rows, width), jnp.bfloat16),
            jax.ShapeDtypeStruct((width, rows), jnp.bfloat16),
            jax.ShapeDtypeStruct((HD, ext_counts.shape[1] * BS), jnp.bfloat16),
        ],
        in_specs=[smem, smem, vmem, pl.BlockSpec(memory_space=pl.ANY)],
        out_specs=[vmem] * 4,
        scratch_shapes=[
            pltpu.VMEM((rows, width), jnp.bfloat16), pltpu.SemaphoreType.DMA((3, blocks)),
        ],
        name="unpack_blocks",
    )(slot_table, ext_counts, ext_counts, made)


def patch_kernel(
    regions, tile, group, chunk,
    q_ref, k_ref, vt_ref, valid_ref, w_ref, b_ref, out_ref,
    kh, vth, w_other, acc, peaks, att, att_in, ahead, ahead_peak,
    send_sem, recv_sem, side_sem,
):
    r = lax.axis_index("region")
    h = lax.axis_index("head")
    other = 1 - h
    half = kh.shape[1]
    width = q_ref.shape[1]
    heads = width // HD
    per = LANES // HD
    tiles = half // tile
    trips = heads // group
    lane = lax.broadcasted_iota(jnp.int32, (1, LANES), 1)

    def toward(a):
        return lax.rem(r + 1 - 2 * a + regions, regions)

    barrier = pltpu.get_barrier_semaphore()
    for a in range(2):
        pl.semaphore_signal(
            barrier, inc=1, device_id={"region": toward(a)}, device_id_type=MESH
        )
    pl.semaphore_signal(barrier, inc=1, device_id={"head": other}, device_id_type=MESH)
    pl.semaphore_wait(barrier, 3)

    def start_of(a):
        return pl.multiple_of(a * half, half)

    def halo(a, which):
        rows = pl.ds(start_of(1 - a), half)
        source = k_ref.at[rows, :] if which == 0 else vt_ref.at[:, rows]
        target = kh.at[a] if which == 0 else vth.at[a]
        return pltpu.make_async_remote_copy(
            src_ref=source, dst_ref=target,
            send_sem=send_sem.at[which, a], recv_sem=recv_sem.at[which, a],
            device_id={"region": toward(a)}, device_id_type=MESH,
        )

    def across(source, target, slot):
        return pltpu.make_async_remote_copy(
            src_ref=source, dst_ref=target,
            send_sem=side_sem.at[0, slot], recv_sem=side_sem.at[1, slot],
            device_id={"head": other}, device_id_type=MESH,
        )

    weights = across(w_ref, w_other, 0)
    halo(other, 0).start()
    halo(other, 1).start()
    halo(h, 0).start()
    halo(h, 1).start()
    weights.start()

    def score(slot, a, n, i, keys):
        columns = pl.ds(pl.multiple_of(n // per * LANES, LANES), LANES)
        mine = (lane // HD == n % per).astype(jnp.float32).astype(jnp.bfloat16)
        queries = q_ref[pl.ds(pl.multiple_of(a * half + i * tile, tile), tile), columns] * mine
        top = None
        for first in range(0, half, chunk):
            scores = lax.dot_general(
                keys(a, first, columns), queries, (((1,), (1,)), ((), ())),
                preferred_element_type=jnp.float32,
            )
            ahead[slot, first:first + chunk] = scores
            part = jnp.max(scores.reshape(chunk // 8, 8, tile), axis=0)
            top = part if top is None else jnp.maximum(top, part)
        ahead_peak[slot] = jnp.broadcast_to(jnp.max(top, axis=0, keepdims=True), (8, tile))

    def weigh(slot, a, n, peak, vals, flags):
        total = None
        rows = pl.ds(pl.multiple_of(n * HD, HD), HD)
        for first in range(0, half, chunk):
            scores = ahead[slot, first:first + chunk].reshape(chunk // 8, 8, tile)
            expo = jnp.exp2(scores - peak[None]).reshape(chunk, tile).astype(jnp.bfloat16)
            left = jnp.concatenate([vals(a, rows, first), flags(a, first)], axis=0)
            part = jnp.dot(left, expo, preferred_element_type=jnp.float32)
            total = part if total is None else total + part
        return total

    def run(trip_from, trip_to, limit, where, keys, use):
        def body(trip, carry):
            units = [(u, i) for u in range(group) for i in range(tiles)]
            for turn, (u, i) in enumerate(units):
                if turn + 1 < len(units):
                    v, j = units[turn + 1]
                    a, n = where(trip)
                    score((turn + 1) % 2, a, n + v, j, keys)
                else:
                    a, n = where(jnp.minimum(trip + 1, limit - 1))
                    score((turn + 1) % 2, a, n, 0, keys)
                a, n = where(trip)
                use(turn % 2, a, n + u, i)
            return carry

        lax.fori_loop(trip_from, trip_to, body, 0)

    def near_keys(a, first, columns):
        return k_ref[pl.ds(pl.multiple_of(a * half + first, chunk), chunk), columns]

    def near_vals(a, rows, first):
        return vt_ref[rows, pl.ds(pl.multiple_of(a * half + first, chunk), chunk)]

    def near_flags(a, first):
        return valid_ref[:, pl.ds(pl.multiple_of((a + 1) * half + first, chunk), chunk)]

    def far_keys(a, first, columns):
        return kh[a, first:first + chunk, columns]

    def far_vals(a, rows, first):
        return vth[a, rows, first:first + chunk]

    def far_flags(a, first):
        return valid_ref[:, pl.ds(pl.multiple_of(a * 3 * half + first, chunk), chunk)]

    def near_use(slot, a, n, i):
        peak = ahead_peak[slot]
        columns = slice(i * tile, (i + 1) * tile)
        acc[a, n, :, columns] = weigh(slot, a, n, peak, near_vals, near_flags)
        peaks[a, n, :, columns] = peak

    def far_use(slot, a, n, i):
        columns = slice(i * tile, (i + 1) * tile)
        old = peaks[a, n, :, columns]
        peak = jnp.maximum(ahead_peak[slot], old)
        keep = jnp.exp2(old - peak)
        total = weigh(slot, a, n, peak, far_vals, far_flags)
        before = acc[a, n, :, columns].reshape(2 * HD // 8, 8, tile)
        total = total + (before * keep[None]).reshape(2 * HD, tile)
        att[a, pl.ds(pl.multiple_of(n * HD, HD), HD), columns] = (
            total[:HD] / total[HD:]
        ).astype(jnp.bfloat16)

    def near_where(trip):
        late = lax.div(trip, trips)
        return lax.rem(other + late, 2), lax.rem(trip, trips) * group

    score(0, other, 0, 0, near_keys)
    run(0, 2 * trips, 2 * trips, near_where, near_keys, near_use)

    halo(other, 0).wait_recv()
    halo(other, 1).wait_recv()
    score(0, other, 0, 0, far_keys)
    run(0, trips, trips, lambda trip: (other, trip * group), far_keys, far_use)

    halo(h, 0).wait_recv()
    halo(h, 1).wait_recv()
    score(0, h, 0, 0, far_keys)
    swap_att = across(att.at[other], att_in, 1)
    run(0, 1, trips, lambda trip: (h, trip * group), far_keys, far_use)
    swap_att.start()
    run(1, trips, trips, lambda trip: (h, trip * group), far_keys, far_use)

    def share(attended, weight):
        return lax.dot_general(
            attended, weight, (((0,), (0,)), ((), ())), preferred_element_type=jnp.float32
        ).astype(jnp.bfloat16).astype(jnp.float32)

    flags = valid_ref[:, pl.ds(pl.multiple_of((h + 1) * half, half), half)]
    ones = jnp.full((HD, out_ref.shape[1]), 1.0 / HD, jnp.bfloat16)
    own = share(att[h], w_ref[...]) + b_ref[...]
    live = lax.dot_general(
        flags, ones, (((0,), (0,)), ((), ())), preferred_element_type=jnp.float32
    )
    weights.wait_recv()
    swap_att.wait_recv()
    update = own + share(att_in[...], w_other[...])
    out_ref[...] = jnp.where(live > 0.5, update, 0.0).astype(jnp.bfloat16)
    weights.wait_send()
    swap_att.wait_send()
    for a in range(2):
        for which in range(2):
            halo(a, which).wait_send()


def attend_patches(q, k, vt, valid, w_proj, b_proj, regions, tile=512, group=4, chunk=256):
    rows, width = q.shape
    half = rows // 2
    heads = width // HD
    columns = w_proj.shape[1]
    vmem = pl.BlockSpec(memory_space=pltpu.VMEM)
    return pl.pallas_call(
        functools.partial(patch_kernel, regions, tile, group, chunk),
        out_shape=jax.ShapeDtypeStruct((half, columns), jnp.bfloat16),
        in_specs=[vmem] * 6,
        out_specs=vmem,
        scratch_shapes=[
            pltpu.VMEM((2, half, width), jnp.bfloat16),
            pltpu.VMEM((2, width, half), jnp.bfloat16),
            pltpu.VMEM((width, columns), jnp.bfloat16),
            pltpu.VMEM((2, heads, 2 * HD, half), jnp.float32),
            pltpu.VMEM((2, heads, 8, half), jnp.float32),
            pltpu.VMEM((2, width, half), jnp.bfloat16),
            pltpu.VMEM((width, half), jnp.bfloat16),
            pltpu.VMEM((2, half, tile), jnp.float32),
            pltpu.VMEM((2, 8, tile), jnp.float32),
            pltpu.SemaphoreType.DMA((2, 2)),
            pltpu.SemaphoreType.DMA((2, 2)),
            pltpu.SemaphoreType.DMA((2, 2)),
        ],
        compiler_params=pltpu.CompilerParams(collective_id=2, has_side_effects=True),
        name="attend_patches",
    )(q, k, vt, valid, w_proj, b_proj.reshape(1, -1))


def shards(points, ln_gain, ln_bias, w_qkv, b_qkv, w_proj, b_proj, counts, hilbert_pos):
    regions = lax.axis_size("region")
    heads_axis = lax.axis_size("head")
    r = lax.axis_index("region")
    h = lax.axis_index("head")
    rows, model_width = points.shape
    group_width = w_qkv.shape[2]
    heads = group_width // HD
    width = max(group_width, LANES)
    blocks = rows // BS
    total_blocks = blocks * regions
    slots = max(2, 2 * blocks // regions)
    half_rows = PATCH // 2
    half_blocks = half_rows // BS

    if heads_axis == 2:
        send = gather_blocks(points, hilbert_pos, regions, slots, heads_axis)
        made, slot_table, ext_counts = swap(
            send, hilbert_pos, counts, ln_gain, ln_bias, jnp.transpose(w_qkv, (1, 0, 2)), b_qkv,
            regions, slots, blocks, half_blocks,
        )
        q, k, vt, flags = unpack_blocks(made, slot_table, ext_counts, blocks)
        return attend_patches(q, k, vt, flags, w_proj, b_proj, regions)

    position = jnp.arange(blocks, dtype=jnp.int32)
    my_dest = lax.dynamic_slice_in_dim(hilbert_pos, r * blocks, blocks) // blocks
    earlier = (my_dest[:, None] == my_dest[None, :]) & (position[None, :] < position[:, None])
    my_slot = my_dest * slots + jnp.sum(earlier, axis=1, dtype=jnp.int32)
    pack_table = jnp.sum(
        jnp.where(
            my_slot[None, :] == jnp.arange(regions * slots, dtype=jnp.int32)[:, None],
            position[None, :], 0,
        ),
        axis=1, dtype=jnp.int32,
    )
    every = jnp.arange(total_blocks, dtype=jnp.int32)
    ext = (
        r * blocks - half_blocks + jnp.arange(blocks + 2 * half_blocks, dtype=jnp.int32)
        + total_blocks
    ) % total_blocks
    here = hilbert_pos[None, :] == ext[:, None]
    ext_counts = jnp.sum(jnp.where(here, counts[None, :], 0), axis=1, dtype=jnp.int32)
    origin = jnp.sum(
        jnp.where(here[half_blocks:half_blocks + blocks], every[None, :], 0),
        axis=1, dtype=jnp.int32,
    )
    same = (
        (every[None, :] < origin[:, None])
        & (every[None, :] // blocks == origin[:, None] // blocks)
        & (hilbert_pos[None, :] // blocks == r)
    )
    slot_table = origin // blocks * slots + jnp.sum(same, axis=1, dtype=jnp.int32)
    own_counts = ext_counts[half_blocks:half_blocks + blocks]
    valid_ext = (
        jnp.arange(BS, dtype=jnp.int32)[None, :, None] < ext_counts[:, None, None]
    )
    valid_ext = jnp.broadcast_to(valid_ext, (blocks + 2 * half_blocks, BS, LANES))
    valid_ext = valid_ext.reshape(-1, LANES).astype(jnp.bfloat16)

    pad = width - group_width
    valid = valid_ext[half_rows:half_rows + rows]
    w_out = jnp.pad(w_proj, ((0, pad), (0, 0)))
    packed = pack_blocks(points, ln_gain, ln_bias, h, pack_table, heads_axis)
    recv = exchange(packed, regions, heads_axis)
    weight = jnp.pad(w_qkv, ((0, 0), (0, 0), (0, pad))).reshape(model_width, 3 * width)
    bias = jnp.pad(b_qkv, ((0, 0), (0, pad))).reshape(3 * width)
    qkv = project(recv, slot_table, own_counts, valid, weight, bias)

    up = [(i, (i + 1) % regions) for i in range(regions)]
    down = [(j, i) for i, j in up]
    kv = qkv[:, width:]
    before = lax.ppermute(kv[rows - half_rows:], "region", up)
    after = lax.ppermute(kv[:half_rows], "region", down)
    partials = [
        attend(jnp.int32(0), qkv, valid, before, valid_ext[:half_rows], w_out, heads),
        attend(jnp.int32(1), qkv, valid, after, valid_ext[rows + half_rows:], w_out, heads),
    ]
    summed_rows = lax.psum_scatter(
        jnp.concatenate(partials, axis=0), "head", scatter_dimension=0, tiled=True
    ).astype(jnp.float32)
    share = rows // heads_axis
    share_valid = lax.dynamic_slice(valid, (h * share, 0), (share, LANES))[:, :1] > 0
    return jnp.where(share_valid, summed_rows + b_proj, 0.0).astype(jnp.bfloat16)


def solution(mesh):
    return jax.shard_map(
        shards,
        mesh=mesh,
        in_specs=(
            P("region", None),
            P(),
            P(),
            P(None, None, "head"),
            P(None, "head"),
            P("head", None),
            P(),
            P(),
            P(),
        ),
        out_specs=P(("region", "head"), None),
        check_vma=False,
    )
```

```python
import functools

import jax
import jax.numpy as jnp
from jax import lax
from jax.experimental import pallas as pl
from jax.experimental.pallas import tpu as pltpu
from jax.sharding import PartitionSpec as P

HD = 16
PATCH = 1024
BS = 32
LANES = 128

epsilon = 1e-05
LOG2E = 1.4426950408889634
MESH = pl.DeviceIdType.MESH


def pack_kernel(total, parts, tile, pack_ref, head_ref, x_ref, gain_ref, bias_ref, out_ref, own):
    rows, depth = x_ref.shape
    width = depth // parts
    h = head_ref[0]

    def pick(value):
        chosen = value[:, :width]
        for part in range(1, parts):
            chosen = jnp.where(h == part, value[:, part * width:(part + 1) * width], chosen)
        return chosen

    gain = pick(gain_ref[...])
    bias = pick(bias_ref[...])

    def normalize(i, carry):
        part = pl.ds(pl.multiple_of(i * tile, tile), tile)
        values = x_ref[part, :].astype(jnp.float32)
        centred = values - jnp.mean(values, axis=-1, keepdims=True)
        row_var = jnp.mean(centred * centred, axis=-1, keepdims=True)
        own[part, :] = (pick(centred) * lax.rsqrt(row_var + epsilon) * gain + bias).astype(
            jnp.bfloat16
        )
        return carry

    lax.fori_loop(0, rows // tile, normalize, 0)

    def pack(j, carry):
        source = pl.multiple_of(pack_ref[j] * BS, BS)
        out_ref[pl.ds(pl.multiple_of(j * BS, BS), BS), :] = own[pl.ds(source, BS), :]
        return carry

    lax.fori_loop(0, total, pack, 0, unroll=8)


def pack_blocks(points, ln_gain, ln_bias, head, pack_table, parts, tile=256):
    total = pack_table.shape[0]
    rows, depth = points.shape
    vmem = pl.BlockSpec(memory_space=pltpu.VMEM)
    smem = pl.BlockSpec(memory_space=pltpu.SMEM)
    return pl.pallas_call(
        functools.partial(pack_kernel, total, parts, tile),
        out_shape=jax.ShapeDtypeStruct((total * BS, depth // parts), jnp.bfloat16),
        in_specs=[smem, smem, vmem, vmem, vmem],
        out_specs=vmem,
        scratch_shapes=[pltpu.VMEM((rows, depth // parts), jnp.bfloat16)],
        name="pack",
    )(pack_table, head.reshape(1), points, ln_gain.reshape(1, -1), ln_bias.reshape(1, -1))


def exchange_kernel(
    regions, heads_axis, chunk,
    send, recv, own_sem, send_sem, recv_sem, fsend_sem, frecv_sem,
):
    r = lax.axis_index("region")
    h = lax.axis_index("head")

    barrier = pltpu.get_barrier_semaphore()

    def greet(d, carry):
        pl.semaphore_signal(
            barrier, inc=1, device_id={"region": lax.rem(r + d, regions)}, device_id_type=MESH
        )
        return carry

    lax.fori_loop(1, regions, greet, 0)
    for e in range(1, heads_axis):
        pl.semaphore_signal(
            barrier, inc=1, device_id={"head": lax.rem(h + e, heads_axis)}, device_id_type=MESH
        )
    pl.semaphore_wait(barrier, regions - 1 + heads_axis - 1)

    def rows(s):
        return pl.ds(pl.multiple_of(s * chunk, chunk), chunk)

    def to_region(t):
        return pltpu.make_async_remote_copy(
            src_ref=send.at[rows(t)],
            dst_ref=recv.at[h, rows(r)],
            send_sem=send_sem.at[t],
            recv_sem=recv_sem.at[r],
            device_id={"region": t},
            device_id_type=MESH,
        )

    def from_region(s):
        return pltpu.make_async_remote_copy(
            src_ref=send.at[rows(s)],
            dst_ref=recv.at[h, rows(s)],
            send_sem=send_sem.at[s],
            recv_sem=recv_sem.at[s],
            device_id={"region": s},
            device_id_type=MESH,
        )

    def to_head(e, s, source):
        return pltpu.make_async_remote_copy(
            src_ref=source,
            dst_ref=recv.at[h, rows(s)],
            send_sem=fsend_sem.at[e, s],
            recv_sem=frecv_sem.at[h, s],
            device_id={"head": lax.rem(h + e, heads_axis)},
            device_id_type=MESH,
        )

    def from_head(e, s):
        other = lax.rem(h + e, heads_axis)
        return pltpu.make_async_remote_copy(
            src_ref=recv.at[other, rows(s)],
            dst_ref=recv.at[other, rows(s)],
            send_sem=fsend_sem.at[e, s],
            recv_sem=frecv_sem.at[other, s],
            device_id={"head": other},
            device_id_type=MESH,
        )

    def push(d, carry):
        to_region(lax.rem(r + d, regions)).start()
        return carry

    own = pltpu.make_async_copy(send.at[rows(r)], recv.at[h, rows(r)], own_sem)
    own.start()
    for e in range(1, heads_axis):
        to_head(e, r, send.at[rows(r)]).start()
    lax.fori_loop(1, regions, push, 0)

    def relay(d, carry):
        s = lax.rem(r - d + regions, regions)
        from_region(s).wait_recv()
        for e in range(1, heads_axis):
            to_head(e, s, recv.at[h, rows(s)]).start()
        return carry

    lax.fori_loop(1, regions, relay, 0)
    own.wait()

    def finish(d, carry):
        s = lax.rem(r - d + regions, regions)
        for e in range(1, heads_axis):
            from_head(e, s).wait_recv()
            to_head(e, s, recv.at[h, rows(s)]).wait_send()
        return carry

    lax.fori_loop(0, regions, finish, 0)

    def drain(d, carry):
        from_region(lax.rem(r + d, regions)).wait_send()
        return carry

    lax.fori_loop(1, regions, drain, 0)


def exchange(packed, regions, heads_axis):
    rows, width = packed.shape
    return pl.pallas_call(
        functools.partial(exchange_kernel, regions, heads_axis, rows // regions),
        out_shape=jax.ShapeDtypeStruct((heads_axis, rows, width), jnp.bfloat16),
        in_specs=[pl.BlockSpec(memory_space=pltpu.VMEM)],
        out_specs=pl.BlockSpec(memory_space=pltpu.VMEM),
        scratch_shapes=[
            pltpu.SemaphoreType.DMA,
            pltpu.SemaphoreType.DMA((regions,)),
            pltpu.SemaphoreType.DMA((regions,)),
            pltpu.SemaphoreType.DMA((heads_axis, regions)),
            pltpu.SemaphoreType.DMA((heads_axis, regions)),
        ],
        compiler_params=pltpu.CompilerParams(collective_id=0, has_side_effects=True),
        name="exchange",
    )(packed)


def project_kernel(
    blocks, tile, slot_ref, count_ref, recv, valid_ref, w_ref, b_ref, out_ref, full
):
    parts, _, piece = recv.shape
    width = w_ref.shape[1] // 3
    row_index = lax.broadcasted_iota(jnp.int32, (BS, piece), 0)

    def unpack(t, carry):
        source = pl.multiple_of(slot_ref[t] * BS, BS)
        count = count_ref[t]
        for part in range(parts):
            block = recv[part, pl.ds(source, BS), :].astype(jnp.float32)
            block = jnp.where(row_index < count, block, block[0:1, :])
            full[pl.ds(pl.multiple_of(t * BS, BS), BS), part * piece:(part + 1) * piece] = (
                block.astype(jnp.bfloat16)
            )
        return carry

    def multiply(i, carry):
        first = i * (tile // BS)
        lax.fori_loop(0, tile // BS, lambda t, c: unpack(first + t, c), 0, unroll=4)
        part = pl.ds(pl.multiple_of(i * tile, tile), tile)
        for c in range(3):
            columns = slice(c * width, (c + 1) * width)
            summed = jnp.dot(full[part, :], w_ref[:, columns], preferred_element_type=jnp.float32)
            summed = summed + b_ref[:, columns]
            if c == 0:
                summed = summed * HD ** (-0.5)
            if c == 2:
                keep = valid_ref[part, :].astype(jnp.float32)
                keep = jnp.concatenate([keep] * (width // LANES), axis=1)
                summed = jnp.where(keep > 0, summed, 0.0)
            out_ref[part, columns] = summed.astype(jnp.bfloat16)
        return carry

    lax.fori_loop(0, blocks * BS // tile, multiply, 0)


def project(recv, slot_table, own_counts, valid, weight, bias, tile=256):
    blocks = slot_table.shape[0]
    vmem = pl.BlockSpec(memory_space=pltpu.VMEM)
    smem = pl.BlockSpec(memory_space=pltpu.SMEM)
    return pl.pallas_call(
        functools.partial(project_kernel, blocks, tile),
        out_shape=jax.ShapeDtypeStruct((blocks * BS, weight.shape[1]), jnp.bfloat16),
        in_specs=[smem, smem, vmem, vmem, vmem, vmem],
        out_specs=vmem,
        scratch_shapes=[pltpu.VMEM((blocks * BS, weight.shape[0]), jnp.bfloat16)],
        name="project",
    )(slot_table, own_counts, recv, valid, weight, bias.reshape(1, -1))


def over_heads(heads, tile, q_ref, keys, vals, acc, den, ahead, peaks_out=None, peaks_in=None):
    queries, width = q_ref.shape
    lane = lax.broadcasted_iota(jnp.int32, (1, LANES), 1)
    steps = queries // tile
    per = LANES // HD

    for c in range(width // LANES):
        columns = slice(c * LANES, (c + 1) * LANES)
        count = min(per, heads - c * per)
        trip_heads = 4 if count % 4 == 0 else 2

        def score(n, i):
            mine = (lane // HD == n).astype(jnp.float32).astype(jnp.bfloat16)
            return lax.dot_general(
                q_ref[i * tile:(i + 1) * tile, columns] * mine, keys[:, columns],
                (((1,), (1,)), ((), ())), preferred_element_type=jnp.float32,
            )

        ahead[0] = score(0, 0)

        def several(trip, carry):
            order = [(trip_heads * trip + u, i) for u in range(trip_heads) for i in range(steps)]
            after = order[1:] + [(jnp.minimum(trip_heads * (trip + 1), count - 1), 0)]
            for turn, (n, i) in enumerate(order):
                part = slice(i * tile, (i + 1) * tile)
                ahead[(turn + 1) % 2] = score(*after[turn])
                scores = ahead[turn % 2]
                peak = jnp.max(scores, axis=-1, keepdims=True)
                if peaks_in is not None:
                    old = jnp.sum(
                        jnp.where(lane == n + c * per, peaks_in[part, :], 0.0),
                        axis=-1, keepdims=True,
                    )
                    peak = jnp.maximum(peak, old)
                    keep = jnp.exp(old - peak)
                if peaks_out is not None:
                    peaks_out[part, :] = jnp.where(
                        lane == n + c * per, peak, peaks_out[part, :]
                    )
                expo = jnp.exp(scores - peak).astype(jnp.bfloat16)
                result = jnp.dot(expo, vals[c], preferred_element_type=jnp.float32)
                mine = lane // HD == n
                over, under = acc[part, columns], den[part, columns]
                top, low = result[:, :LANES], result[:, LANES:]
                if peaks_in is not None:
                    top, low = over * keep + top, under * keep + low
                acc[part, columns] = jnp.where(mine, top, over)
                den[part, columns] = jnp.where(mine, low, under)
            return carry

        lax.fori_loop(0, count // trip_heads, several, 0)


def finish_heads(acc, den, w_ref, out_ref):
    attended = (acc[...] / den[...]).astype(jnp.bfloat16)
    out_ref[...] = jnp.dot(attended, w_ref[...], preferred_element_type=jnp.float32).astype(
        jnp.bfloat16
    )


def fill_values(vals, v_ref, on_ref, first):
    count = v_ref.shape[0]
    for c in range(vals.shape[0]):
        vals[c, first:first + count, :LANES] = v_ref[:, c * LANES:(c + 1) * LANES]
        vals[c, first:first + count, LANES:] = on_ref[...]


def attend_kernel(
    heads, tile,
    half_ref, q_ref, kn_ref, vn_ref, on_ref, kf_ref, vf_ref, of_ref, w_ref, out_ref,
    keys, vals, acc, den, ahead,
):
    near = kn_ref.shape[0]
    keys[:near, :] = kn_ref[...]
    keys[near:, :] = kf_ref[...]
    fill_values(vals, vn_ref, on_ref, 0)
    fill_values(vals, vf_ref, of_ref, near)
    acc[...] = jnp.zeros_like(acc)
    den[...] = jnp.ones_like(den)
    over_heads(heads, tile, q_ref, keys, vals, acc, den, ahead)
    finish_heads(acc, den, w_ref, out_ref)


def whole_block(*shape):
    return pl.BlockSpec(shape, lambda i, half: (0,) * len(shape))


def half_block(queries, width, column):
    return pl.BlockSpec((queries, width), lambda i, half: (half[0], column))


def attend_cost(heads, queries, keys, width):
    return pl.CostEstimate(
        flops=heads * queries * keys * width * 4,
        bytes_accessed=queries * width * 20,
        transcendentals=heads * queries * keys,
    )


def attend(half, qkv, valid, far_kv, far_valid, w_proj, heads, tile=512):
    width = w_proj.shape[0]
    columns = w_proj.shape[1]
    queries = far_kv.shape[0]
    whole = lambda *shape: pl.BlockSpec(shape, lambda i, half: (0,) * len(shape))
    part = lambda c, w=width: pl.BlockSpec((queries, w), lambda i, half: (half[0], c))
    return pl.pallas_call(
        functools.partial(attend_kernel, heads, tile),
        out_shape=jax.ShapeDtypeStruct((queries, columns), jnp.bfloat16),
        grid_spec=pltpu.PrefetchScalarGridSpec(
            num_scalar_prefetch=1,
            grid=(1,),
            in_specs=[
                part(0), part(1), part(2), part(0, LANES),
                pl.BlockSpec((queries, width), lambda i, half: (0, 0)),
                pl.BlockSpec((queries, width), lambda i, half: (0, 1)),
                whole(queries, LANES),
                whole(width, columns),
            ],
            out_specs=whole(queries, columns),
            scratch_shapes=[pltpu.VMEM((2 * queries, width), jnp.bfloat16)]
            + [pltpu.VMEM((width // LANES, 2 * queries, 2 * LANES), jnp.bfloat16)]
            + [pltpu.VMEM((queries, width), jnp.float32)] * 2
            + [pltpu.VMEM((2, tile, 2 * queries), jnp.float32)],
        ),
        cost_estimate=pl.CostEstimate(
            flops=heads * queries * 2 * queries * width * 4,
            bytes_accessed=queries * columns * 10,
            transcendentals=heads * queries * 2 * queries,
        ),
        name="attend",
    )(half.reshape(1), qkv, qkv, qkv, valid, far_kv, far_kv, far_valid, w_proj)


def gather_kernel(slots, pos_ref, x_ref, out_ref, taken, sems):
    rows, depth = x_ref.shape
    parts, _, width = out_ref.shape
    blocks = rows // BS
    first = lax.axis_index("region") * blocks
    for d in range(taken.shape[0]):
        taken[d] = 0

    def move(i, part, into):
        return pltpu.make_async_copy(
            x_ref.at[
                pl.ds(pl.multiple_of(i * BS, BS), BS), part * width:(part + 1) * width
            ],
            out_ref.at[part, pl.ds(pl.multiple_of(into * BS, BS), BS)],
            sems.at[part, i],
        )

    def place(i, carry):
        target = lax.div(pos_ref[first + i], blocks)
        used = taken[target]
        taken[target] = used + 1
        for part in range(parts):
            move(i, part, target * slots + used).start()
        return carry

    def settle(i, carry):
        for part in range(parts):
            move(i, part, i).wait()
        return carry

    lax.fori_loop(0, blocks, place, 0, unroll=4)
    lax.fori_loop(0, blocks, settle, 0, unroll=4)


def gather_blocks(points, hilbert_pos, regions, slots, parts):
    rows, depth = points.shape
    vmem = pl.BlockSpec(memory_space=pltpu.VMEM)
    return pl.pallas_call(
        functools.partial(gather_kernel, slots),
        out_shape=jax.ShapeDtypeStruct(
            (parts, regions * slots * BS, depth // parts), jnp.bfloat16
        ),
        in_specs=[pl.BlockSpec(memory_space=pltpu.SMEM), vmem],
        out_specs=pl.BlockSpec(memory_space=pl.ANY),
        scratch_shapes=[
            pltpu.SMEM((regions,), jnp.int32), pltpu.SemaphoreType.DMA((parts, rows // BS)),
        ],
        name="gather_blocks",
    )(hilbert_pos, points)


def tabulate(slots, r, pos_ref, amount_ref, slot_ref, count_ref):
    total = pos_ref.shape[1]
    rows = 8
    span = slot_ref.shape[1]
    blocks = slots[1]
    position = jnp.broadcast_to(pos_ref[...], (rows, total))
    lane = lax.broadcasted_iota(jnp.int32, (rows, total), 1)
    within = lax.rem(lane, blocks)
    goal = lax.div(position, blocks)
    rank = jnp.zeros((rows, total), jnp.int32)
    for k in range(1, blocks):
        same = (pltpu.roll(goal, k, 1) == goal) & (within >= k)
        rank = rank + same.astype(jnp.int32)
    slot = (lax.div(lane, blocks) * slots[0] + rank).astype(jnp.float32).astype(jnp.bfloat16)
    amount = jnp.broadcast_to(amount_ref[...], (rows, total)).astype(jnp.float32)
    wanted = lax.rem(
        lax.broadcasted_iota(jnp.int32, (span, total), 0)
        + (r * blocks - (span - blocks) // 2 + total),
        total,
    )
    found = (jnp.broadcast_to(pos_ref[...], (span, total)) == wanted).astype(jnp.float32)
    found = found.astype(jnp.bfloat16)

    def pick(values):
        picked = lax.dot_general(
            values, found, (((1,), (1,)), ((), ())), preferred_element_type=jnp.float32
        )
        return picked[0:1, :].astype(jnp.int32)

    slot_ref[...] = pick(slot)
    count_ref[...] = pick(amount.astype(jnp.bfloat16))


def swap_kernel(
    regions, near, slots,
    send, pos_ref, amount_ref, gain_ref, bias_ref, w_ref, b_ref, out_ref, slot_ref, count_ref,
    recv, made, send_sem, recv_sem, relay_sem, leave_sem,
):
    r = lax.axis_index("region")
    h = lax.axis_index("head")
    other = 1 - h
    chunk = recv.shape[1] // regions
    piece = recv.shape[2]
    width = w_ref.shape[2]
    seat = lax.rem(r, near)
    level = lax.div(r, near)
    high = lax.div(level, 2)
    low = lax.rem(level, 2)
    whole = 2 * near

    barrier = pltpu.get_barrier_semaphore()

    def greet(d, carry):
        pl.semaphore_signal(
            barrier, inc=1, device_id={"region": lax.rem(r + d, regions)}, device_id_type=MESH
        )
        return carry

    lax.fori_loop(1, regions, greet, 0)
    pl.semaphore_signal(barrier, inc=1, device_id={"head": other}, device_id_type=MESH)
    pl.semaphore_wait(barrier, regions)

    def rows(s):
        return pl.ds(pl.multiple_of(s * chunk, chunk), chunk)

    def to_region(t, part):
        return pltpu.make_async_remote_copy(
            src_ref=send.at[part, rows(t)],
            dst_ref=recv.at[part, rows(r)],
            send_sem=send_sem.at[part, t],
            recv_sem=recv_sem.at[part, r],
            device_id={"region": t},
            device_id_type=MESH,
        )

    def arrival(s, part):
        return pltpu.make_async_remote_copy(
            src_ref=send.at[part, rows(s)],
            dst_ref=recv.at[part, rows(s)],
            send_sem=send_sem.at[part, s],
            recv_sem=recv_sem.at[part, s],
            device_id={"head": other},
            device_id_type=MESH,
        )

    def relay(s):
        return pltpu.make_async_remote_copy(
            src_ref=recv.at[h, rows(s)],
            dst_ref=recv.at[h, rows(s)],
            send_sem=relay_sem.at[s],
            recv_sem=recv_sem.at[h, s],
            device_id={"head": other},
            device_id_type=MESH,
        )

    def keep(part):
        return pltpu.make_async_copy(
            send.at[part, rows(r)], recv.at[part, rows(r)], recv_sem.at[part, r]
        )

    def target(i):
        group = lax.div(i, near)
        beyond = lax.div(group, 2)
        there = 2 * lax.rem(high + beyond, 2) + lax.rem(low + group, 2)
        return there * near + lax.rem(seat + i, near)

    def source(i):
        group = lax.div(i, near)
        beyond = lax.div(group, 2)
        inner = (1 - beyond) * low + beyond * high + group
        there = 2 * lax.rem(high + beyond, 2) + lax.rem(inner, 2)
        return there * near + lax.rem(seat + regions - i, near)

    def push_whole(i, carry):
        t = target(i)
        to_region(t, h).start()
        to_region(t, other).start()
        return carry

    def push_part(i, carry):
        to_region(target(i), h).start()
        return carry

    keep(0).start()
    keep(1).start()
    lax.fori_loop(1, whole, push_whole, 0)
    lax.fori_loop(whole, regions, push_part, 0)

    def project(s):
        part = rows(s)
        left = recv[0, part, :].astype(jnp.float32)
        right = recv[1, part, :].astype(jnp.float32)
        depth = 2 * piece
        mean = (
            jnp.sum(left, axis=-1, keepdims=True) + jnp.sum(right, axis=-1, keepdims=True)
        ) * (1.0 / depth)
        left = left - mean
        right = right - mean
        row_var = (
            jnp.sum(left * left, axis=-1, keepdims=True)
            + jnp.sum(right * right, axis=-1, keepdims=True)
        ) * (1.0 / depth)
        scale = lax.rsqrt(row_var + epsilon)
        left = (left * scale * gain_ref[:, :piece] + bias_ref[:, :piece]).astype(jnp.bfloat16)
        right = (right * scale * gain_ref[:, piece:] + bias_ref[:, piece:]).astype(jnp.bfloat16)
        for c in range(3):
            summed = jnp.dot(left, w_ref[c, :piece, :], preferred_element_type=jnp.float32)
            summed = summed + jnp.dot(
                right, w_ref[c, piece:, :], preferred_element_type=jnp.float32
            )
            summed = summed + b_ref[c:c + 1, :]
            if c == 0:
                summed = summed * (HD ** (-0.5) * LOG2E)
            made[part, c * width:(c + 1) * width] = summed.astype(jnp.bfloat16)

    def leave(s):
        return pltpu.make_async_copy(made.at[rows(s)], out_ref.at[rows(s)], leave_sem.at[s])

    def forward(i):
        s = source(i)
        arrival(s, h).wait_recv()
        relay(s).start()

    last = regions - near

    def close(i, carry):
        @pl.when((i >= 1) & (i < 1 + near))
        def _():
            forward(whole + i - 1)

        s = source(i)
        arrival(s, 0).wait_recv()
        arrival(s, 1).wait_recv()
        project(s)
        leave(s).start()
        return carry

    def distant(i, carry):
        @pl.when(i == last - 2)
        def _():
            forward(last)

        @pl.when((i >= last) & (i < regions - 1))
        def _():
            forward(i + 1)

        s = source(i)
        arrival(s, other).wait_recv()
        project(s)
        leave(s).start()
        return carry

    tabulate(slots, r, pos_ref, amount_ref, slot_ref, count_ref)
    lax.fori_loop(0, whole, close, 0)
    lax.fori_loop(whole, regions, distant, 0)

    def drain_whole(i, carry):
        t = target(i)
        to_region(t, h).wait_send()
        to_region(t, other).wait_send()
        return carry

    def drain_part(i, carry):
        to_region(target(i), h).wait_send()
        relay(source(i)).wait_send()
        return carry

    def drain_leave(i, carry):
        leave(i).wait()
        return carry

    lax.fori_loop(1, whole, drain_whole, 0)
    lax.fori_loop(whole, regions, drain_part, 0)
    lax.fori_loop(0, regions, drain_leave, 0)


def swap(send, hilbert_pos, counts, ln_gain, ln_bias, weight, bias, regions, slots, blocks, near):
    parts, rows, piece = send.shape
    width = weight.shape[2]
    vmem = pl.BlockSpec(memory_space=pltpu.VMEM)
    return pl.pallas_call(
        functools.partial(swap_kernel, regions, regions // 4, (slots, blocks)),
        out_shape=[
            jax.ShapeDtypeStruct((rows, 3 * width), jnp.bfloat16),
            jax.ShapeDtypeStruct((1, blocks + 2 * near), jnp.int32),
            jax.ShapeDtypeStruct((1, blocks + 2 * near), jnp.int32),
        ],
        in_specs=[pl.BlockSpec(memory_space=pl.ANY)] + [vmem] * 6,
        out_specs=[pl.BlockSpec(memory_space=pl.ANY), vmem, vmem],
        scratch_shapes=[
            pltpu.VMEM((parts, rows, piece), jnp.bfloat16),
            pltpu.VMEM((rows, 3 * width), jnp.bfloat16),
            pltpu.SemaphoreType.DMA((parts, regions)),
            pltpu.SemaphoreType.DMA((parts, regions)),
            pltpu.SemaphoreType.DMA((regions,)),
            pltpu.SemaphoreType.DMA((regions,)),
        ],
        compiler_params=pltpu.CompilerParams(collective_id=1, has_side_effects=True),
        name="swap",
    )(
        send, hilbert_pos.reshape(1, -1), counts.reshape(1, -1), ln_gain.reshape(1, -1),
        ln_bias.reshape(1, -1), weight, bias,
    )


def unpack(slot_ref, count_ref, ext_ref, made, qkv_ref, vt_ref, valid_ref):
    blocks = qkv_ref.shape[0] // BS
    width = vt_ref.shape[0]
    near = (ext_ref.shape[1] - blocks) // 2
    row_index = lax.broadcasted_iota(jnp.int32, (BS, width), 0)

    def place(t, carry):
        source = slot_ref[0, near + t]
        into = pl.ds(pl.multiple_of(t * BS, BS), BS)
        qkv_ref[into, :width] = made[source, :, :width]
        keys = made[source, :, width:2 * width].astype(jnp.float32)
        live = row_index < count_ref[0, near + t]
        qkv_ref[into, width:2 * width] = jnp.where(live, keys, keys[0:1, :]).astype(jnp.bfloat16)
        qkv_ref[into, 2 * width:] = made[source, :, 2 * width:]
        return carry

    lax.fori_loop(0, blocks, place, 0, unroll=4)

    total = valid_ref.shape[1]
    spread = (
        lax.broadcasted_iota(jnp.int32, (ext_ref.shape[1], total), 1) // BS
        == lax.broadcasted_iota(jnp.int32, (ext_ref.shape[1], total), 0)
    ).astype(jnp.float32).astype(jnp.bfloat16)
    rows = valid_ref.shape[0]
    ext = jnp.broadcast_to(ext_ref[...].astype(jnp.float32), (rows, ext_ref.shape[1]))
    limit = jnp.dot(ext.astype(jnp.bfloat16), spread, preferred_element_type=jnp.float32)
    offset = (lax.broadcasted_iota(jnp.int32, (rows, total), 1) % BS).astype(jnp.float32)
    valid_ref[...] = (offset < limit).astype(jnp.float32).astype(jnp.bfloat16)

    step = 256
    for i in range(blocks * BS // step):
        part = slice(i * step, (i + 1) * step)
        own = valid_ref[0:1, near * BS + i * step:near * BS + (i + 1) * step].astype(jnp.float32)
        turned = jnp.transpose(qkv_ref[part, 2 * width:].astype(jnp.float32))
        vt_ref[:, part] = (turned * own).astype(jnp.bfloat16)


def patch_kernel(
    regions, tile, group, chunk,
    slot_ref, count_ref, ext_ref, made, w_ref, b_ref, out_ref,
    qkv_ref, vt_ref, valid_ref, kh, vth, w_other, acc, peaks, att, att_in, ahead, ahead_peak,
    send_sem, recv_sem, side_sem,
):
    r = lax.axis_index("region")
    h = lax.axis_index("head")
    other = 1 - h
    half = kh.shape[1]
    width = kh.shape[2]
    heads = width // HD
    per = LANES // HD
    tiles = half // tile
    trips = heads // group
    lane = lax.broadcasted_iota(jnp.int32, (1, LANES), 1)

    def toward(a):
        return lax.rem(r + 1 - 2 * a + regions, regions)

    barrier = pltpu.get_barrier_semaphore()
    for a in range(2):
        pl.semaphore_signal(
            barrier, inc=1, device_id={"region": toward(a)}, device_id_type=MESH
        )
    pl.semaphore_signal(barrier, inc=1, device_id={"head": other}, device_id_type=MESH)
    unpack(slot_ref, count_ref, ext_ref, made, qkv_ref, vt_ref, valid_ref)
    pl.semaphore_wait(barrier, 3)

    def start_of(a):
        return pl.multiple_of(a * half, half)

    def halo(a, which):
        rows = pl.ds(start_of(1 - a), half)
        source = qkv_ref.at[rows, width:2 * width] if which == 0 else vt_ref.at[:, rows]
        target = kh.at[a] if which == 0 else vth.at[a]
        return pltpu.make_async_remote_copy(
            src_ref=source, dst_ref=target,
            send_sem=send_sem.at[which, a], recv_sem=recv_sem.at[which, a],
            device_id={"region": toward(a)}, device_id_type=MESH,
        )

    def across(source, target, slot):
        return pltpu.make_async_remote_copy(
            src_ref=source, dst_ref=target,
            send_sem=side_sem.at[0, slot], recv_sem=side_sem.at[1, slot],
            device_id={"head": other}, device_id_type=MESH,
        )

    weights = across(w_ref, w_other, 0)
    halo(other, 0).start()
    halo(other, 1).start()
    halo(h, 0).start()
    halo(h, 1).start()
    weights.start()

    def score(slot, a, n, i, keys):
        column = pl.multiple_of(n // per * LANES, LANES)
        columns = pl.ds(column, LANES)
        mine = (lane // HD == n % per).astype(jnp.float32).astype(jnp.bfloat16)
        queries = qkv_ref[pl.ds(pl.multiple_of(a * half + i * tile, tile), tile), columns] * mine
        top = None
        for first in range(0, half, chunk):
            scores = lax.dot_general(
                keys(a, first, column), queries, (((1,), (1,)), ((), ())),
                preferred_element_type=jnp.float32,
            )
            ahead[slot, first:first + chunk] = scores
            part = jnp.max(scores.reshape(chunk // 8, 8, tile), axis=0)
            top = part if top is None else jnp.maximum(top, part)
        ahead_peak[slot] = jnp.broadcast_to(jnp.max(top, axis=0, keepdims=True), (8, tile))

    def weigh(slot, a, n, peak, vals, flags):
        total = None
        rows = pl.ds(pl.multiple_of(n * HD, HD), HD)
        for first in range(0, half, chunk):
            scores = ahead[slot, first:first + chunk].reshape(chunk // 8, 8, tile)
            expo = jnp.exp2(scores - peak[None]).reshape(chunk, tile).astype(jnp.bfloat16)
            left = jnp.concatenate([vals(a, rows, first), flags(a, first)], axis=0)
            part = jnp.dot(left, expo, preferred_element_type=jnp.float32)
            total = part if total is None else total + part
        return total

    def run(trip_from, trip_to, limit, where, keys, use):
        def body(trip, carry):
            units = [(u, i) for u in range(group) for i in range(tiles)]
            for turn, (u, i) in enumerate(units):
                if turn + 1 < len(units):
                    v, j = units[turn + 1]
                    a, n = where(trip)
                    score((turn + 1) % 2, a, n + v, j, keys)
                else:
                    a, n = where(jnp.minimum(trip + 1, limit - 1))
                    score((turn + 1) % 2, a, n, 0, keys)
                a, n = where(trip)
                use(turn % 2, a, n + u, i)
            return carry

        lax.fori_loop(trip_from, trip_to, body, 0)

    def near_keys(a, first, column):
        columns = pl.ds(pl.multiple_of(width + column, LANES), LANES)
        return qkv_ref[pl.ds(pl.multiple_of(a * half + first, chunk), chunk), columns]

    def near_vals(a, rows, first):
        return vt_ref[rows, pl.ds(pl.multiple_of(a * half + first, chunk), chunk)]

    def near_flags(a, first):
        return valid_ref[:, pl.ds(pl.multiple_of((a + 1) * half + first, chunk), chunk)]

    def far_keys(a, first, column):
        return kh[a, first:first + chunk, pl.ds(column, LANES)]

    def far_vals(a, rows, first):
        return vth[a, rows, first:first + chunk]

    def far_flags(a, first):
        return valid_ref[:, pl.ds(pl.multiple_of(a * 3 * half + first, chunk), chunk)]

    def near_use(slot, a, n, i):
        peak = ahead_peak[slot]
        columns = slice(i * tile, (i + 1) * tile)
        acc[a, n, :, columns] = weigh(slot, a, n, peak, near_vals, near_flags)
        peaks[a, n, :, columns] = peak

    def far_use(slot, a, n, i):
        columns = slice(i * tile, (i + 1) * tile)
        old = peaks[a, n, :, columns]
        peak = jnp.maximum(ahead_peak[slot], old)
        keep = jnp.exp2(old - peak)
        total = weigh(slot, a, n, peak, far_vals, far_flags)
        before = acc[a, n, :, columns].reshape(2 * HD // 8, 8, tile)
        total = total + (before * keep[None]).reshape(2 * HD, tile)
        att[a, pl.ds(pl.multiple_of(n * HD, HD), HD), columns] = (
            total[:HD] / total[HD:]
        ).astype(jnp.bfloat16)

    def near_where(trip):
        late = lax.div(trip, trips)
        return lax.rem(other + late, 2), lax.rem(trip, trips) * group

    score(0, other, 0, 0, near_keys)
    run(0, 2 * trips, 2 * trips, near_where, near_keys, near_use)

    halo(other, 0).wait_recv()
    halo(other, 1).wait_recv()
    score(0, other, 0, 0, far_keys)
    run(0, trips, trips, lambda trip: (other, trip * group), far_keys, far_use)

    halo(h, 0).wait_recv()
    halo(h, 1).wait_recv()
    score(0, h, 0, 0, far_keys)
    swap_att = across(att.at[other], att_in, 1)
    run(0, 1, trips, lambda trip: (h, trip * group), far_keys, far_use)
    swap_att.start()
    run(1, trips, trips, lambda trip: (h, trip * group), far_keys, far_use)

    def share(attended, weight):
        return lax.dot_general(
            attended, weight, (((0,), (0,)), ((), ())), preferred_element_type=jnp.float32
        ).astype(jnp.bfloat16).astype(jnp.float32)

    flags = valid_ref[:, pl.ds(pl.multiple_of((h + 1) * half, half), half)]
    ones = jnp.full((HD, out_ref.shape[1]), 1.0 / HD, jnp.bfloat16)
    own = share(att[h], w_ref[...]) + b_ref[...]
    live = lax.dot_general(
        flags, ones, (((0,), (0,)), ((), ())), preferred_element_type=jnp.float32
    )
    weights.wait_recv()
    swap_att.wait_recv()
    update = own + share(att_in[...], w_other[...])
    out_ref[...] = jnp.where(live > 0.5, update, 0.0).astype(jnp.bfloat16)
    weights.wait_send()
    swap_att.wait_send()
    for a in range(2):
        for which in range(2):
            halo(a, which).wait_send()


def attend_patches(made, slots, counts, w_proj, b_proj, regions, blocks, tile=512, group=4, chunk=256):
    width = made.shape[1] // 3
    rows = blocks * BS
    span = counts.shape[1] * BS
    smem = pl.BlockSpec(memory_space=pltpu.SMEM)
    half = rows // 2
    heads = width // HD
    columns = w_proj.shape[1]
    vmem = pl.BlockSpec(memory_space=pltpu.VMEM)
    return pl.pallas_call(
        functools.partial(patch_kernel, regions, tile, group, chunk),
        out_shape=jax.ShapeDtypeStruct((half, columns), jnp.bfloat16),
        in_specs=[smem, smem] + [vmem] * 4,
        out_specs=vmem,
        scratch_shapes=[
            pltpu.VMEM((rows, 3 * width), jnp.bfloat16),
            pltpu.VMEM((width, rows), jnp.bfloat16),
            pltpu.VMEM((HD, span), jnp.bfloat16),
            pltpu.VMEM((2, half, width), jnp.bfloat16),
            pltpu.VMEM((2, width, half), jnp.bfloat16),
            pltpu.VMEM((width, columns), jnp.bfloat16),
            pltpu.VMEM((2, heads, 2 * HD, half), jnp.float32),
            pltpu.VMEM((2, heads, 8, half), jnp.float32),
            pltpu.VMEM((2, width, half), jnp.bfloat16),
            pltpu.VMEM((width, half), jnp.bfloat16),
            pltpu.VMEM((2, half, tile), jnp.float32),
            pltpu.VMEM((2, 8, tile), jnp.float32),
            pltpu.SemaphoreType.DMA((2, 2)),
            pltpu.SemaphoreType.DMA((2, 2)),
            pltpu.SemaphoreType.DMA((2, 2)),
        ],
        compiler_params=pltpu.CompilerParams(collective_id=2, has_side_effects=True),
        name="attend_patches",
    )(slots, counts, counts, made.reshape(-1, BS, 3 * width), w_proj, b_proj.reshape(1, -1))


def shards(points, ln_gain, ln_bias, w_qkv, b_qkv, w_proj, b_proj, counts, hilbert_pos):
    regions = lax.axis_size("region")
    heads_axis = lax.axis_size("head")
    r = lax.axis_index("region")
    h = lax.axis_index("head")
    rows, model_width = points.shape
    group_width = w_qkv.shape[2]
    heads = group_width // HD
    width = max(group_width, LANES)
    blocks = rows // BS
    total_blocks = blocks * regions
    slots = max(2, 2 * blocks // regions)
    half_rows = PATCH // 2
    half_blocks = half_rows // BS

    if heads_axis == 2:
        send = gather_blocks(points, hilbert_pos, regions, slots, heads_axis)
        made, slot_table, ext_counts = swap(
            send, hilbert_pos, counts, ln_gain, ln_bias, jnp.transpose(w_qkv, (1, 0, 2)), b_qkv,
            regions, slots, blocks, half_blocks,
        )
        return attend_patches(made, slot_table, ext_counts, w_proj, b_proj, regions, blocks)

    position = jnp.arange(blocks, dtype=jnp.int32)
    my_dest = lax.dynamic_slice_in_dim(hilbert_pos, r * blocks, blocks) // blocks
    earlier = (my_dest[:, None] == my_dest[None, :]) & (position[None, :] < position[:, None])
    my_slot = my_dest * slots + jnp.sum(earlier, axis=1, dtype=jnp.int32)
    pack_table = jnp.sum(
        jnp.where(
            my_slot[None, :] == jnp.arange(regions * slots, dtype=jnp.int32)[:, None],
            position[None, :], 0,
        ),
        axis=1, dtype=jnp.int32,
    )
    every = jnp.arange(total_blocks, dtype=jnp.int32)
    ext = (
        r * blocks - half_blocks + jnp.arange(blocks + 2 * half_blocks, dtype=jnp.int32)
        + total_blocks
    ) % total_blocks
    here = hilbert_pos[None, :] == ext[:, None]
    ext_counts = jnp.sum(jnp.where(here, counts[None, :], 0), axis=1, dtype=jnp.int32)
    origin = jnp.sum(
        jnp.where(here[half_blocks:half_blocks + blocks], every[None, :], 0),
        axis=1, dtype=jnp.int32,
    )
    same = (
        (every[None, :] < origin[:, None])
        & (every[None, :] // blocks == origin[:, None] // blocks)
        & (hilbert_pos[None, :] // blocks == r)
    )
    slot_table = origin // blocks * slots + jnp.sum(same, axis=1, dtype=jnp.int32)
    own_counts = ext_counts[half_blocks:half_blocks + blocks]
    valid_ext = (
        jnp.arange(BS, dtype=jnp.int32)[None, :, None] < ext_counts[:, None, None]
    )
    valid_ext = jnp.broadcast_to(valid_ext, (blocks + 2 * half_blocks, BS, LANES))
    valid_ext = valid_ext.reshape(-1, LANES).astype(jnp.bfloat16)

    pad = width - group_width
    valid = valid_ext[half_rows:half_rows + rows]
    w_out = jnp.pad(w_proj, ((0, pad), (0, 0)))
    packed = pack_blocks(points, ln_gain, ln_bias, h, pack_table, heads_axis)
    recv = exchange(packed, regions, heads_axis)
    weight = jnp.pad(w_qkv, ((0, 0), (0, 0), (0, pad))).reshape(model_width, 3 * width)
    bias = jnp.pad(b_qkv, ((0, 0), (0, pad))).reshape(3 * width)
    qkv = project(recv, slot_table, own_counts, valid, weight, bias)

    up = [(i, (i + 1) % regions) for i in range(regions)]
    down = [(j, i) for i, j in up]
    kv = qkv[:, width:]
    before = lax.ppermute(kv[rows - half_rows:], "region", up)
    after = lax.ppermute(kv[:half_rows], "region", down)
    partials = [
        attend(jnp.int32(0), qkv, valid, before, valid_ext[:half_rows], w_out, heads),
        attend(jnp.int32(1), qkv, valid, after, valid_ext[rows + half_rows:], w_out, heads),
    ]
    summed_rows = lax.psum_scatter(
        jnp.concatenate(partials, axis=0), "head", scatter_dimension=0, tiled=True
    ).astype(jnp.float32)
    share = rows // heads_axis
    share_valid = lax.dynamic_slice(valid, (h * share, 0), (share, LANES))[:, :1] > 0
    return jnp.where(share_valid, summed_rows + b_proj, 0.0).astype(jnp.bfloat16)


def solution(mesh):
    return jax.shard_map(
        shards,
        mesh=mesh,
        in_specs=(
            P("region", None),
            P(),
            P(),
            P(None, None, "head"),
            P(None, "head"),
            P("head", None),
            P(),
            P(),
            P(),
        ),
        out_specs=P(("region", "head"), None),
        check_vma=False,
    )
```
